32 devices in a mesh: dp: 8 (over z, x), tensor: 4 (over y, core).
Axes of the slice: x: 2, y: 2, z: 4, core: 2. Of those that a mesh axis runs over, the one named last changes fastest.
Arguments:
- tokens: bfloat16 [8192, 2048], P(('dp', 'tensor')), may hold values from -6 to 6
- out_grad: bfloat16 [8192, 2048], P(('dp', 'tensor')), may hold values from -6 to 6
- segments: int32 [8, 1024], P('dp'), may hold values from 0 to 7, never falling along the last dimension, each value on 1 to 341 neighbouring positions
- ln_gain: float32 [2048], replicated, may hold values from 0.1 to 1.9
- ln_bias: float32 [2048], replicated, may hold values from -3 to 3
- qkv_weight: bfloat16 [2048, 3, 2048], P('dp', None, 'tensor'), may hold values from -0.125 to 0.125
- qkv_bias: float32 [3, 2048], P(None, 'tensor'), may hold values from -3 to 3
- dense_weight: bfloat16 [2048, 2048], P('dp', 'tensor'), may hold values from -0.75 to 0.75
- dense_bias: float32 [2048], replicated, may hold values from -2 to 2
- fc1_weight: bfloat16 [2048, 8192], P('dp', 'tensor'), may hold values from -0.125 to 0.125
- fc1_bias: float32 [8192], P('tensor'), may hold values from -3 to 3
- fc2_weight: bfloat16 [2048, 8192], P('dp', 'tensor'), may hold values from -0.0625 to 0.0625
- fc2_bias: float32 [2048], replicated, may hold values from -2 to 2
Outputs:
- output: bfloat16 [8192, 2048], P(('dp', 'tensor'))
- input_grad: bfloat16 [8192, 2048], P(('dp', 'tensor'))
- ln_gain_grad: float32 [2048], replicated
- ln_bias_grad: float32 [2048], replicated
- qkv_weight_grad: float32 [2048, 3, 2048], P('dp', None, 'tensor')
- qkv_bias_grad: float32 [3, 2048], P(None, 'tensor')
- dense_weight_grad: float32 [2048, 2048], P('dp', 'tensor')
- dense_bias_grad: float32 [2048], replicated
- fc1_weight_grad: float32 [2048, 8192], P('dp', 'tensor')
- fc1_bias_grad: float32 [8192], P('tensor')
- fc2_weight_grad: float32 [2048, 8192], P('dp', 'tensor')
- fc2_bias_grad: float32 [2048], replicated
The draws below stay inside these ranges and needn't reach their ends.
Inputs may be any that keep to these rules, and one draw needn't show every extreme that they name: `segments`: segment numbers never fall along a sequence; a segment holds at most one third of 1024 tokens.
All inputs are finite; a program needn't handle non-finite values.
Results may differ from the reference program's by a relative error of at most 0.0099.
Values may be sent and summed in bfloat16 or wider, within the bound.
No kernel may reach another device: no remote copies, remote signals or barrier semaphores. Data moves between devices by JAX's collectives and lax.ppermute only.
A program may use at most 256 MiB of HBM per device.

```python
import math
import jax
import jax.numpy as jnp
import numpy as np
from jax import lax

D = 2048
H = 32
FF = 8192
ROT = 32
LEN = 1024
ROWS = 8
TOKENS = 8192


def spiked(entries, stream_key, source, target, shards_of, factor):
    owner, partner = [(jnp.arange(entries.shape[axis_at]) // (entries.shape[axis_at] // shards_of)).reshape([-1 if axis == axis_at else 1 for axis in range(entries.ndim)]) for axis_at in (source, target)]
    chosen = jax.random.permutation(stream_key, shards_of)[partner]
    strong = (owner == chosen) | (owner == (partner + shards_of // 2) % shards_of)
    return jnp.where(strong, factor * entries, entries)


def levels(key, extent, pieces, smallest, largest):
    factor_of = 1.0
    for axis_at, shards_of in pieces:
        steps = jax.random.uniform(jax.random.fold_in(jax.random.fold_in(key, 6), axis_at), (shards_of,), jnp.float32, smallest / len(pieces), largest / len(pieces))
        factor_of = factor_of * jnp.repeat(jnp.exp(steps), extent[axis_at] // shards_of).reshape((-1,) + (1,) * (len(extent) - 1 - axis_at))
    return factor_of


def profile(amount, total, most, lean):
    portions = [(1 << 20) // math.isqrt(rank ** lean) + 1 for rank in range(2, amount + 1)]
    spare, holding = total - most - (amount - 1), [1] * (amount - 1)
    while spare > 0:
        movable = [i for i in range(amount - 1) if holding[i] < most]
        pool, budget = sum([portions[i] for i in movable]), spare
        for i in movable:
            addition = min(most - holding[i], max(1, budget * portions[i] // pool), spare)
            holding[i] = holding[i] + addition
            spare = spare - addition
    return np.array([most] + holding)


def ragged_sizes(rng, number_of, total, reach, lean):
    if number_of == 2:
        one = jax.random.randint(rng, (), max(1, total - reach), min(reach, total - 1) + 1)
        return jnp.stack([one, total - one])
    tallies = jnp.asarray(profile(number_of, total, reach, lean), jnp.int32)
    couples = (number_of - 1) // 2
    source_of, receiver = tallies[1:1 + 2 * couples:2], tallies[2:2 + 2 * couples:2]
    room = jnp.minimum(source_of - 1, reach - receiver)
    passed = jax.random.randint(jax.random.fold_in(rng, 1), (couples,), 0, 1 << 20) % (room + 1)
    tallies = tallies.at[1:1 + 2 * couples:2].set(source_of - passed).at[2:2 + 2 * couples:2].set(receiver + passed)
    return tallies[jax.random.permutation(jax.random.fold_in(rng, 2), number_of)]


def noise(stream_key, shape, width, bound, cuts=(), dtype=jnp.bfloat16):
    entries = jax.random.normal(stream_key, shape, jnp.float32) * width
    if len(cuts) > 0:
        entries = levels(stream_key, shape, cuts, -0.22, 0.18) * entries
    return jnp.clip(entries, min=-bound, max=bound).astype(dtype)


def noise_with(rng, shape, spread, reach, cuts, heavy, dtype=jnp.bfloat16):
    entries = spread * jax.random.normal(rng, shape, jnp.float32)
    if cuts:
        entries = entries * levels(rng, shape, cuts, -0.22, 0.18)
    return jnp.clip(spiked(entries, jax.random.fold_in(rng, 3), *heavy), -reach, reach).astype(dtype)


def setup_inputs(seed: int = 0) -> dict:
    key_of = jax.random.split(jax.random.key(seed), 14)
    return {
        "tokens": noise_with(key_of[0], (TOKENS, D), 1.0, 6.0, ((0, 32),), (0, 1, 32, 2.75)),
        "out_grad": noise_with(key_of[1], (TOKENS, D), 1.0, 6.0, ((0, 32),), (0, 1, 32, 2.75)),
        "segments": jax.vmap(lambda own: jnp.searchsorted(jnp.cumsum(ragged_sizes(own, 8, LEN, LEN // 3, 2)), jnp.arange(LEN), side="right"))(jax.random.split(key_of[2], ROWS)).reshape((ROWS, LEN)).astype(jnp.int32),
        "ln_gain": jnp.clip(1.0 + 0.18 * jax.random.normal(key_of[3], (D,), jnp.float32), 0.1, 1.9),
        "ln_bias": noise(key_of[4], (D,), 0.5, 3.0, (), jnp.float32),
        "qkv_weight": noise(key_of[5], (D, 3, D), D ** -0.5, 0.125, ((0, 8), (2, 4))),
        "qkv_bias": noise(key_of[6], (3, D), 0.5, 3.0, ((1, 4),), jnp.float32),
        "dense_weight": noise(key_of[7], (D, D), (D // 32) ** -0.5, 0.75, ((0, 8), (1, 4))),
        "dense_bias": noise(key_of[8], (D,), 0.3, 2.0, (), jnp.float32),
        "fc1_weight": noise(key_of[9], (D, FF), D ** -0.5, 0.125, ((0, 8), (1, 4))),
        "fc1_bias": noise(key_of[10], (FF,), 0.5, 3.0, ((0, 4),), jnp.float32),
        "fc2_weight": noise(key_of[11], (D, FF), FF ** -0.5, 0.0625, ((0, 8), (1, 4))),
        "fc2_bias": noise(key_of[12], (D,), 0.3, 2.0, (), jnp.float32),
    }


EPSILON = 1e-05
GELU_SCALE = math.sqrt(2.0 / math.pi)
GELU_CUBIC = 0.044715
MASK_VALUE = -1e+30
ROPE_BASE = 10000.0

def gelu_value(pre_gelu):
    tanh_arg = GELU_SCALE * (pre_gelu + GELU_CUBIC * pre_gelu * pre_gelu * pre_gelu)
    return 0.5 * pre_gelu * (1.0 + jnp.tanh(tanh_arg))

def gelu_slope(pre_gelu):
    tanh_arg = GELU_SCALE * (pre_gelu + GELU_CUBIC * pre_gelu * pre_gelu * pre_gelu)
    tangent = jnp.tanh(tanh_arg)
    return 0.5 * (1.0 + tangent) + 0.5 * pre_gelu * (1.0 - tangent * tangent) * GELU_SCALE * (1.0 + 3.0 * GELU_CUBIC * pre_gelu * pre_gelu)

def normalize_rows(token_rows):
    values = token_rows.astype(jnp.float32)
    centered = values - lax.optimization_barrier(jnp.mean(values, axis=-1, keepdims=True))
    inv_std = lax.rsqrt(lax.optimization_barrier(jnp.mean(centered * centered, axis=-1, keepdims=True)) + EPSILON)
    return (centered * inv_std, inv_std)

def rotary_tables(row_total, period, rotated):
    half_rot = rotated // 2
    positions = (jnp.arange(row_total) % period).astype(jnp.float32)
    inverse = ROPE_BASE ** (-(2.0 * jnp.arange(half_rot).astype(jnp.float32)) / rotated)
    angles = positions[:, None] * inverse[None, :]
    return (jnp.cos(angles)[:, None, :], jnp.sin(angles)[:, None, :])

def rotate_heads(heads, cosine, sine, rotated):
    half_rot = rotated // 2
    former = heads[..., :half_rot]
    latter = heads[..., half_rot:rotated]
    return jnp.concatenate([former * cosine - latter * sine, latter * cosine + former * sine, heads[..., rotated:]], axis=-1)

def unrotate_heads(grads, cosine, sine, rotated):
    half_rot = rotated // 2
    former = grads[..., :half_rot]
    latter = grads[..., half_rot:rotated]
    return jnp.concatenate([former * cosine + latter * sine, latter * cosine - former * sine, grads[..., rotated:]], axis=-1)

def reference(tokens, out_grad, segments, ln_gain, ln_bias, qkv_weight, qkv_bias, dense_weight, dense_bias, fc1_weight, fc1_bias, fc2_weight, fc2_bias):
    head_dim = D // H
    score_scale = 1.0 / math.sqrt(head_dim)
    cosine, sine = rotary_tables(LEN, LEN, ROT)
    qkv_matrix = qkv_weight.reshape(D, 3 * D)
    position = jnp.arange(LEN)
    causal = position[None, :] <= position[:, None]
    seq_count = tokens.shape[0] // LEN

    def one_sequence(carried, inputs):
        seq_tokens, seq_grad, doc_ids = inputs
        x_hat, inv_std = normalize_rows(seq_tokens)
        normed = (x_hat * ln_gain + ln_bias).astype(jnp.bfloat16)
        projected = jnp.dot(normed, qkv_matrix, preferred_element_type=jnp.float32).reshape(LEN, 3, D) + qkv_bias
        query_rows = rotate_heads(projected[:, 0].reshape(LEN, H, head_dim), cosine, sine, ROT).astype(jnp.bfloat16)
        key_rows = rotate_heads(projected[:, 1].reshape(LEN, H, head_dim), cosine, sine, ROT).astype(jnp.bfloat16)
        value_rows = projected[:, 2].reshape(LEN, H, head_dim).astype(jnp.bfloat16)
        allowed = (doc_ids[:, None] == doc_ids[None, :]) & causal
        query_heads = query_rows.transpose(1, 0, 2)
        key_heads = key_rows.transpose(1, 0, 2)
        value_heads = value_rows.transpose(1, 0, 2)

        def masked(query_head, key_head):
            raw = jnp.dot(query_head, key_head.T, preferred_element_type=jnp.float32) * score_scale
            return jnp.where(allowed, raw, MASK_VALUE)

        def head_forward(members):
            query_head, key_head, value_head = members
            scores = masked(query_head, key_head)
            row_max = lax.optimization_barrier(jnp.max(scores, axis=-1, keepdims=True))
            log_total = row_max + jnp.log(lax.optimization_barrier(jnp.sum(jnp.exp(scores - row_max), axis=-1, keepdims=True)))
            probs_low = jnp.exp(scores - log_total).astype(jnp.bfloat16)
            head_out = jnp.dot(probs_low, value_head, preferred_element_type=jnp.float32).astype(jnp.bfloat16)
            return (head_out, log_total[:, 0])
        head_outputs, log_totals = lax.map(head_forward, (query_heads, key_heads, value_heads))
        attended = head_outputs.transpose(1, 0, 2).reshape(LEN, D)
        pre_gelu = jnp.dot(normed, fc1_weight, preferred_element_type=jnp.float32) + fc1_bias
        activated = gelu_value(pre_gelu).astype(jnp.bfloat16)
        branch = jnp.dot(attended, dense_weight.T, preferred_element_type=jnp.float32) + jnp.dot(activated, fc2_weight.T, preferred_element_type=jnp.float32)
        output = (seq_tokens.astype(jnp.float32) + branch + dense_bias + fc2_bias).astype(jnp.bfloat16)
        pre_grad_full = jnp.dot(seq_grad, fc2_weight, preferred_element_type=jnp.float32) * gelu_slope(pre_gelu)
        pre_grad = pre_grad_full.astype(jnp.bfloat16)
        attended_grad = jnp.dot(seq_grad, dense_weight, preferred_element_type=jnp.float32).astype(jnp.bfloat16)
        grad_heads = attended_grad.reshape(LEN, H, head_dim).transpose(1, 0, 2)

        def head_backward(members):
            query_head, key_head, value_head, log_total, grad_head = members
            scores = masked(query_head, key_head)
            probs_full = jnp.exp(scores - log_total[:, None])
            probs_low = probs_full.astype(jnp.bfloat16)
            value_grad = jnp.dot(probs_low.T, grad_head, preferred_element_type=jnp.float32)
            prob_grad = jnp.dot(grad_head, value_head.T, preferred_element_type=jnp.float32)
            row_dot = lax.optimization_barrier(jnp.sum(probs_full * prob_grad, axis=-1, keepdims=True))
            score_grad = (probs_full * (prob_grad - row_dot) * score_scale).astype(jnp.bfloat16)
            query_grad = jnp.dot(score_grad, key_head, preferred_element_type=jnp.float32)
            key_grad = jnp.dot(score_grad.T, query_head, preferred_element_type=jnp.float32)
            return (query_grad, key_grad, value_grad)
        query_grads, key_grads, value_grads = lax.map(head_backward, (query_heads, key_heads, value_heads, log_totals, grad_heads))
        query_grad = unrotate_heads(query_grads.transpose(1, 0, 2), cosine, sine, ROT).reshape(LEN, D)
        key_grad = unrotate_heads(key_grads.transpose(1, 0, 2), cosine, sine, ROT).reshape(LEN, D)
        value_grad = value_grads.transpose(1, 0, 2).reshape(LEN, D)
        qkv_grad_full = jnp.stack([query_grad, key_grad, value_grad], axis=1)
        qkv_grad = qkv_grad_full.astype(jnp.bfloat16).reshape(LEN, 3 * D)
        normed_grad = jnp.dot(qkv_grad, qkv_matrix.T, preferred_element_type=jnp.float32) + jnp.dot(pre_grad, fc1_weight.T, preferred_element_type=jnp.float32)
        scaled = normed_grad * ln_gain
        token_grad = inv_std * (scaled - lax.optimization_barrier(jnp.mean(scaled, axis=-1, keepdims=True)) - x_hat * lax.optimization_barrier(jnp.mean(scaled * x_hat, axis=-1, keepdims=True)))
        input_grad = (seq_grad.astype(jnp.float32) + token_grad).astype(jnp.bfloat16)
        updates = (lax.optimization_barrier(jnp.sum(normed_grad * x_hat, axis=0)), lax.optimization_barrier(jnp.sum(normed_grad, axis=0)), jnp.dot(normed.T, qkv_grad, preferred_element_type=jnp.float32), lax.optimization_barrier(jnp.sum(qkv_grad_full, axis=0)), jnp.dot(seq_grad.T, attended, preferred_element_type=jnp.float32), lax.optimization_barrier(jnp.sum(seq_grad.astype(jnp.float32), axis=0)), jnp.dot(normed.T, pre_grad, preferred_element_type=jnp.float32), lax.optimization_barrier(jnp.sum(pre_grad_full, axis=0)), jnp.dot(seq_grad.T, activated, preferred_element_type=jnp.float32))
        carried = tuple((old + new for old, new in zip(carried, updates)))
        return (carried, (output, input_grad))
    initial = (jnp.zeros((D,), jnp.float32), jnp.zeros((D,), jnp.float32), jnp.zeros((D, 3 * D), jnp.float32), jnp.zeros((3, D), jnp.float32), jnp.zeros((D, D), jnp.float32), jnp.zeros((D,), jnp.float32), jnp.zeros((D, FF), jnp.float32), jnp.zeros((FF,), jnp.float32), jnp.zeros((D, FF), jnp.float32))
    sums, (outputs, input_grads) = lax.scan(one_sequence, initial, (tokens.reshape(seq_count, LEN, D), out_grad.reshape(seq_count, LEN, D), segments))
    gain_sum, shift_sum, qkv_sum, qkv_bias_sum, dense_sum, out_bias_sum, fc1_sum, fc1_bias_sum, fc2_sum = sums
    return (outputs.reshape(seq_count * LEN, D), input_grads.reshape(seq_count * LEN, D), gain_sum, shift_sum, qkv_sum.reshape(D, 3, D), qkv_bias_sum, dense_sum, out_bias_sum, fc1_sum, fc1_bias_sum, fc2_sum, out_bias_sum)
```

```python
import functools
import math

import jax
import jax.numpy as jnp
import numpy as np
from jax import lax
from jax.experimental import pallas as pl
from jax.experimental.pallas import tpu as pltpu
from jax.sharding import Mesh
from jax.sharding import PartitionSpec as P

D = 2048
H = 32
ROT = 32
LEN = 1024
LONGEST = LEN // 3
HEAD = D // H
QB = 128
BACK = -(-(LONGEST - 1) // QB)

EPSILON = 1e-05
GELU_SCALE = math.sqrt(2.0 / math.pi)
GELU_CUBIC = 0.044715
MASK_VALUE = -1e30
ROPE_BASE = 10000.0
LOW = jnp.bfloat16
FULL = jnp.float32


def gelu_both(pre_gelu):
    square = pre_gelu * pre_gelu
    tangent = jnp.tanh(GELU_SCALE * pre_gelu * (1.0 + GELU_CUBIC * square))
    value = 0.5 * pre_gelu * (1.0 + tangent)
    slope = 0.5 * (1.0 + tangent) + 0.5 * pre_gelu * (1.0 - tangent * tangent) * GELU_SCALE * (
        1.0 + 3.0 * GELU_CUBIC * square
    )
    return value, slope


def normalize_rows(token_rows):
    values = token_rows.astype(FULL)
    centered = values - jnp.mean(values, axis=-1, keepdims=True)
    inv_std = lax.rsqrt(jnp.mean(centered * centered, axis=-1, keepdims=True) + EPSILON)
    return (centered * inv_std, inv_std)


def rotary_lanes():
    half = ROT // 2
    inverse = ROPE_BASE ** (-(2.0 * np.arange(half)) / ROT)
    angles = np.arange(LEN)[:, None] * inverse[None, :]
    rest = np.zeros((LEN, HEAD - ROT))
    cosine = np.concatenate([np.cos(angles), np.cos(angles), rest + 1.0], axis=1)
    sine = np.concatenate([-np.sin(angles), np.sin(angles), rest], axis=1)
    return tuple(jnp.asarray(np.tile(table, (1, 2)), FULL) for table in (cosine, sine))


def matmul(left, right, left_dim, right_dim):
    return lax.dot_general(
        left, right, (((left_dim,), (right_dim,)), ((), ())), preferred_element_type=FULL
    )


def attention_kernel(
    proj_ref, grad_ref, start_ref, cos_ref, sin_ref, att_ref, dqkv_ref, sums_ref,
    q_st, g_st, k_low, v_low, k_turn, v_turn, dk_sum, dv_sum, dq_sum,
):
    pair = 2 * HEAD
    scale = 1.0 / math.sqrt(HEAD)
    lane = lax.broadcasted_iota(jnp.int32, (LEN, pair), 1)
    first = lane < HEAD
    near = lane % HEAD < ROT // 2
    cosine, sine = cos_ref[...], sin_ref[...]

    def partner(x):
        return jnp.where(near, pltpu.roll(x, pair - ROT // 2, 1), pltpu.roll(x, ROT // 2, 1))

    def rotate(x):
        return x * cosine + partner(x) * sine

    def unrotate(x):
        return x * cosine - partner(x) * sine

    q = rotate(proj_ref[:, 0:pair]) * scale
    k = rotate(proj_ref[:, pair : 2 * pair])
    v = proj_ref[:, 2 * pair : 3 * pair]
    g = grad_ref[...].astype(FULL)
    zero = jnp.zeros_like(q)
    blocks = LEN // QB
    for stacked, whole in ((q_st, q), (g_st, g)):
        for head, part in enumerate(
            (jnp.where(first, whole, zero), jnp.where(first, zero, whole))
        ):
            stacked[:, head * QB : (head + 1) * QB, :] = part.astype(LOW).reshape(blocks, QB, pair)
    k_low[...] = k.astype(LOW)
    v_low[...] = v.astype(LOW)
    k_turn[...] = k.T.astype(LOW)
    v_turn[...] = v.T.astype(LOW)
    dk_sum[...] = jnp.zeros_like(dk_sum)
    dv_sum[...] = jnp.zeros_like(dv_sum)
    upper = lax.broadcasted_iota(jnp.int32, (pair, QB), 0) < HEAD
    for block in range(blocks):
        begin = max(0, block - BACK) * QB
        keys = slice(begin, (block + 1) * QB)
        rows = slice(block * QB, (block + 1) * QB)
        width = (block + 1) * QB - begin
        key_at = begin + lax.broadcasted_iota(jnp.int32, (width, QB), 0)
        query_at = block * QB + lax.broadcasted_iota(jnp.int32, (width, QB), 1)
        allowed = (key_at >= start_ref[0, block : block + 1, :]) & (key_at <= query_at)
        allowed = jnp.concatenate([allowed, allowed], axis=1)
        queries, grads = q_st[block], g_st[block]
        scores = jnp.where(allowed, matmul(k_low[keys], queries, 1, 1), MASK_VALUE)
        powers = jnp.exp(scores - jnp.max(scores, axis=0, keepdims=True))
        probs = powers * (1.0 / jnp.sum(powers, axis=0, keepdims=True))
        probs_low = probs.astype(LOW)
        prob_grad = matmul(v_low[keys], grads, 1, 1)
        row_dot = jnp.sum(probs * prob_grad, axis=0, keepdims=True)
        score_grad = (probs * (prob_grad - row_dot)).astype(LOW)
        dv_sum[keys] += matmul(probs_low, grads, 1, 0)
        dk_sum[keys] += matmul(score_grad, queries, 1, 0)
        turned = matmul(v_turn[:, keys], probs_low, 1, 0)
        att_ref[rows, :] = jnp.where(upper, turned[:, :QB], turned[:, QB:]).T.astype(LOW)
        turned = matmul(k_turn[:, keys], score_grad, 1, 0)
        dq_sum[rows, :] = jnp.where(upper, turned[:, :QB], turned[:, QB:]).T
    for part, grad in enumerate((unrotate(dq_sum[...] * scale), unrotate(dk_sum[...]), dv_sum[...])):
        columns = slice(part * pair, (part + 1) * pair)
        dqkv_ref[:, columns] = grad.astype(LOW)
        sums_ref[0, :, columns] = jnp.sum(grad, axis=0, keepdims=True)


def attention(projected, grads, starts):
    rows, width = projected.shape
    seqs, pair = rows // LEN, 2 * HEAD
    pairs = width // (3 * pair)
    cosine, sine = rotary_lanes()
    table = pl.BlockSpec((LEN, pair), lambda s, h: (0, 0))
    return pl.pallas_call(
        attention_kernel,
        grid=(seqs, pairs),
        in_specs=[
            pl.BlockSpec((LEN, 3 * pair), lambda s, h: (s, h)),
            pl.BlockSpec((LEN, pair), lambda s, h: (s, h)),
            pl.BlockSpec((1, LEN // QB, QB), lambda s, h: (s, 0, 0)),
            table,
            table,
        ],
        out_specs=[
            pl.BlockSpec((LEN, pair), lambda s, h: (s, h)),
            pl.BlockSpec((LEN, 3 * pair), lambda s, h: (s, h)),
            pl.BlockSpec((1, 1, 3 * pair), lambda s, h: (s, 0, h)),
        ],
        out_shape=[
            jax.ShapeDtypeStruct((rows, pairs * pair), LOW),
            jax.ShapeDtypeStruct((rows, width), LOW),
            jax.ShapeDtypeStruct((seqs, 1, width), FULL),
        ],
        scratch_shapes=[
            pltpu.VMEM((LEN // QB, 2 * QB, pair), LOW),
            pltpu.VMEM((LEN // QB, 2 * QB, pair), LOW),
            pltpu.VMEM((LEN, pair), LOW),
            pltpu.VMEM((LEN, pair), LOW),
            pltpu.VMEM((pair, LEN), LOW),
            pltpu.VMEM((pair, LEN), LOW),
            pltpu.VMEM((LEN, pair), FULL),
            pltpu.VMEM((LEN, pair), FULL),
            pltpu.VMEM((LEN, pair), FULL),
        ],
        compiler_params=pltpu.CompilerParams(vmem_limit_bytes=40 << 20),
        cost_estimate=pl.CostEstimate(
            flops=seqs * pairs * 6 * 2 * 2 * LEN * QB * (BACK + 1) * pair,
            transcendentals=seqs * pairs * 2 * LEN * QB * (BACK + 1),
            bytes_accessed=rows * (width * 6 + pairs * pair * 4),
        ),
        name="attention_both_ways",
    )(projected, grads, starts.reshape(seqs, LEN // QB, QB), cosine, sine)


def swap(value, axis, bit):
    return lax.ppermute(value, axis, [(i, i ^ bit) for i in range(lax.axis_size(axis))])


def sum_over(value, axis):
    bit = 1
    while bit < lax.axis_size(axis):
        value = value + swap(value, axis, bit)
        bit *= 2
    return value


def pick(value, index, axis):
    return lax.dynamic_index_in_dim(value, index, axis, keepdims=False)


def in_order(mine, other, index, axis):
    return jnp.where(
        index == 0, jnp.concatenate([mine, other], axis), jnp.concatenate([other, mine], axis)
    )


def share_over_x(halves, x_at):
    mine = pick(halves, x_at, 1)
    other = swap(pick(halves, 1 - x_at, 1), "x", 1)
    return in_order(mine, other, x_at, 0)


def reduce_over_z(partial, z_at):
    count = lax.axis_size("z")
    blocks = partial.astype(LOW).reshape(count, partial.shape[0] // count, partial.shape[1])
    bit = 1
    while count > 1:
        paired = blocks.reshape(count // 2, 2, *blocks.shape[1:])
        low = (z_at // bit) % 2
        other = swap(pick(paired, 1 - low, 1), "z", bit)
        blocks = pick(paired, low, 1).astype(FULL) + other.astype(FULL)
        count //= 2
        bit *= 2
        if count > 1:
            blocks = blocks.astype(LOW)
    return blocks[0]


def return_over_x(block, x_at):
    rows, columns = block.shape
    parts = block.reshape(2, rows // 2, columns)
    mine = pick(parts, x_at, 0)[:, None, :]
    other = swap(pick(parts, 1 - x_at, 0).astype(LOW), "x", 1)[:, None, :].astype(FULL)
    return in_order(mine, other, x_at, 1)


def by_pair(flat, lead):
    halves = flat.shape[-1] // 2
    pairs = halves // (2 * HEAD)
    shaped = flat.reshape(lead, 3, 2, pairs, 2 * HEAD)
    return shaped.transpose(0, 2, 3, 1, 4).reshape(lead, 2, 3 * halves)


def from_pair(halves, lead):
    pairs = halves.shape[-1] // (6 * HEAD)
    shaped = halves.reshape(lead, 2, pairs, 3, 2 * HEAD)
    return shaped.transpose(0, 3, 1, 2, 4).reshape(lead, 3, 4 * pairs * HEAD)


def body(
    tokens,
    out_grad,
    segments,
    ln_gain,
    ln_bias,
    qkv_weight,
    qkv_bias,
    dense_weight,
    dense_bias,
    fc1_weight,
    fc1_bias,
    fc2_weight,
    fc2_bias,
):
    x_at, z_at = lax.axis_index("x"), lax.axis_index("z")
    weight_rows = qkv_weight.shape[0]
    dense_half = dense_weight.shape[1] // 2
    qkv_half = 3 * dense_half
    hidden_half = fc1_weight.shape[1] // 2

    heads_halves = jnp.concatenate(
        [by_pair(qkv_weight, weight_rows), dense_weight.reshape(weight_rows, 2, dense_half)], axis=2
    )
    heads_full, fc1_full, fc2_full = (
        lax.all_gather(share_over_x(halves, x_at), "z", axis=0, tiled=True)
        for halves in (
            heads_halves,
            fc1_weight.reshape(weight_rows, 2, hidden_half),
            fc2_weight.reshape(weight_rows, 2, hidden_half),
        )
    )
    qkv_full, dense_full = heads_full[:, :qkv_half], heads_full[:, qkv_half:]

    x_hat, inv_std = normalize_rows(tokens)
    normed = (x_hat * ln_gain + ln_bias).astype(LOW)
    all_normed = lax.all_gather(normed, ("x", "t"), axis=0, tiled=True)
    all_grad = lax.all_gather(out_grad, ("x", "t"), axis=0, tiled=True)
    all_segments = in_order(segments, swap(segments, "x", 1), x_at, 0)
    starts = jnp.sum(
        (all_segments[:, None, :] < all_segments[:, :, None]).astype(jnp.int32), axis=2
    )

    bias_here = pick(by_pair(qkv_bias[None], 1)[0], x_at, 0)
    projected = matmul(all_normed, qkv_full, 1, 0) + bias_here
    attended_grad = matmul(all_grad, dense_full, 1, 0).astype(LOW)
    attended, qkv_grad, qkv_sums = attention(projected, attended_grad, starts)

    pre_gelu = matmul(all_normed, fc1_full, 1, 0) + pick(
        fc1_bias.reshape(2, hidden_half), x_at, 0
    )
    value, slope = gelu_both(pre_gelu)
    activated = value.astype(LOW)
    pre_grad_full = matmul(all_grad, fc2_full, 1, 0) * slope
    pre_grad = pre_grad_full.astype(LOW)

    heads_grad = jnp.concatenate(
        [matmul(all_normed, qkv_grad, 0, 0), matmul(all_grad, attended, 0, 0)], axis=1
    )
    heads_grad, fc1_grad, fc2_grad = (
        return_over_x(reduce_over_z(partial, z_at), x_at)
        for partial in (
            heads_grad,
            matmul(all_normed, pre_grad, 0, 0),
            matmul(all_grad, activated, 0, 0),
        )
    )

    branch = lax.psum_scatter(
        (matmul(attended, dense_full, 1, 1) + matmul(activated, fc2_full, 1, 1)).astype(LOW),
        ("x", "t"),
        scatter_dimension=0,
        tiled=True,
    )
    output = (
        tokens.astype(FULL) + branch.astype(FULL) + dense_bias + fc2_bias
    ).astype(LOW)
    normed_grad = lax.psum_scatter(
        (matmul(qkv_grad, qkv_full, 1, 1) + matmul(pre_grad, fc1_full, 1, 1)).astype(LOW),
        ("x", "t"),
        scatter_dimension=0,
        tiled=True,
    ).astype(FULL)
    scaled = normed_grad * ln_gain
    token_grad = inv_std * (
        scaled
        - jnp.mean(scaled, axis=-1, keepdims=True)
        - x_hat * jnp.mean(scaled * x_hat, axis=-1, keepdims=True)
    )
    input_grad = (out_grad.astype(FULL) + token_grad).astype(LOW)

    sums = jnp.concatenate(
        [
            jnp.sum(all_grad.astype(FULL), axis=0),
            jnp.sum(qkv_sums, axis=(0, 1)),
            jnp.sum(pre_grad_full, axis=0),
        ]
    )
    sums = sum_over(sums, "z")
    out_bias_sum, here = sums[:D], sums[D:]
    both = in_order(here[None], swap(here, "x", 1)[None], x_at, 0)
    qkv_bias_grad = from_pair(both[None, :, :qkv_half], 1)[0]
    fc1_bias_grad = both[:, qkv_half:].reshape(2 * hidden_half)
    norm_sums = jnp.stack([jnp.sum(normed_grad * x_hat, axis=0), jnp.sum(normed_grad, axis=0)])
    for axis in ("t", "x", "z"):
        norm_sums = sum_over(norm_sums, axis)
    return (
        output,
        input_grad,
        norm_sums[0],
        norm_sums[1],
        from_pair(heads_grad[:, :, :qkv_half], weight_rows),
        qkv_bias_grad,
        heads_grad[:, :, qkv_half:].reshape(weight_rows, 2 * dense_half),
        out_bias_sum,
        fc1_grad.reshape(weight_rows, 2 * hidden_half),
        fc1_bias_grad,
        fc2_grad.reshape(weight_rows, 2 * hidden_half),
        out_bias_sum,
    )


def solution(mesh):
    dp, tensor = mesh.shape["dp"], mesh.shape["tensor"]
    split = Mesh(np.asarray(mesh.devices).reshape(dp // 2, 2, tensor), ("z", "x", "t"))
    rows = ("z", "x")
    everywhere = ("z", "x", "t")
    return jax.shard_map(
        body,
        mesh=split,
        in_specs=(
            P(everywhere, None),
            P(everywhere, None),
            P(rows, None),
            P(),
            P(),
            P(rows, None, "t"),
            P(None, "t"),
            P(rows, "t"),
            P(),
            P(rows, "t"),
            P("t"),
            P(rows, "t"),
            P(),
        ),
        out_specs=(
            P(everywhere, None),
            P(everywhere, None),
            P(),
            P(),
            P(rows, None, "t"),
            P(None, "t"),
            P(rows, "t"),
            P(),
            P(rows, "t"),
            P("t"),
            P(rows, "t"),
            P(),
        ),
        check_vma=False,
    )
```

```python
import functools
import math

import jax
import jax.numpy as jnp
import numpy as np
from jax import lax
from jax.experimental import pallas as pl
from jax.experimental.pallas import tpu as pltpu
from jax.sharding import Mesh
from jax.sharding import PartitionSpec as P

D = 2048
H = 32
ROT = 32
LEN = 1024
LONGEST = LEN // 3
HEAD = D // H
QB = 128
BACK = -(-(LONGEST - 1) // QB)

EPSILON = 1e-05
GELU_SCALE = math.sqrt(2.0 / math.pi)
GELU_CUBIC = 0.044715
MASK_VALUE = -1e30
ROPE_BASE = 10000.0
LOW = jnp.bfloat16
FULL = jnp.float32


def gelu_both(pre_gelu):
    square = pre_gelu * pre_gelu
    tangent = jnp.tanh(GELU_SCALE * pre_gelu * (1.0 + GELU_CUBIC * square))
    value = 0.5 * pre_gelu * (1.0 + tangent)
    slope = 0.5 * (1.0 + tangent) + 0.5 * pre_gelu * (1.0 - tangent * tangent) * GELU_SCALE * (
        1.0 + 3.0 * GELU_CUBIC * square
    )
    return value, slope


def rotary_lanes():
    half = ROT // 2
    inverse = ROPE_BASE ** (-(2.0 * np.arange(half)) / ROT)
    angles = np.arange(LEN)[:, None] * inverse[None, :]
    rest = np.zeros((LEN, HEAD - ROT))
    cosine = np.concatenate([np.cos(angles), np.cos(angles), rest + 1.0], axis=1)
    sine = np.concatenate([-np.sin(angles), np.sin(angles), rest], axis=1)
    return tuple(jnp.asarray(np.tile(table, (1, 2)), FULL) for table in (cosine, sine))


def matmul(left, right, left_dim, right_dim):
    return lax.dot_general(
        left, right, (((left_dim,), (right_dim,)), ((), ())), preferred_element_type=FULL
    )


def attention_kernel(
    place_ref, proj_ref, grad_ref, start_ref, cos_ref, sin_ref, att_ref, dqkv_ref, sums_ref,
    q_st, g_st, k_low, v_low, k_turn, v_turn, dk_sum, dv_sum, dq_sum,
):
    pair = 2 * HEAD
    scale = 1.0 / math.sqrt(HEAD)
    part_rows = proj_ref.shape[3]
    parts = LEN // part_rows
    lane = lax.broadcasted_iota(jnp.int32, (part_rows, pair), 1)
    first = lane < HEAD
    near = lane % HEAD < ROT // 2
    y_at, core_at = place_ref[0], place_ref[1]

    def where_is(part):
        return (part % 2) ^ core_at, (part // 2) ^ y_at

    def partner(x):
        return jnp.where(near, pltpu.roll(x, pair - ROT // 2, 1), pltpu.roll(x, ROT // 2, 1))

    per_part = part_rows // QB
    for part in range(parts):
        core, y = where_is(part)
        rows = slice(part * part_rows, (part + 1) * part_rows)
        cosine, sine = cos_ref[rows, :], sin_ref[rows, :]
        projected = proj_ref[core, y, 0]
        q = projected[:, 0:pair]
        k = projected[:, pair : 2 * pair]
        v = projected[:, 2 * pair : 3 * pair]
        q = (q * cosine + partner(q) * sine) * scale
        k = k * cosine + partner(k) * sine
        g = grad_ref[core, y, 0].astype(FULL)
        zero = jnp.zeros_like(q)
        for stacked, whole in ((q_st, q), (g_st, g)):
            for head, own in enumerate(
                (jnp.where(first, whole, zero), jnp.where(first, zero, whole))
            ):
                stacked[
                    part * per_part : (part + 1) * per_part, head * QB : (head + 1) * QB, :
                ] = own.astype(LOW).reshape(per_part, QB, pair)
        k_low[rows, :] = k.astype(LOW)
        v_low[rows, :] = v.astype(LOW)
        k_turn[:, rows] = k.T.astype(LOW)
        v_turn[:, rows] = v.T.astype(LOW)
    dk_sum[...] = jnp.zeros_like(dk_sum)
    dv_sum[...] = jnp.zeros_like(dv_sum)
    upper = lax.broadcasted_iota(jnp.int32, (pair, QB), 0) < HEAD
    for block in range(LEN // QB):
        begin = max(0, block - BACK) * QB
        keys = slice(begin, (block + 1) * QB)
        rows = slice(block * QB, (block + 1) * QB)
        width = (block + 1) * QB - begin
        key_at = begin + lax.broadcasted_iota(jnp.int32, (width, QB), 0)
        query_at = block * QB + lax.broadcasted_iota(jnp.int32, (width, QB), 1)
        allowed = (key_at >= start_ref[0, block : block + 1, :]) & (key_at <= query_at)
        allowed = jnp.concatenate([allowed, allowed], axis=1)
        queries, grads = q_st[block], g_st[block]
        scores = jnp.where(allowed, matmul(k_low[keys], queries, 1, 1), MASK_VALUE)
        powers = jnp.exp(scores - jnp.max(scores, axis=0, keepdims=True))
        probs = powers * (1.0 / jnp.sum(powers, axis=0, keepdims=True))
        probs_low = probs.astype(LOW)
        prob_grad = matmul(v_low[keys], grads, 1, 1)
        row_dot = jnp.sum(probs * prob_grad, axis=0, keepdims=True)
        score_grad = (probs * (prob_grad - row_dot)).astype(LOW)
        dv_sum[keys] += matmul(probs_low, grads, 1, 0)
        dk_sum[keys] += matmul(score_grad, queries, 1, 0)
        turned = matmul(v_turn[:, keys], probs_low, 1, 0)
        core, y = where_is(block // per_part)
        here = slice((block % per_part) * QB, (block % per_part + 1) * QB)
        att_ref[core, y, 0, here, :] = jnp.where(upper, turned[:, :QB], turned[:, QB:]).T.astype(LOW)
        turned = matmul(k_turn[:, keys], score_grad, 1, 0)
        dq_sum[rows, :] = jnp.where(upper, turned[:, :QB], turned[:, QB:]).T
    totals = [jnp.zeros((1, pair), FULL)] * 3
    for part in range(parts):
        core, y = where_is(part)
        rows = slice(part * part_rows, (part + 1) * part_rows)
        cosine, sine = cos_ref[rows, :], sin_ref[rows, :]
        dq, dk = dq_sum[rows, :] * scale, dk_sum[rows, :]
        grads = (
            dq * cosine - partner(dq) * sine,
            dk * cosine - partner(dk) * sine,
            dv_sum[rows, :],
        )
        for at, grad in enumerate(grads):
            dqkv_ref[core, y, 0, :, at * pair : (at + 1) * pair] = grad.astype(LOW)
            totals[at] = totals[at] + jnp.sum(grad, axis=0, keepdims=True)
    for at, total in enumerate(totals):
        sums_ref[0, :, at * pair : (at + 1) * pair] = total


def attention(projected, grads, starts, place):
    rows, width = projected.shape
    seqs, pair = rows // LEN, 2 * HEAD
    pairs = width // (3 * pair)
    part_rows = rows // 8
    cosine, sine = rotary_lanes()
    table = pl.BlockSpec((LEN, pair), lambda s, h, place: (0, 0))

    def block(columns):
        return pl.BlockSpec((2, 2, 1, part_rows, columns), lambda s, h, place: (0, 0, s, 0, h))

    def view(columns):
        return (2, 2, seqs, part_rows, columns)

    attended, grad, sums = pl.pallas_call(
        attention_kernel,
        grid_spec=pltpu.PrefetchScalarGridSpec(
            num_scalar_prefetch=1,
            grid=(seqs, pairs),
            in_specs=[
                block(3 * pair),
                block(pair),
                pl.BlockSpec((1, LEN // QB, QB), lambda s, h, place: (s, 0, 0)),
                table,
                table,
            ],
            out_specs=[
                block(pair),
                block(3 * pair),
                pl.BlockSpec((1, 1, 3 * pair), lambda s, h, place: (s, 0, h)),
            ],
            scratch_shapes=[
                pltpu.VMEM((LEN // QB, 2 * QB, pair), LOW),
                pltpu.VMEM((LEN // QB, 2 * QB, pair), LOW),
                pltpu.VMEM((LEN, pair), LOW),
                pltpu.VMEM((LEN, pair), LOW),
                pltpu.VMEM((pair, LEN), LOW),
                pltpu.VMEM((pair, LEN), LOW),
                pltpu.VMEM((LEN, pair), FULL),
                pltpu.VMEM((LEN, pair), FULL),
                pltpu.VMEM((LEN, pair), FULL),
            ],
        ),
        out_shape=[
            jax.ShapeDtypeStruct(view(pairs * pair), LOW),
            jax.ShapeDtypeStruct(view(width), LOW),
            jax.ShapeDtypeStruct((seqs, 1, width), FULL),
        ],
        compiler_params=pltpu.CompilerParams(vmem_limit_bytes=40 << 20),
        cost_estimate=pl.CostEstimate(
            flops=seqs * LEN * QB * (BACK + 1) * pair // 8,
            transcendentals=0,
            bytes_accessed=rows * width // 8,
        ),
        name="attention_both_ways",
    )(
        place,
        projected.reshape(view(width)),
        grads.reshape(view(pairs * pair)),
        starts.reshape(seqs, LEN // QB, QB),
        cosine,
        sine,
    )
    return attended.reshape(rows, pairs * pair), grad.reshape(rows, width), sums


def swap(value, axis, bit):
    return lax.ppermute(value, axis, [(i, i ^ bit) for i in range(lax.axis_size(axis))])


def sum_over(value, axis):
    bit = 1
    while bit < lax.axis_size(axis):
        value = value + swap(value, axis, bit)
        bit *= 2
    return value


def normalize_rows(token_rows):
    values = token_rows.astype(FULL)
    centered = values - jnp.mean(values, axis=-1, keepdims=True)
    inv_std = lax.rsqrt(jnp.mean(centered * centered, axis=-1, keepdims=True) + EPSILON)
    return centered * inv_std, inv_std


def row_blocks(columns, rows):
    return pl.BlockSpec((rows, columns), lambda i, *_: (i, 0))


def resident(*shape):
    return pl.BlockSpec(shape, lambda i, *_: (0,) * len(shape), pipeline_mode=pl.Buffered(1))


def like(*shape, dtype=LOW):
    return jax.ShapeDtypeStruct(shape, dtype)


def run_kernel(kernel, steps, in_specs, out_specs, out_shape, name, *operands, scalars=()):
    if scalars:
        scalars = (jnp.stack([jnp.asarray(scalar, jnp.int32) for scalar in scalars]),)
    return pl.pallas_call(
        kernel,
        grid_spec=pltpu.PrefetchScalarGridSpec(
            num_scalar_prefetch=len(scalars),
            grid=(steps,),
            in_specs=in_specs,
            out_specs=out_specs,
        ),
        out_shape=out_shape,
        compiler_params=pltpu.CompilerParams(vmem_limit_bytes=52 << 20),
        cost_estimate=pl.CostEstimate(flops=1 << 24, transcendentals=0, bytes_accessed=1 << 18),
        name=name,
    )(*scalars, *operands)


def whole(*values):
    return [resident(*value.shape) for value in values]


def halves_kernel(low_ref, *refs):
    count = len(refs) // 3
    for source, mine, given in zip(refs[:count], refs[count : 2 * count], refs[2 * count :]):
        columns = mine.shape[1]
        for target, at in ((mine, low_ref[0]), (given, 1 - low_ref[0])):
            target[...] = source[:, pl.ds(pl.multiple_of(at * columns, columns), columns)]


def halves_of(low_at, *weights):
    outs = [like(weight.shape[0], weight.shape[1] // 2) for weight in weights] * 2
    found = run_kernel(
        halves_kernel, 1, whole(*weights), whole(*outs), outs, "halves", *weights, scalars=[low_at]
    )
    return found[: len(weights)], found[len(weights) :]


def heads_halves_kernel(low_ref, q_ref, k_ref, v_ref, dense_ref, mine_ref, given_ref):
    pair = 2 * HEAD
    half = dense_ref.shape[1] // 2
    for target, at in ((mine_ref, low_ref[0]), (given_ref, 1 - low_ref[0])):
        for which in range(half // pair):
            columns = pl.ds(pl.multiple_of(at * half + which * pair, pair), pair)
            for part, source in enumerate((q_ref, k_ref, v_ref)):
                begin = (3 * which + part) * pair
                target[:, begin : begin + pair] = source[:, columns]
        target[:, 3 * half :] = dense_ref[:, pl.ds(pl.multiple_of(at * half, half), half)]


def heads_halves(low_at, qkv_weight, dense_weight):
    operands = (*(qkv_weight[:, part] for part in range(3)), dense_weight)
    out = like(dense_weight.shape[0], 2 * dense_weight.shape[1])
    return run_kernel(
        heads_halves_kernel,
        1,
        whole(*operands),
        whole(out, out),
        [out, out],
        "heads_halves",
        *operands,
        scalars=[low_at],
    )


def shard_kernel(low_ref, mine_ref, got_ref, *shard_refs):
    rows, columns = mine_ref.shape[0], shard_refs[0].shape[1]
    for source, at in ((mine_ref, low_ref[0]), (got_ref, 1 - low_ref[0])):
        for which, shard_ref in enumerate(shard_refs):
            here = slice(which * columns, (which + 1) * columns)
            shard_ref[pl.ds(pl.multiple_of(at * rows, rows), rows), :] = source[:, here]


def shards_of(low_at, mine, got):
    out = like(2 * mine.shape[0], mine.shape[1] // 2)
    return run_kernel(
        shard_kernel,
        1,
        whole(mine, got),
        whole(out, out),
        [out, out],
        "shards",
        mine,
        got,
        scalars=[low_at],
    )


def place_kernel(at_ref, *refs):
    *pieces, full = refs
    rows = pieces[0].shape[0] // 2
    for at, piece in enumerate(pieces):
        slot = 4 * (at_ref[0] ^ (at // 2)) + (at_ref[1] ^ (at % 2))
        for low in (0, 1):
            begin = pl.multiple_of((slot + 2 * low) * rows, rows)
            full[pl.ds(begin, rows), :] = piece[low * rows : (low + 1) * rows, :]


def place_pieces(high_at, x_at, *pieces):
    rows, columns = pieces[0].shape
    steps = 2
    block = pl.BlockSpec((rows, columns // steps), lambda i, *_: (0, i))
    return run_kernel(
        place_kernel,
        steps,
        [block] * 4,
        pl.BlockSpec((4 * rows, columns // steps), lambda i, *_: (0, i)),
        like(4 * rows, columns),
        "place_pieces",
        *pieces,
        scalars=[high_at, x_at],
    )


def from_piece(pieces, use):
    for at, piece in enumerate(pieces):

        @pl.when(pl.program_id(0) == at)
        def _(piece=piece):
            use(piece)


def normalize_kernel(*refs):
    *pieces, gain_ref, shift_ref, normed_ref = refs

    def use(piece):
        x_hat, _ = normalize_rows(piece[...])
        normed_ref[...] = (x_hat * gain_ref[...] + shift_ref[...]).astype(LOW)

    from_piece(pieces, use)


def normalize_all(pieces, gain, shift):
    step, width = pieces[0].shape
    return run_kernel(
        normalize_kernel,
        len(pieces),
        whole(*pieces, gain, shift),
        row_blocks(width, step),
        like(step * len(pieces), width),
        "normalize_all",
        *pieces,
        gain,
        shift,
    )


def stack_kernel(*refs):
    *pieces, whole_ref, sums_ref = refs

    @pl.when(pl.program_id(0) == 0)
    def _():
        sums_ref[...] = jnp.zeros_like(sums_ref)

    def use(piece):
        whole_ref[...] = piece[...]
        sums_ref[...] += jnp.sum(piece[...].astype(FULL), axis=0, keepdims=True)

    from_piece(pieces, use)


def stack_pieces(pieces):
    step, width = pieces[0].shape
    return run_kernel(
        stack_kernel,
        len(pieces),
        whole(*pieces),
        [row_blocks(width, step), resident(1, width)],
        [like(step * len(pieces), width), like(1, width, dtype=FULL)],
        "stack_pieces",
        *pieces,
    )


def column_parts(width, count):
    return [slice(at * width // count, (at + 1) * width // count) for at in range(count)]


def hidden_kernel(normed_ref, *refs):
    *weight_refs, bias_ref, activated_ref, slope_ref = refs
    for weight_ref, here in zip(weight_refs, column_parts(bias_ref.shape[1], len(weight_refs))):
        pre_gelu = matmul(normed_ref[...], weight_ref[...], 1, 0) + bias_ref[:, here]
        value, slope = gelu_both(pre_gelu)
        activated_ref[:, here] = value.astype(LOW)
        slope_ref[:, here] = slope.astype(LOW)


def hidden_forward(normed, weights, bias):
    rows, columns, step = normed.shape[0], bias.shape[1], 256
    return run_kernel(
        hidden_kernel,
        rows // step,
        [row_blocks(normed.shape[1], step), *whole(*weights, bias)],
        [row_blocks(columns, step)] * 2,
        [like(rows, columns)] * 2,
        "hidden_forward",
        normed,
        *weights,
        bias,
    )


def hidden_back_kernel(grad_ref, *refs):
    *weight_refs, slope_ref, pre_grad_ref, sums_ref = refs

    @pl.when(pl.program_id(0) == 0)
    def _():
        sums_ref[...] = jnp.zeros_like(sums_ref)

    for weight_ref, here in zip(weight_refs, column_parts(slope_ref.shape[1], len(weight_refs))):
        pre_grad = matmul(grad_ref[...], weight_ref[...], 1, 0) * slope_ref[:, here].astype(FULL)
        pre_grad_ref[:, here] = pre_grad.astype(LOW)
        sums_ref[:, here] += jnp.sum(pre_grad, axis=0, keepdims=True)


def hidden_back(grad, weights, slope):
    rows, columns, step = grad.shape[0], slope.shape[1], 256
    return run_kernel(
        hidden_back_kernel,
        rows // step,
        [row_blocks(grad.shape[1], step), *whole(*weights), row_blocks(columns, step)],
        [row_blocks(columns, step), resident(1, columns)],
        [like(rows, columns), like(1, columns, dtype=FULL)],
        "hidden_back",
        grad,
        *weights,
        slope,
    )


def heads_kernel(normed_ref, grad_ref, left_ref, right_ref, bias_ref, projected_ref, back_ref):
    columns = left_ref.shape[1]
    split = projected_ref.shape[1] - columns
    projected_ref[:, :columns] = (
        matmul(normed_ref[...], left_ref[...], 1, 0) + bias_ref[:, :columns]
    )
    projected_ref[:, columns:] = (
        matmul(normed_ref[...], right_ref[:, :split], 1, 0) + bias_ref[:, columns:]
    )
    back_ref[...] = matmul(grad_ref[...], right_ref[:, split:], 1, 0).astype(LOW)


def heads_inputs(normed, grad, weights, bias):
    rows, split, step = normed.shape[0], bias.shape[1], 256
    columns = sum(weight.shape[1] for weight in weights) - split
    return run_kernel(
        heads_kernel,
        rows // step,
        [
            row_blocks(normed.shape[1], step),
            row_blocks(grad.shape[1], step),
            *whole(*weights, bias),
        ],
        [row_blocks(split, step), row_blocks(columns, step)],
        [like(rows, split, dtype=FULL), like(rows, columns)],
        "heads_inputs",
        normed,
        grad,
        *weights,
        bias,
    )


def products_of(lefts, rights):
    values = [matmul(left[...], right[...], 0, 0).astype(LOW) for left, right in zip(lefts, rights)]
    return values[0] if len(values) == 1 else jnp.concatenate(values, axis=1)


def weight_grad_kernel(count, x_ref, *refs):
    lefts, rights, outs = refs[:count], refs[count : 2 * count], refs[2 * count :]
    value = products_of(lefts, rights)
    columns = outs[0].shape[1]
    for first, targets in ((True, outs[:2]), (False, outs[2:])):

        @pl.when((pl.program_id(0) < 4) == first)
        def _(targets=targets):
            for which, target in enumerate(targets):
                target[...] = value[:, which * columns : (which + 1) * columns]


def weight_grad(x_at, *products):
    lefts, rights = zip(*products)
    tokens, width = lefts[0].shape
    columns, step = sum(right.shape[1] for right in rights) // 2, width // 8

    def rows_of(i, x_ref):
        return (0, (i % 4) * 2 + jnp.where(i < 4, 1 - x_ref[0], x_ref[0]))

    return run_kernel(
        functools.partial(weight_grad_kernel, len(products)),
        8,
        [pl.BlockSpec((tokens, step), rows_of)] * len(products) + whole(*rights),
        [pl.BlockSpec((step, columns), lambda i, *_: (jnp.minimum(i, 3), 0))] * 2
        + [pl.BlockSpec((step, columns), lambda i, *_: (jnp.maximum(i - 4, 0), 0))] * 2,
        [like(width // 2, columns)] * 4,
        "weight_grad",
        *lefts,
        *rights,
        scalars=[x_at],
    )


def weight_grad_plain_kernel(count, *refs):
    lefts, rights, outs = refs[:count], refs[count : 2 * count], refs[2 * count :]
    value = products_of(lefts, rights)
    for out_ref, here in zip(outs, column_parts(value.shape[1], 2)):
        out_ref[...] = value[:, here]


def weight_grad_plain(*products):
    lefts, rights = zip(*products)
    tokens, width = lefts[0].shape
    columns, step = sum(right.shape[1] for right in rights) // 2, 256
    return run_kernel(
        functools.partial(weight_grad_plain_kernel, len(products)),
        width // step,
        [pl.BlockSpec((tokens, step), lambda i, *_: (0, i))] * len(products) + whole(*rights),
        [row_blocks(columns, step)] * 2,
        [like(width, columns)] * 2,
        "weight_grad",
        *lefts,
        *rights,
    )


def fold_kernel(at_ref, kept_ref, got_ref, mine_ref, given_ref):
    rows = mine_ref.shape[0]
    for target, at in ((mine_ref, at_ref[0]), (given_ref, 1 - at_ref[0])):
        here = pl.ds(pl.multiple_of(at * rows, rows), rows)
        target[...] = (kept_ref[here, :].astype(FULL) + got_ref[here, :].astype(FULL)).astype(LOW)


def fold(at, kept, got):
    out = like(kept.shape[0] // 2, kept.shape[1])
    return run_kernel(
        fold_kernel, 1, whole(kept, got), whole(out, out), [out, out], "fold", kept, got, scalars=[at]
    )


def final_kernel(low_ref, *refs):
    *pairs, out_ref = refs
    columns = pairs[0].shape[1]
    for which in (0, 1):
        for source, at in ((pairs[2 * which], low_ref[0]), (pairs[2 * which + 1], 1 - low_ref[0])):
            begin = pl.multiple_of((2 * at + which) * columns, columns)
            out_ref[:, pl.ds(begin, columns)] = source[...].astype(FULL)


def final_grad(low_at, *pairs):
    out = like(pairs[0].shape[0], 4 * pairs[0].shape[1], dtype=FULL)
    return run_kernel(
        final_kernel, 1, whole(*pairs), resident(*out.shape), out, "final_grad", *pairs, scalars=[low_at]
    )


def final_heads_kernel(low_ref, *refs):
    pairs, (q_ref, k_ref, v_ref, dense_ref) = refs[:4], refs[4:]
    pair = 2 * HEAD
    half = dense_ref.shape[1] // 2
    for own, at in ((0, low_ref[0]), (1, 1 - low_ref[0])):
        source = jnp.concatenate([pairs[own][...], pairs[2 + own][...]], axis=1).astype(FULL)
        for which in range(half // pair):
            columns = pl.ds(pl.multiple_of(at * half + which * pair, pair), pair)
            for part, target in enumerate((q_ref, k_ref, v_ref)):
                begin = (3 * which + part) * pair
                target[:, columns] = source[:, begin : begin + pair]
        dense_ref[:, pl.ds(pl.multiple_of(at * half, half), half)] = source[:, 3 * half :]


def final_heads(low_at, *pairs):
    out = like(pairs[0].shape[0], pairs[0].shape[1], dtype=FULL)
    return run_kernel(
        final_heads_kernel,
        1,
        whole(*pairs),
        whole(*[out] * 4),
        [out] * 4,
        "final_heads",
        *pairs,
        scalars=[low_at],
    )


def sum_of_products(left_refs, right_refs, terms):
    total = None
    for left_at, left_columns, right_at, right_columns in terms:
        product = matmul(left_refs[left_at][:, left_columns], right_refs[right_at][:, right_columns], 1, 1)
        total = product if total is None else total + product
    return total


def far_rows_first(i):
    return jnp.where(i < 4, i + 4, i - 4)


def to_given_or_kept(value, given_ref, kept_ref):
    @pl.when(pl.program_id(0) < 4)
    def _():
        given_ref[...] = value

    @pl.when(pl.program_id(0) >= 4)
    def _():
        kept_ref[...] = value


def branch_kernel(counts, terms, *refs):
    lefts, rights = refs[: counts[0]], refs[counts[0] : sum(counts)]
    total = sum_of_products(lefts, rights, terms)
    to_given_or_kept(total.astype(LOW), *refs[sum(counts) :])


def token_grad_kernel(counts, terms, *refs):
    lefts, rights = refs[: counts[0]], refs[counts[0] : sum(counts)]
    pieces, (given_ref, kept_ref, sums_ref) = refs[sum(counts) : -3], refs[-3:]

    @pl.when(pl.program_id(0) == 0)
    def _():
        sums_ref[...] = jnp.zeros_like(sums_ref)

    grad = sum_of_products(lefts, rights, terms)
    to_given_or_kept(grad.astype(LOW), given_ref, kept_ref)
    sums_ref[1:2, :] += jnp.sum(grad, axis=0, keepdims=True)

    def use(piece):
        x_hat, _ = normalize_rows(piece[...])
        sums_ref[0:1, :] += jnp.sum(grad * x_hat, axis=0, keepdims=True)

    from_piece([*pieces[4:], *pieces[:4]], use)


def over_tokens(kernel, name, lefts, rights, terms, pieces=()):
    rows, width = lefts[0].shape[0], rights[0].shape[0]
    step = rows // 8
    sums = [like(2, width, dtype=FULL)] if pieces else []
    return run_kernel(
        functools.partial(kernel, (len(lefts), len(rights)), terms),
        8,
        [
            pl.BlockSpec((step, left.shape[1]), lambda i, *_: (far_rows_first(i), 0))
            for left in lefts
        ]
        + whole(*rights, *pieces),
        [
            pl.BlockSpec((step, width), lambda i, *_: (jnp.minimum(i, 3), 0)),
            pl.BlockSpec((step, width), lambda i, *_: (jnp.maximum(i - 4, 0), 0)),
            *whole(*sums),
        ],
        [like(rows // 2, width)] * 2 + sums,
        name,
        *lefts,
        *rights,
        *pieces,
    )


def link_kernel(kept_ref, got_ref, left_ref, left_given_ref, right_ref, right_given_ref):
    quarter, columns = left_ref.shape
    part = quarter // 2
    y, low = pl.program_id(0) // 2, pl.program_id(0) % 2
    held = (kept_ref[...].astype(FULL) + got_ref[...].astype(FULL)).astype(LOW)

    for at in range(4):

        @pl.when(pl.program_id(0) == at)
        def _(y=at // 2, low=at % 2):
            left = left_given_ref if y else left_ref
            left[low * part : (low + 1) * part, :] = held[:, :columns]
            right = right_given_ref if low else right_ref
            right[y * part : (y + 1) * part, :] = held[:, columns:]


def link_stage(kept, got):
    rows, width = kept.shape
    out = like(rows // 2, width // 2)
    return run_kernel(
        link_kernel,
        4,
        [row_blocks(width, rows // 4)] * 2,
        whole(*[out] * 4),
        [out] * 4,
        "link_stage",
        kept,
        got,
    )


def last_kernel(left_ref, left_got_ref, right_ref, right_got_ref, *outs):
    rows = outs[0].shape[0]
    pairs = ((left_ref, left_got_ref), (right_ref, right_got_ref))
    for at, (kept_ref, got_ref) in enumerate(pairs):
        total = (kept_ref[...].astype(FULL) + got_ref[...].astype(FULL)).astype(LOW)
        outs[2 * at][...] = total[:rows]
        outs[2 * at + 1][...] = total[rows:]


def last_stage(*values):
    rows, columns = values[0].shape
    out = like(rows // 2, columns)
    return run_kernel(
        last_kernel, 1, whole(*values), whole(*[out] * 4), [out] * 4, "last_stage", *values
    )


def joined(refs):
    left, left_got, right, right_got = (ref[...].astype(FULL) for ref in refs)
    return jnp.concatenate([left + left_got, right + right_got], axis=1)


def output_kernel(*refs):
    tokens_ref, dense_bias_ref, fc2_bias_ref, output_ref = refs[4:]
    total = tokens_ref[...].astype(FULL) + joined(refs[:4])
    output_ref[...] = (total + dense_bias_ref[...] + fc2_bias_ref[...]).astype(LOW)


def input_grad_kernel(*refs):
    tokens_ref, out_grad_ref, gain_ref, grad_ref = refs[4:]
    x_hat, inv_std = normalize_rows(tokens_ref[...])
    scaled = joined(refs[:4]) * gain_ref[...]
    token_grad = inv_std * (
        scaled
        - jnp.mean(scaled, axis=-1, keepdims=True)
        - x_hat * jnp.mean(scaled * x_hat, axis=-1, keepdims=True)
    )
    grad_ref[...] = (out_grad_ref[...].astype(FULL) + token_grad).astype(LOW)


def row_result(kernel, name, *operands):
    out = like(*operands[4].shape)
    return run_kernel(kernel, 1, whole(*operands), resident(*out.shape), out, name, *operands)


def body(
    tokens,
    out_grad,
    segments,
    ln_gain,
    ln_bias,
    qkv_weight,
    qkv_bias,
    dense_weight,
    dense_bias,
    fc1_weight,
    fc1_bias,
    fc2_weight,
    fc2_bias,
):
    low_at, high_at, x_at = lax.axis_index("zl"), lax.axis_index("zh"), lax.axis_index("x")
    t_at = lax.axis_index("t")
    pairwise = lax.axis_size("zh") == 2
    place = jnp.stack([t_at // 2, t_at % 2]).astype(jnp.int32)
    weight_rows = qkv_weight.shape[0]
    pair = 2 * HEAD
    half = dense_weight.shape[1] // 2
    pairs = half // pair
    hidden = fc1_weight.shape[1] // 2

    before = [()]

    def sync(*values):
        before[0] = lax.optimization_barrier((values, before[0]))[0]
        return before[0]

    def to_low(value):
        return swap(value, "zl", 1)

    def to_high(value):
        return swap(value, "zh", 1)

    def to_x(value):
        return swap(value, "x", 1)

    def to_y(value):
        return swap(value, "t", 2)

    def to_core(value):
        return swap(value, "t", 1)

    class Gather:
        def __init__(self, shard):
            self.own = shard
            self.moving = []

        def start(self):
            if pairwise:
                self.moving = [to_high(self.own), to_x(self.own)]
            else:
                rows, columns = self.own.shape
                gathered = lax.all_gather(self.own, ("zh", "x"), axis=0, tiled=True)
                natural = gathered.reshape(-1, 2, 2, rows // 2, columns).transpose(0, 2, 1, 3, 4)
                self.moving = [natural.reshape(-1, columns)]

        def forward(self):
            if pairwise:
                self.high, self.x = self.moving
                self.moving = [to_x(self.high)]

        def whole(self):
            if pairwise:
                return place_pieces(high_at, x_at, self.own, self.x, self.high, self.moving[0])
            return self.moving[0]

    class Sum:
        def __init__(self, given, kept):
            self.given, self.kept = given, kept
            self.moving = []

        def start(self):
            if pairwise:
                self.moving = [to_x(self.given)]
            else:
                rows, columns = self.given.shape
                blocks = self.given.reshape(-1, 2, 2, weight_rows, columns)
                ordered = blocks.transpose(0, 2, 1, 3, 4).reshape(rows, columns)
                self.moving = [
                    lax.psum_scatter(ordered, ("zh", "x"), scatter_dimension=0, tiled=True)
                ]

        def second(self):
            if pairwise:
                self.kept, given = fold(high_at, self.kept, self.moving[0])
                self.moving = [to_high(given)]

        def third(self):
            other = self.kept if pairwise else jnp.zeros_like(self.moving[0])
            self.kept, given = fold(low_at, other, self.moving[0])
            self.moving = [to_low(given)]

        def halves(self):
            return [self.kept, self.moving[0]]

    def segment(values, *transfers):
        tied = sync(*values, *[piece for transfer in transfers for piece in transfer.moving])
        at = len(values)
        for transfer in transfers:
            many = len(transfer.moving)
            transfer.moving = list(tied[at : at + many])
            at += many
        return tied[: len(values)]

    def gathers_of(mine, got):
        return [Gather(shard) for shard in sync(*shards_of(low_at, mine, got))]

    def sums_of(*products):
        if pairwise:
            given_a, given_b, kept_a, kept_b = weight_grad(x_at, *products)
        else:
            given_a, given_b = weight_grad_plain(*products)
            kept_a = kept_b = given_a
        return [given_a, given_b, kept_a, kept_b]

    def as_sums(tied):
        return [Sum(tied[0], tied[2]), Sum(tied[1], tied[3])]

    (fc1_mine,), (fc1_given,) = halves_of(low_at, fc1_weight)
    fc1_given, tokens, out_grad, segments, qkv_weight, dense_weight, fc2_weight = sync(
        fc1_given, tokens, out_grad, segments, qkv_weight, dense_weight, fc2_weight
    )
    got = to_low(fc1_given)
    tokens_core, grad_core = to_core(tokens), to_core(out_grad)
    heads_mine, heads_given = heads_halves(low_at, qkv_weight, dense_weight)
    (fc2_mine,), (fc2_given,) = halves_of(low_at, fc2_weight)
    got, tokens_core, grad_core, heads_given, fc2_given, tokens, out_grad, segments = sync(
        got, tokens_core, grad_core, heads_given, fc2_given, tokens, out_grad, segments
    )
    fc1_a, fc1_b = gathers_of(fc1_mine, got)
    tokens, out_grad, segments, heads_given, fc2_given = sync(
        tokens, out_grad, segments, heads_given, fc2_given
    )
    fc1_a.start()
    tokens_low, tokens_y, segments_low = to_low(tokens), to_y(tokens), to_low(segments)
    tokens_low, tokens_y, segments_low, heads_given, fc1_b.own, fc2_given, out_grad = segment(
        [tokens_low, tokens_y, segments_low, heads_given, fc1_b.own, fc2_given, out_grad], fc1_a
    )
    fc1_a.forward()
    fc1_b.start()
    tokens_both, got = to_y(tokens_low), to_low(heads_given)
    tokens_low_core, tokens_y_core = to_core(tokens_low), to_core(tokens_y)
    all_segments = jnp.concatenate([segments, segments_low])
    starts = jnp.sum(
        (all_segments[:, None, :] < all_segments[:, :, None]).astype(jnp.int32), axis=2
    )
    tokens_both, got, tokens_low_core, tokens_y_core, starts, fc2_given, out_grad = segment(
        [tokens_both, got, tokens_low_core, tokens_y_core, starts, fc2_given, out_grad],
        fc1_a,
        fc1_b,
    )
    tokens_both_core = to_core(tokens_both)
    shards = shards_of(low_at, heads_mine, got)
    tokens_both_core, fc2_given, out_grad, *shards = sync(
        tokens_both_core, fc2_given, out_grad, *shards
    )
    heads_a, heads_b = (Gather(shard) for shard in shards)
    fc1_b.forward()
    heads_a.start()
    grad_low, grad_y = to_low(out_grad), to_y(out_grad)
    token_pieces = [
        tokens,
        tokens_low,
        tokens_y,
        tokens_both,
        tokens_core,
        tokens_low_core,
        tokens_y_core,
        tokens_both_core,
    ]
    all_normed = normalize_all(token_pieces, ln_gain[None], ln_bias[None])
    fc1_full = [fc1_a.whole()]
    all_normed, fc1_full[0], grad_low, grad_y, heads_b.own, fc2_given = segment(
        [all_normed, fc1_full[0], grad_low, grad_y, heads_b.own, fc2_given], fc1_b, heads_a
    )
    heads_a.forward()
    heads_b.start()
    grad_both, got = to_y(grad_low), to_low(fc2_given)
    grad_low_core, grad_y_core = to_core(grad_low), to_core(grad_y)
    fc1_full.append(fc1_b.whole())
    bias = lax.dynamic_slice_in_dim(fc1_bias, low_at * hidden, hidden, 0)[None]
    activated, slope = hidden_forward(all_normed, fc1_full, bias)
    activated, slope, grad_both, got, grad_low_core, grad_y_core = segment(
        [activated, slope, grad_both, got, grad_low_core, grad_y_core], heads_a, heads_b
    )
    grad_both_core = to_core(grad_both)
    grad_both_core, *shards = sync(grad_both_core, *shards_of(low_at, fc2_mine, got))
    fc2_a, fc2_b = (Gather(shard) for shard in shards)
    heads_b.forward()
    fc2_a.start()
    all_grad, grad_sums = stack_pieces(
        [
            out_grad,
            grad_low,
            grad_y,
            grad_both,
            grad_core,
            grad_low_core,
            grad_y_core,
            grad_both_core,
        ]
    )
    heads_full = [heads_a.whole()]
    all_grad, heads_full[0], *partials, fc2_b.own = segment(
        [all_grad, heads_full[0], *sums_of((all_grad, activated)), fc2_b.own], heads_b, fc2_a
    )
    d_fc2_a, d_fc2_b = as_sums(partials)
    fc2_a.forward()
    fc2_b.start()
    heads_full.append(heads_b.whole())
    bias = lax.dynamic_slice_in_dim(qkv_bias, low_at * half, half, 1)
    bias = bias.reshape(3, pairs, pair).transpose(1, 0, 2).reshape(1, 3 * half)
    projected, back = heads_inputs(all_normed, all_grad, heads_full, bias)
    projected, back, d_fc2_a.given, d_fc2_b.given = segment(
        [projected, back, d_fc2_a.given, d_fc2_b.given], fc2_a, fc2_b
    )
    fc2_b.forward()
    d_fc2_a.start()
    attended, qkv_grad, qkv_sums = attention(projected, back, starts, place)
    fc2_full = [fc2_a.whole()]
    attended, qkv_grad, qkv_sums, fc2_full[0], d_fc2_b.given = segment(
        [attended, qkv_grad, qkv_sums, fc2_full[0], d_fc2_b.given], fc2_b, d_fc2_a
    )
    d_fc2_b.start()
    d_fc2_a.second()
    fc2_full.append(fc2_b.whole())
    partials = sums_of((all_normed, qkv_grad), (all_grad, attended))
    fc2_full[1], *partials = segment([fc2_full[1], *partials], d_fc2_a, d_fc2_b)
    d_heads_a, d_heads_b = as_sums(partials)
    d_heads_a.start()
    d_fc2_b.second()
    d_fc2_a.third()
    columns = heads_full[0].shape[1]
    first, second = slice(0, columns), slice(columns, 2 * columns)
    qkv_end = 3 * half - columns
    everything = slice(None)
    given, branch_kept = over_tokens(
        branch_kernel,
        "branch",
        [attended, activated],
        [heads_full[1], *fc2_full],
        [
            (0, everything, 0, slice(qkv_end, columns)),
            (1, first, 1, everything),
            (1, second, 2, everything),
        ],
    )
    given, branch_kept, d_heads_b.given = segment(
        [given, branch_kept, d_heads_b.given], d_heads_a, d_fc2_a, d_fc2_b
    )
    d_heads_b.start()
    d_heads_a.second()
    d_fc2_b.third()
    branch_got = to_core(given)
    pre_grad, pre_sums = hidden_back(all_grad, fc2_full, slope)
    pre_grad, pre_sums, branch_got = segment(
        [pre_grad, pre_sums, branch_got], d_heads_a, d_heads_b, d_fc2_b
    )
    d_heads_b.second()
    d_heads_a.third()
    left, left_given, right, right_given = link_stage(branch_kept, branch_got)
    branch_state = [left, to_y(left_given), right, to_low(right_given)]
    partials = sums_of((all_normed, pre_grad))
    *partials, left, left_got, right, right_got = segment(
        [*partials, *branch_state], d_heads_a, d_heads_b
    )
    d_fc1_a, d_fc1_b = as_sums(partials)
    d_fc1_a.start()
    d_heads_b.third()
    left, left_given, right, right_given = last_stage(left, left_got, right, right_got)
    branch_state = [left, to_low(left_given), right, to_y(right_given)]
    given, kept, norm_sums = over_tokens(
        token_grad_kernel,
        "token_grad",
        [qkv_grad, pre_grad],
        [*heads_full, *fc1_full],
        [
            (0, first, 0, everything),
            (0, slice(columns, 3 * half), 1, slice(0, qkv_end)),
            (1, first, 2, everything),
            (1, second, 3, everything),
        ],
        token_pieces,
    )
    given, kept, norm_sums, d_fc1_b.given, *branch_state = segment(
        [given, kept, norm_sums, d_fc1_b.given, *branch_state], d_fc1_a, d_heads_b
    )
    d_fc1_b.start()
    d_fc1_a.second()
    got, sums = to_core(given), norm_sums.reshape(2 * D)
    sums_got = to_core(sums)
    output = row_result(
        output_kernel, "output", *branch_state, tokens, dense_bias[None], fc2_bias[None]
    )
    fc2_weight_grad = final_grad(low_at, *d_fc2_a.halves(), *d_fc2_b.halves())
    q, k, v, dense_weight_grad = final_heads(low_at, *d_heads_a.halves(), *d_heads_b.halves())
    got, sums, sums_got, output, fc2_weight_grad, q, k, v, dense_weight_grad = segment(
        [got, sums, sums_got, output, fc2_weight_grad, q, k, v, dense_weight_grad],
        d_fc1_a,
        d_fc1_b,
    )
    left, left_given, right, right_given = link_stage(kept, got)
    grad_state = [left, to_y(left_given), right, to_low(right_given)]
    d_fc1_b.second()
    d_fc1_a.third()
    sums = sums + sums_got
    sums_got = to_y(sums)
    sums, sums_got, *grad_state = segment([sums, sums_got, *grad_state], d_fc1_a, d_fc1_b)
    left, left_given, right, right_given = last_stage(*grad_state)
    grad_state = [left, to_low(left_given), right, to_y(right_given)]
    d_fc1_b.third()
    sums = sums + sums_got
    sums_got = to_low(sums)
    sums, sums_got, *grad_state = segment([sums, sums_got, *grad_state], d_fc1_b)
    here = jnp.concatenate([jnp.sum(qkv_sums, axis=(0, 1)), pre_sums[0]])
    sums = jnp.concatenate([sums + sums_got, grad_sums[0], here])
    bias_got = to_low(here)
    sums = sum_over(sum_over(jnp.concatenate([sums, bias_got]), "zh"), "x")
    input_grad = row_result(
        input_grad_kernel, "input_grad", *grad_state, tokens, out_grad, ln_gain[None]
    )
    fc1_weight_grad = final_grad(low_at, *d_fc1_a.halves(), *d_fc1_b.halves())
    both = sums[3 * D :].reshape(2, here.shape[0])
    both = jnp.where(low_at == 0, both, both[::-1])
    qkv_bias_grad = (
        both[:, : 3 * half].reshape(2, pairs, 3, pair).transpose(2, 0, 1, 3).reshape(3, 2 * half)
    )
    return (
        output,
        input_grad,
        sums[:D],
        sums[D : 2 * D],
        jnp.stack([q, k, v], axis=1),
        qkv_bias_grad,
        dense_weight_grad,
        sums[2 * D : 3 * D],
        fc1_weight_grad,
        both[:, 3 * half :].reshape(2 * hidden),
        fc2_weight_grad,
        sums[2 * D : 3 * D],
    )


def solution(mesh):
    dp, tensor = mesh.shape["dp"], mesh.shape["tensor"]
    rows = ("zh", "zl", "x")
    everywhere = (*rows, "t")
    split = Mesh(np.asarray(mesh.devices).reshape(dp // 4, 2, 2, tensor), everywhere)
    return jax.shard_map(
        body,
        mesh=split,
        in_specs=(
            P(everywhere, None),
            P(everywhere, None),
            P(rows, None),
            P(),
            P(),
            P(rows, None, "t"),
            P(None, "t"),
            P(rows, "t"),
            P(),
            P(rows, "t"),
            P("t"),
            P(rows, "t"),
            P(),
        ),
        out_specs=(
            P(everywhere, None),
            P(everywhere, None),
            P(),
            P(),
            P(rows, None, "t"),
            P(None, "t"),
            P(rows, "t"),
            P(),
            P(rows, "t"),
            P("t"),
            P(rows, "t"),
            P(),
        ),
        check_vma=False,
    )
```

```python
import functools
import math

import jax
import jax.numpy as jnp
import numpy as np
from jax import lax
from jax.experimental import pallas as pl
from jax.experimental.pallas import tpu as pltpu
from jax.sharding import Mesh
from jax.sharding import PartitionSpec as P

D = 2048
H = 32
ROT = 32
LEN = 1024
LONGEST = LEN // 3
HEAD = D // H
QB = 128
BACK = -(-(LONGEST - 1) // QB)

EPSILON = 1e-05
GELU_SCALE = math.sqrt(2.0 / math.pi)
GELU_CUBIC = 0.044715
MASK_VALUE = -1e30
ROPE_BASE = 10000.0
LOW = jnp.bfloat16
FULL = jnp.float32


def gelu_both(pre_gelu):
    square = pre_gelu * pre_gelu
    tangent = jnp.tanh(GELU_SCALE * pre_gelu * (1.0 + GELU_CUBIC * square))
    value = 0.5 * pre_gelu * (1.0 + tangent)
    slope = 0.5 * (1.0 + tangent) + 0.5 * pre_gelu * (1.0 - tangent * tangent) * GELU_SCALE * (
        1.0 + 3.0 * GELU_CUBIC * square
    )
    return value, slope


def rotary_lanes():
    half = ROT // 2
    inverse = ROPE_BASE ** (-(2.0 * np.arange(half)) / ROT)
    angles = np.arange(LEN)[:, None] * inverse[None, :]
    rest = np.zeros((LEN, HEAD - ROT))
    cosine = np.concatenate([np.cos(angles), np.cos(angles), rest + 1.0], axis=1)
    sine = np.concatenate([-np.sin(angles), np.sin(angles), rest], axis=1)
    return tuple(jnp.asarray(np.tile(table, (1, 2)), FULL) for table in (cosine, sine))


def matmul(left, right, left_dim, right_dim):
    return lax.dot_general(
        left, right, (((left_dim,), (right_dim,)), ((), ())), preferred_element_type=FULL
    )


def attention_kernel(
    place_ref, proj_ref, grad_ref, start_ref, cos_ref, sin_ref, att_ref, dqkv_ref, sums_ref,
    q_st, g_st, k_low, v_low, k_turn, v_turn, dk_sum, dv_sum, dq_sum,
):
    pair = 2 * HEAD
    scale = 1.0 / math.sqrt(HEAD)
    part_rows = proj_ref.shape[3]
    parts = LEN // part_rows
    lane = lax.broadcasted_iota(jnp.int32, (part_rows, pair), 1)
    first = lane < HEAD
    near = lane % HEAD < ROT // 2
    y_at, core_at = place_ref[0], place_ref[1]

    def where_is(part):
        return (part % 2) ^ core_at, (part // 2) ^ y_at

    def partner(x):
        return jnp.where(near, pltpu.roll(x, pair - ROT // 2, 1), pltpu.roll(x, ROT // 2, 1))

    per_part = part_rows // QB
    for part in range(parts):
        core, y = where_is(part)
        rows = slice(part * part_rows, (part + 1) * part_rows)
        cosine, sine = cos_ref[rows, :], sin_ref[rows, :]
        projected = proj_ref[core, y, 0]
        q = projected[:, 0:pair]
        k = projected[:, pair : 2 * pair]
        v = projected[:, 2 * pair : 3 * pair]
        q = (q * cosine + partner(q) * sine) * scale
        k = k * cosine + partner(k) * sine
        g = grad_ref[core, y, 0].astype(FULL)
        zero = jnp.zeros_like(q)
        for stacked, whole in ((q_st, q), (g_st, g)):
            for head, own in enumerate(
                (jnp.where(first, whole, zero), jnp.where(first, zero, whole))
            ):
                stacked[
                    part * per_part : (part + 1) * per_part, head * QB : (head + 1) * QB, :
                ] = own.astype(LOW).reshape(per_part, QB, pair)
        k_low[rows, :] = k.astype(LOW)
        v_low[rows, :] = v.astype(LOW)
        k_turn[:, rows] = k.T.astype(LOW)
        v_turn[:, rows] = v.T.astype(LOW)
    dk_sum[...] = jnp.zeros_like(dk_sum)
    dv_sum[...] = jnp.zeros_like(dv_sum)
    upper = lax.broadcasted_iota(jnp.int32, (pair, QB), 0) < HEAD
    for block in range(LEN // QB):
        begin = max(0, block - BACK) * QB
        keys = slice(begin, (block + 1) * QB)
        rows = slice(block * QB, (block + 1) * QB)
        width = (block + 1) * QB - begin
        key_at = begin + lax.broadcasted_iota(jnp.int32, (width, QB), 0)
        query_at = block * QB + lax.broadcasted_iota(jnp.int32, (width, QB), 1)
        allowed = (key_at >= start_ref[0, block : block + 1, :]) & (key_at <= query_at)
        allowed = jnp.concatenate([allowed, allowed], axis=1)
        queries, grads = q_st[block], g_st[block]
        scores = jnp.where(allowed, matmul(k_low[keys], queries, 1, 1), MASK_VALUE)
        powers = jnp.exp(scores - jnp.max(scores, axis=0, keepdims=True))
        probs = powers * (1.0 / jnp.sum(powers, axis=0, keepdims=True))
        probs_low = probs.astype(LOW)
        prob_grad = matmul(v_low[keys], grads, 1, 1)
        row_dot = jnp.sum(probs * prob_grad, axis=0, keepdims=True)
        score_grad = (probs * (prob_grad - row_dot)).astype(LOW)
        dv_sum[keys] += matmul(probs_low, grads, 1, 0)
        dk_sum[keys] += matmul(score_grad, queries, 1, 0)
        turned = matmul(v_turn[:, keys], probs_low, 1, 0)
        core, y = where_is(block // per_part)
        here = slice((block % per_part) * QB, (block % per_part + 1) * QB)
        att_ref[core, y, 0, here, :] = jnp.where(upper, turned[:, :QB], turned[:, QB:]).T.astype(LOW)
        turned = matmul(k_turn[:, keys], score_grad, 1, 0)
        dq_sum[rows, :] = jnp.where(upper, turned[:, :QB], turned[:, QB:]).T
    totals = [jnp.zeros((1, pair), FULL)] * 3
    for part in range(parts):
        core, y = where_is(part)
        rows = slice(part * part_rows, (part + 1) * part_rows)
        cosine, sine = cos_ref[rows, :], sin_ref[rows, :]
        dq, dk = dq_sum[rows, :] * scale, dk_sum[rows, :]
        grads = (
            dq * cosine - partner(dq) * sine,
            dk * cosine - partner(dk) * sine,
            dv_sum[rows, :],
        )
        for at, grad in enumerate(grads):
            dqkv_ref[core, y, 0, :, at * pair : (at + 1) * pair] = grad.astype(LOW)
            totals[at] = totals[at] + jnp.sum(grad, axis=0, keepdims=True)
    for at, total in enumerate(totals):
        sums_ref[0, :, at * pair : (at + 1) * pair] = total


def attention(projected, grads, starts, place):
    rows, width = projected.shape
    seqs, pair = rows // LEN, 2 * HEAD
    pairs = width // (3 * pair)
    part_rows = rows // 8
    cosine, sine = rotary_lanes()
    table = pl.BlockSpec((LEN, pair), lambda s, h, place: (0, 0))

    def block(columns):
        return pl.BlockSpec((2, 2, 1, part_rows, columns), lambda s, h, place: (0, 0, s, 0, h))

    def view(columns):
        return (2, 2, seqs, part_rows, columns)

    attended, grad, sums = pl.pallas_call(
        attention_kernel,
        grid_spec=pltpu.PrefetchScalarGridSpec(
            num_scalar_prefetch=1,
            grid=(seqs, pairs),
            in_specs=[
                block(3 * pair),
                block(pair),
                pl.BlockSpec((1, LEN // QB, QB), lambda s, h, place: (s, 0, 0)),
                table,
                table,
            ],
            out_specs=[
                block(pair),
                block(3 * pair),
                pl.BlockSpec((1, 1, 3 * pair), lambda s, h, place: (s, 0, h)),
            ],
            scratch_shapes=[
                pltpu.VMEM((LEN // QB, 2 * QB, pair), LOW),
                pltpu.VMEM((LEN // QB, 2 * QB, pair), LOW),
                pltpu.VMEM((LEN, pair), LOW),
                pltpu.VMEM((LEN, pair), LOW),
                pltpu.VMEM((pair, LEN), LOW),
                pltpu.VMEM((pair, LEN), LOW),
                pltpu.VMEM((LEN, pair), FULL),
                pltpu.VMEM((LEN, pair), FULL),
                pltpu.VMEM((LEN, pair), FULL),
            ],
        ),
        out_shape=[
            jax.ShapeDtypeStruct(view(pairs * pair), LOW),
            jax.ShapeDtypeStruct(view(width), LOW),
            jax.ShapeDtypeStruct((seqs, 1, width), FULL),
        ],
        compiler_params=pltpu.CompilerParams(vmem_limit_bytes=58 << 20),
        cost_estimate=pl.CostEstimate(
            flops=seqs * LEN * QB * (BACK + 1) * pair // 8,
            transcendentals=0,
            bytes_accessed=rows * width // 8,
        ),
        name="attention_both_ways",
    )(
        place,
        projected.reshape(view(width)),
        grads.reshape(view(pairs * pair)),
        starts.reshape(seqs, LEN // QB, QB),
        cosine,
        sine,
    )
    return attended.reshape(rows, pairs * pair), grad.reshape(rows, width), sums


def swap(value, axis, bit):
    return lax.ppermute(value, axis, [(i, i ^ bit) for i in range(lax.axis_size(axis))])


def swap_both(value, axis, bit, other_axis, other_bit):
    inner = lax.axis_size(other_axis)
    pairs = [
        (i, ((i // inner) ^ bit) * inner + ((i % inner) ^ other_bit))
        for i in range(lax.axis_size(axis) * inner)
    ]
    return lax.ppermute(value, (axis, other_axis), pairs)


def normalize_rows(token_rows):
    values = token_rows.astype(FULL)
    centered = values - jnp.mean(values, axis=-1, keepdims=True)
    inv_std = lax.rsqrt(jnp.mean(centered * centered, axis=-1, keepdims=True) + EPSILON)
    return centered * inv_std, inv_std


def row_blocks(columns, rows):
    return pl.BlockSpec((rows, columns), lambda i, *_: (i, 0))


def resident(*shape):
    return pl.BlockSpec(shape, lambda i, *_: (0,) * len(shape), pipeline_mode=pl.Buffered(1))


def like(*shape, dtype=LOW):
    return jax.ShapeDtypeStruct(shape, dtype)


def run_kernel(kernel, steps, in_specs, out_specs, out_shape, name, *operands, scalars=()):
    if scalars:
        scalars = (jnp.stack([jnp.asarray(scalar, jnp.int32) for scalar in scalars]),)
    return pl.pallas_call(
        kernel,
        grid_spec=pltpu.PrefetchScalarGridSpec(
            num_scalar_prefetch=len(scalars),
            grid=(steps,),
            in_specs=in_specs,
            out_specs=out_specs,
        ),
        out_shape=out_shape,
        compiler_params=pltpu.CompilerParams(vmem_limit_bytes=(52 if steps > 1 else 32) << 20),
        cost_estimate=pl.CostEstimate(flops=1 << 24, transcendentals=0, bytes_accessed=1 << 18),
        name=name,
    )(*scalars, *operands)


def whole(*values):
    return [resident(*value.shape) for value in values]


def halves_kernel(low_ref, *refs):
    count = len(refs) // 3
    for source, mine, given in zip(refs[:count], refs[count : 2 * count], refs[2 * count :]):
        columns = mine.shape[1]
        for target, at in ((mine, low_ref[0]), (given, 1 - low_ref[0])):
            target[...] = source[:, pl.ds(pl.multiple_of(at * columns, columns), columns)]


def halves_of(low_at, *weights):
    outs = [like(weight.shape[0], weight.shape[1] // 2) for weight in weights] * 2
    found = run_kernel(
        halves_kernel, 1, whole(*weights), whole(*outs), outs, "halves", *weights, scalars=[low_at]
    )
    return found[: len(weights)], found[len(weights) :]


def heads_halves_kernel(low_ref, q_ref, k_ref, v_ref, dense_ref, mine_ref, given_ref):
    pair = 2 * HEAD
    half = dense_ref.shape[1] // 2
    for target, at in ((mine_ref, low_ref[0]), (given_ref, 1 - low_ref[0])):
        for which in range(half // pair):
            columns = pl.ds(pl.multiple_of(at * half + which * pair, pair), pair)
            for part, source in enumerate((q_ref, k_ref, v_ref)):
                begin = (3 * which + part) * pair
                target[:, begin : begin + pair] = source[:, columns]
        target[:, 3 * half :] = dense_ref[:, pl.ds(pl.multiple_of(at * half, half), half)]


def heads_halves(low_at, qkv_weight, dense_weight):
    operands = (*(qkv_weight[:, part] for part in range(3)), dense_weight)
    out = like(dense_weight.shape[0], 2 * dense_weight.shape[1])
    return run_kernel(
        heads_halves_kernel,
        1,
        whole(*operands),
        whole(out, out),
        [out, out],
        "heads_halves",
        *operands,
        scalars=[low_at],
    )


def shard_kernel(low_ref, mine_ref, got_ref, *shard_refs):
    rows, columns = mine_ref.shape[0], shard_refs[0].shape[1]
    for source, at in ((mine_ref, low_ref[0]), (got_ref, 1 - low_ref[0])):
        for which, shard_ref in enumerate(shard_refs):
            here = slice(which * columns, (which + 1) * columns)
            shard_ref[pl.ds(pl.multiple_of(at * rows, rows), rows), :] = source[:, here]


def shards_of(low_at, mine, got):
    out = like(2 * mine.shape[0], mine.shape[1] // 2)
    return run_kernel(
        shard_kernel,
        1,
        whole(mine, got),
        whole(out, out),
        [out, out],
        "shards",
        mine,
        got,
        scalars=[low_at],
    )


def place_kernel(at_ref, *refs):
    *pieces, full = refs
    rows = pieces[0].shape[0] // 2
    for at, piece in enumerate(pieces):
        slot = 4 * (at_ref[0] ^ (at // 2)) + (at_ref[1] ^ (at % 2))
        for low in (0, 1):
            begin = pl.multiple_of((slot + 2 * low) * rows, rows)
            full[pl.ds(begin, rows), :] = piece[low * rows : (low + 1) * rows, :]


def place_pieces(high_at, x_at, *pieces):
    rows, columns = pieces[0].shape
    steps = 2
    block = pl.BlockSpec((rows, columns // steps), lambda i, *_: (0, i))
    return run_kernel(
        place_kernel,
        steps,
        [block] * 4,
        pl.BlockSpec((4 * rows, columns // steps), lambda i, *_: (0, i)),
        like(4 * rows, columns),
        "place_pieces",
        *pieces,
        scalars=[high_at, x_at],
    )


def from_piece(pieces, use):
    for at, piece in enumerate(pieces):

        @pl.when(pl.program_id(0) == at)
        def _(piece=piece):
            use(piece)


def normalize_kernel(*refs):
    *pieces, gain_ref, shift_ref, normed_ref = refs

    def use(piece):
        x_hat, _ = normalize_rows(piece[...])
        normed_ref[...] = (x_hat * gain_ref[...] + shift_ref[...]).astype(LOW)

    from_piece(pieces, use)


def normalize_all(pieces, gain, shift):
    step, width = pieces[0].shape
    return run_kernel(
        normalize_kernel,
        len(pieces),
        whole(*pieces, gain, shift),
        row_blocks(width, step),
        like(step * len(pieces), width),
        "normalize_all",
        *pieces,
        gain,
        shift,
    )


def stack_kernel(*refs):
    *pieces, whole_ref, sums_ref = refs

    @pl.when(pl.program_id(0) == 0)
    def _():
        sums_ref[...] = jnp.zeros_like(sums_ref)

    def use(piece):
        whole_ref[...] = piece[...]
        sums_ref[...] += jnp.sum(piece[...].astype(FULL), axis=0, keepdims=True)

    from_piece(pieces, use)


def stack_pieces(pieces):
    step, width = pieces[0].shape
    return run_kernel(
        stack_kernel,
        len(pieces),
        whole(*pieces),
        [row_blocks(width, step), resident(1, width)],
        [like(step * len(pieces), width), like(1, width, dtype=FULL)],
        "stack_pieces",
        *pieces,
    )


def column_parts(width, count):
    return [slice(at * width // count, (at + 1) * width // count) for at in range(count)]


def hidden_kernel(normed_ref, *refs):
    *weight_refs, bias_ref, activated_ref, slope_ref = refs
    for weight_ref, here in zip(weight_refs, column_parts(bias_ref.shape[1], len(weight_refs))):
        pre_gelu = matmul(normed_ref[...], weight_ref[...], 1, 0) + bias_ref[:, here]
        value, slope = gelu_both(pre_gelu)
        activated_ref[:, here] = value.astype(LOW)
        slope_ref[:, here] = slope.astype(LOW)


def hidden_forward(normed, weights, bias):
    rows, columns, step = normed.shape[0], bias.shape[1], 256
    return run_kernel(
        hidden_kernel,
        rows // step,
        [row_blocks(normed.shape[1], step), *whole(*weights, bias)],
        [row_blocks(columns, step)] * 2,
        [like(rows, columns)] * 2,
        "hidden_forward",
        normed,
        *weights,
        bias,
    )


def hidden_back_kernel(grad_ref, *refs):
    *weight_refs, slope_ref, pre_grad_ref, sums_ref = refs

    @pl.when(pl.program_id(0) == 0)
    def _():
        sums_ref[...] = jnp.zeros_like(sums_ref)

    for weight_ref, here in zip(weight_refs, column_parts(slope_ref.shape[1], len(weight_refs))):
        pre_grad = matmul(grad_ref[...], weight_ref[...], 1, 0) * slope_ref[:, here].astype(FULL)
        pre_grad_ref[:, here] = pre_grad.astype(LOW)
        sums_ref[:, here] += jnp.sum(pre_grad, axis=0, keepdims=True)


def hidden_back(grad, weights, slope):
    rows, columns, step = grad.shape[0], slope.shape[1], 256
    return run_kernel(
        hidden_back_kernel,
        rows // step,
        [row_blocks(grad.shape[1], step), *whole(*weights), row_blocks(columns, step)],
        [row_blocks(columns, step), resident(1, columns)],
        [like(rows, columns), like(1, columns, dtype=FULL)],
        "hidden_back",
        grad,
        *weights,
        slope,
    )


def heads_kernel(normed_ref, grad_ref, left_ref, right_ref, bias_ref, projected_ref, back_ref):
    columns = left_ref.shape[1]
    split = projected_ref.shape[1] - columns
    projected_ref[:, :columns] = (
        matmul(normed_ref[...], left_ref[...], 1, 0) + bias_ref[:, :columns]
    )
    projected_ref[:, columns:] = (
        matmul(normed_ref[...], right_ref[:, :split], 1, 0) + bias_ref[:, columns:]
    )
    back_ref[...] = matmul(grad_ref[...], right_ref[:, split:], 1, 0).astype(LOW)


def heads_inputs(normed, grad, weights, bias):
    rows, split, step = normed.shape[0], bias.shape[1], 256
    columns = sum(weight.shape[1] for weight in weights) - split
    return run_kernel(
        heads_kernel,
        rows // step,
        [
            row_blocks(normed.shape[1], step),
            row_blocks(grad.shape[1], step),
            *whole(*weights, bias),
        ],
        [row_blocks(split, step), row_blocks(columns, step)],
        [like(rows, split, dtype=FULL), like(rows, columns)],
        "heads_inputs",
        normed,
        grad,
        *weights,
        bias,
    )


def products_of(lefts, rights):
    values = [matmul(left[...], right[...], 0, 0).astype(LOW) for left, right in zip(lefts, rights)]
    return values[0] if len(values) == 1 else jnp.concatenate(values, axis=1)


def weight_grad_kernel(count, x_ref, *refs):
    lefts, rights, outs = refs[:count], refs[count : 2 * count], refs[2 * count :]
    value = products_of(lefts, rights)
    columns = outs[0].shape[1]
    for first, targets in ((True, outs[:2]), (False, outs[2:])):

        @pl.when((pl.program_id(0) < 4) == first)
        def _(targets=targets):
            for which, target in enumerate(targets):
                target[...] = value[:, which * columns : (which + 1) * columns]


def weight_grad(x_at, *products):
    lefts, rights = zip(*products)
    tokens, width = lefts[0].shape
    columns, step = sum(right.shape[1] for right in rights) // 2, width // 8

    def rows_of(i, x_ref):
        return (0, (i % 4) * 2 + jnp.where(i < 4, 1 - x_ref[0], x_ref[0]))

    return run_kernel(
        functools.partial(weight_grad_kernel, len(products)),
        8,
        [pl.BlockSpec((tokens, step), rows_of)] * len(products) + whole(*rights),
        [pl.BlockSpec((step, columns), lambda i, *_: (jnp.minimum(i, 3), 0))] * 2
        + [pl.BlockSpec((step, columns), lambda i, *_: (jnp.maximum(i - 4, 0), 0))] * 2,
        [like(width // 2, columns)] * 4,
        "weight_grad",
        *lefts,
        *rights,
        scalars=[x_at],
    )


def weight_grad_plain_kernel(count, *refs):
    lefts, rights, outs = refs[:count], refs[count : 2 * count], refs[2 * count :]
    value = products_of(lefts, rights)
    for out_ref, here in zip(outs, column_parts(value.shape[1], 2)):
        out_ref[...] = value[:, here]


def weight_grad_plain(*products):
    lefts, rights = zip(*products)
    tokens, width = lefts[0].shape
    columns, step = sum(right.shape[1] for right in rights) // 2, 256
    return run_kernel(
        functools.partial(weight_grad_plain_kernel, len(products)),
        width // step,
        [pl.BlockSpec((tokens, step), lambda i, *_: (0, i))] * len(products) + whole(*rights),
        [row_blocks(columns, step)] * 2,
        [like(width, columns)] * 2,
        "weight_grad",
        *lefts,
        *rights,
    )


def fold_kernel(at_ref, kept_ref, got_ref, mine_ref, given_ref):
    rows = mine_ref.shape[0]
    for target, at in ((mine_ref, at_ref[0]), (given_ref, 1 - at_ref[0])):
        here = pl.ds(pl.multiple_of(at * rows, rows), rows)
        target[...] = (kept_ref[here, :].astype(FULL) + got_ref[here, :].astype(FULL)).astype(LOW)


def fold(at, kept, got):
    out = like(kept.shape[0] // 2, kept.shape[1])
    return run_kernel(
        fold_kernel, 1, whole(kept, got), whole(out, out), [out, out], "fold", kept, got, scalars=[at]
    )


def final_kernel(low_ref, *refs):
    *pairs, out_ref = refs
    columns = pairs[0].shape[1]
    for which in (0, 1):
        for source, at in ((pairs[2 * which], low_ref[0]), (pairs[2 * which + 1], 1 - low_ref[0])):
            begin = pl.multiple_of((2 * at + which) * columns, columns)
            out_ref[:, pl.ds(begin, columns)] = source[...].astype(FULL)


def final_grad(low_at, *pairs):
    out = like(pairs[0].shape[0], 4 * pairs[0].shape[1], dtype=FULL)
    return run_kernel(
        final_kernel, 1, whole(*pairs), resident(*out.shape), out, "final_grad", *pairs, scalars=[low_at]
    )


def final_heads_kernel(low_ref, *refs):
    pairs, (q_ref, k_ref, v_ref, dense_ref) = refs[:4], refs[4:]
    pair = 2 * HEAD
    half = dense_ref.shape[1] // 2
    for own, at in ((0, low_ref[0]), (1, 1 - low_ref[0])):
        source = jnp.concatenate([pairs[own][...], pairs[2 + own][...]], axis=1).astype(FULL)
        for which in range(half // pair):
            columns = pl.ds(pl.multiple_of(at * half + which * pair, pair), pair)
            for part, target in enumerate((q_ref, k_ref, v_ref)):
                begin = (3 * which + part) * pair
                target[:, columns] = source[:, begin : begin + pair]
        dense_ref[:, pl.ds(pl.multiple_of(at * half, half), half)] = source[:, 3 * half :]


def final_heads(low_at, *pairs):
    out = like(pairs[0].shape[0], pairs[0].shape[1], dtype=FULL)
    return run_kernel(
        final_heads_kernel,
        1,
        whole(*pairs),
        whole(*[out] * 4),
        [out] * 4,
        "final_heads",
        *pairs,
        scalars=[low_at],
    )


def sum_of_products(left_refs, right_refs, terms):
    total = None
    for left_at, left_columns, right_at, right_columns in terms:
        product = matmul(left_refs[left_at][:, left_columns], right_refs[right_at][:, right_columns], 1, 1)
        total = product if total is None else total + product
    return total


def branch_kernel(counts, terms, *refs):
    lefts, rights = refs[: counts[0]], refs[counts[0] : sum(counts)]
    refs[-1][...] = sum_of_products(lefts, rights, terms).astype(LOW)


def token_grad_kernel(counts, terms, *refs):
    lefts, rights = refs[: counts[0]], refs[counts[0] : sum(counts)]
    pieces, (out_ref, sums_ref) = refs[sum(counts) : -2], refs[-2:]

    @pl.when(pl.program_id(0) == 0)
    def _():
        sums_ref[...] = jnp.zeros_like(sums_ref)

    grad = sum_of_products(lefts, rights, terms)
    out_ref[...] = grad.astype(LOW)
    sums_ref[1:2, :] += jnp.sum(grad, axis=0, keepdims=True)

    def use(piece):
        x_hat, _ = normalize_rows(piece[...])
        sums_ref[0:1, :] += jnp.sum(grad * x_hat, axis=0, keepdims=True)

    from_piece(pieces, use)


def half_rows(kernel, name, far, lefts, rights, terms, pieces=()):
    rows, width = lefts[0].shape[0], rights[0].shape[0]
    step = rows // 8
    pieces = pieces[4 * far : 4 * far + 4]
    sums = [like(2, width, dtype=FULL)] if pieces else []
    return run_kernel(
        functools.partial(kernel, (len(lefts), len(rights)), terms),
        4,
        [pl.BlockSpec((step, left.shape[1]), lambda i, *_: (i + 4 * far, 0)) for left in lefts]
        + whole(*rights, *pieces),
        [row_blocks(width, step), *whole(*sums)],
        [like(4 * step, width)] + sums,
        name,
        *lefts,
        *rights,
        *pieces,
    )


def to_links(held, left_ref, left_given_ref, right_ref, right_given_ref):
    columns = left_ref.shape[1]

    for at in range(4):

        @pl.when(pl.program_id(0) == at)
        def _(y=at // 2, low=at % 2):
            left = left_given_ref if y else left_ref
            left[...] = held[:, :columns]
            right = right_given_ref if low else right_ref
            right[...] = held[:, columns:]


def links(step, width):
    columns = width * 5 // 8
    specs = [
        pl.BlockSpec((step, columns), lambda i, *_: (jnp.minimum(i, 1), 0)),
        pl.BlockSpec((step, columns), lambda i, *_: (jnp.maximum(i - 2, 0), 0)),
        pl.BlockSpec((step, width - columns), lambda i, *_: (i // 2, 0)),
        pl.BlockSpec((step, width - columns), lambda i, *_: (i // 2, 0)),
    ]
    return specs, [like(2 * step, columns)] * 2 + [like(2 * step, width - columns)] * 2


def link_kernel(kept_ref, got_ref, *outs):
    to_links((kept_ref[...].astype(FULL) + got_ref[...].astype(FULL)).astype(LOW), *outs)


def link_stage(kept, got):
    rows, width = kept.shape
    specs, outs = links(rows // 4, width)
    return run_kernel(
        link_kernel,
        4,
        [row_blocks(width, rows // 4)] * 2,
        specs,
        outs,
        "link_stage",
        kept,
        got,
    )


def last_kernel(left_ref, left_got_ref, right_ref, right_got_ref, *outs):
    rows = outs[0].shape[0]
    pairs = ((left_ref, left_got_ref), (right_ref, right_got_ref))
    for at, (kept_ref, got_ref) in enumerate(pairs):
        total = (kept_ref[...].astype(FULL) + got_ref[...].astype(FULL)).astype(LOW)
        outs[2 * at][...] = total[:rows]
        outs[2 * at + 1][...] = total[rows:]


def last_stage(*values):
    outs = [like(value.shape[0] // 2, value.shape[1]) for value in values]
    return run_kernel(last_kernel, 1, whole(*values), whole(*outs), outs, "last_stage", *values)


def joined(refs):
    left, left_got, right, right_got = (ref[...].astype(FULL) for ref in refs)
    return jnp.concatenate([left + left_got, right + right_got], axis=1)


def output_kernel(*refs):
    tokens_ref, dense_bias_ref, fc2_bias_ref, output_ref = refs[4:]
    total = tokens_ref[...].astype(FULL) + joined(refs[:4])
    output_ref[...] = (total + dense_bias_ref[...] + fc2_bias_ref[...]).astype(LOW)


def input_grad_kernel(*refs):
    tokens_ref, out_grad_ref, gain_ref, grad_ref = refs[4:]
    x_hat, inv_std = normalize_rows(tokens_ref[...])
    scaled = joined(refs[:4]) * gain_ref[...]
    token_grad = inv_std * (
        scaled
        - jnp.mean(scaled, axis=-1, keepdims=True)
        - x_hat * jnp.mean(scaled * x_hat, axis=-1, keepdims=True)
    )
    grad_ref[...] = (out_grad_ref[...].astype(FULL) + token_grad).astype(LOW)


def row_result(kernel, name, *operands):
    out = like(*operands[4].shape)
    return run_kernel(kernel, 1, whole(*operands), resident(*out.shape), out, name, *operands)


def body(
    tokens,
    out_grad,
    segments,
    ln_gain,
    ln_bias,
    qkv_weight,
    qkv_bias,
    dense_weight,
    dense_bias,
    fc1_weight,
    fc1_bias,
    fc2_weight,
    fc2_bias,
):
    low_at, high_at, x_at = lax.axis_index("zl"), lax.axis_index("zh"), lax.axis_index("x")
    t_at = lax.axis_index("t")
    pairwise = lax.axis_size("zh") == 2
    place = jnp.stack([t_at // 2, t_at % 2]).astype(jnp.int32)
    weight_rows = qkv_weight.shape[0]
    pair = 2 * HEAD
    half = dense_weight.shape[1] // 2
    pairs = half // pair
    hidden = fc1_weight.shape[1] // 2

    before = [()]

    def sync(*values):
        before[0] = lax.optimization_barrier((values, before[0]))[0]
        return before[0]

    def to_low(value):
        return swap(value, "zl", 1)

    def to_high(value):
        return swap(value, "zh", 1)

    def to_x(value):
        return swap(value, "x", 1)

    def to_y(value):
        return swap(value, "t", 2)

    def to_core(value):
        return swap(value, "t", 1)

    class Gather:
        def __init__(self, shard):
            self.own = shard
            self.moving = []

        def start(self):
            if pairwise:
                self.moving = [to_high(self.own), to_x(self.own)]
            else:
                rows, columns = self.own.shape
                gathered = lax.all_gather(self.own, ("zh", "x"), axis=0, tiled=True)
                natural = gathered.reshape(-1, 2, 2, rows // 2, columns).transpose(0, 2, 1, 3, 4)
                self.moving = [natural.reshape(-1, columns)]

        def forward(self):
            if pairwise:
                self.high, self.x = self.moving
                self.moving = [to_x(self.high)]

        def whole(self):
            if pairwise:
                return place_pieces(high_at, x_at, self.own, self.x, self.high, self.moving[0])
            return self.moving[0]

    class Sum:
        def __init__(self, given, kept):
            self.given, self.kept = given, kept
            self.moving = []

        def start(self):
            if pairwise:
                self.moving = [to_x(self.given)]
            else:
                rows, columns = self.given.shape
                blocks = self.given.reshape(-1, 2, 2, weight_rows, columns)
                ordered = blocks.transpose(0, 2, 1, 3, 4).reshape(rows, columns)
                self.moving = [
                    lax.psum_scatter(
                        ordered.astype(FULL), ("zh", "x"), scatter_dimension=0, tiled=True
                    )
                ]

        def second(self):
            if pairwise:
                self.kept, given = fold(high_at, self.kept, self.moving[0])
                self.moving = [to_high(given)]

        def third(self):
            other = self.kept if pairwise else jnp.zeros_like(self.moving[0])
            self.kept, given = fold(low_at, other, self.moving[0])
            self.moving = [to_low(given)]

        def halves(self):
            return [self.kept, self.moving[0]]

    def segment(values, *transfers):
        tied = sync(*values, *[piece for transfer in transfers for piece in transfer.moving])
        at = len(values)
        for transfer in transfers:
            many = len(transfer.moving)
            transfer.moving = list(tied[at : at + many])
            at += many
        return tied[: len(values)]

    def gathers_of(mine, got):
        return [Gather(shard) for shard in sync(*shards_of(low_at, mine, got))]

    def sums_of(*products):
        if pairwise:
            given_a, given_b, kept_a, kept_b = weight_grad(x_at, *products)
        else:
            given_a, given_b = weight_grad_plain(*products)
            kept_a = kept_b = given_a
        return [given_a, given_b, kept_a, kept_b]

    def as_sums(tied):
        return [Sum(tied[0], tied[2]), Sum(tied[1], tied[3])]

    (fc1_mine,), (fc1_given,) = halves_of(low_at, fc1_weight)
    fc1_given, tokens, out_grad, segments, qkv_weight, dense_weight, fc2_weight = sync(
        fc1_given, tokens, out_grad, segments, qkv_weight, dense_weight, fc2_weight
    )
    got = to_low(fc1_given)
    tokens_core, grad_core = to_core(tokens), to_core(out_grad)
    heads_mine, heads_given = heads_halves(low_at, qkv_weight, dense_weight)
    (fc2_mine,), (fc2_given,) = halves_of(low_at, fc2_weight)
    got, tokens_core, grad_core, heads_given, fc2_given, tokens, out_grad, segments = sync(
        got, tokens_core, grad_core, heads_given, fc2_given, tokens, out_grad, segments
    )
    fc1_a, fc1_b = gathers_of(fc1_mine, got)
    tokens, out_grad, segments, heads_given, fc2_given = sync(
        tokens, out_grad, segments, heads_given, fc2_given
    )
    fc1_a.start()
    tokens_low, tokens_y, segments_low = to_low(tokens), to_y(tokens), to_low(segments)
    tokens_low, tokens_y, segments_low, heads_given, fc1_b.own, fc2_given, out_grad = segment(
        [tokens_low, tokens_y, segments_low, heads_given, fc1_b.own, fc2_given, out_grad], fc1_a
    )
    fc1_a.forward()
    fc1_b.start()
    tokens_both, got = to_y(tokens_low), to_low(heads_given)
    all_segments = jnp.concatenate([segments, segments_low])
    starts = jnp.sum(
        (all_segments[:, None, :] < all_segments[:, :, None]).astype(jnp.int32), axis=2
    )
    tokens_both, got, starts, fc2_given, out_grad, tokens_low, tokens_y = segment(
        [tokens_both, got, starts, fc2_given, out_grad, tokens_low, tokens_y], fc1_a, fc1_b
    )
    tokens_low_core, tokens_y_core = to_core(tokens_low), to_core(tokens_y)
    tokens_both_core = to_core(tokens_both)
    shards = shards_of(low_at, heads_mine, got)
    tokens_low_core, tokens_y_core, tokens_both_core, fc2_given, out_grad, *shards = sync(
        tokens_low_core, tokens_y_core, tokens_both_core, fc2_given, out_grad, *shards
    )
    heads_a, heads_b = (Gather(shard) for shard in shards)
    fc1_b.forward()
    heads_a.start()
    grad_low, grad_y = to_low(out_grad), to_y(out_grad)
    token_pieces = [
        tokens,
        tokens_low,
        tokens_y,
        tokens_both,
        tokens_core,
        tokens_low_core,
        tokens_y_core,
        tokens_both_core,
    ]
    all_normed = normalize_all(token_pieces, ln_gain[None], ln_bias[None])
    fc1_full = [fc1_a.whole()]
    all_normed, fc1_full[0], grad_low, grad_y, heads_b.own, fc2_given = segment(
        [all_normed, fc1_full[0], grad_low, grad_y, heads_b.own, fc2_given], fc1_b, heads_a
    )
    heads_a.forward()
    heads_b.start()
    grad_both, got = to_y(grad_low), to_low(fc2_given)
    fc1_full.append(fc1_b.whole())
    bias = lax.dynamic_slice_in_dim(fc1_bias, low_at * hidden, hidden, 0)[None]
    activated, slope = hidden_forward(all_normed, fc1_full, bias)
    activated, slope, grad_both, got, grad_low, grad_y = segment(
        [activated, slope, grad_both, got, grad_low, grad_y], heads_a, heads_b
    )
    grad_low_core, grad_y_core = to_core(grad_low), to_core(grad_y)
    grad_both_core = to_core(grad_both)
    grad_low_core, grad_y_core, grad_both_core, *shards = sync(
        grad_low_core, grad_y_core, grad_both_core, *shards_of(low_at, fc2_mine, got)
    )
    fc2_a, fc2_b = (Gather(shard) for shard in shards)
    heads_b.forward()
    fc2_a.start()
    all_grad, grad_sums = stack_pieces(
        [
            out_grad,
            grad_low,
            grad_y,
            grad_both,
            grad_core,
            grad_low_core,
            grad_y_core,
            grad_both_core,
        ]
    )
    heads_full = [heads_a.whole()]
    all_grad, heads_full[0], *partials, fc2_b.own = segment(
        [all_grad, heads_full[0], *sums_of((all_grad, activated)), fc2_b.own], heads_b, fc2_a
    )
    d_fc2_a, d_fc2_b = as_sums(partials)
    fc2_a.forward()
    fc2_b.start()
    heads_full.append(heads_b.whole())
    bias = lax.dynamic_slice_in_dim(qkv_bias, low_at * half, half, 1)
    bias = bias.reshape(3, pairs, pair).transpose(1, 0, 2).reshape(1, 3 * half)
    projected, back = heads_inputs(all_normed, all_grad, heads_full, bias)
    projected, back, d_fc2_a.given, d_fc2_b.given = segment(
        [projected, back, d_fc2_a.given, d_fc2_b.given], fc2_a, fc2_b
    )
    fc2_b.forward()
    d_fc2_a.start()
    attended, qkv_grad, qkv_sums = attention(projected, back, starts, place)
    fc2_full = [fc2_a.whole()]
    attended, qkv_grad, qkv_sums, fc2_full[0], d_fc2_b.given = segment(
        [attended, qkv_grad, qkv_sums, fc2_full[0], d_fc2_b.given], fc2_b, d_fc2_a
    )
    d_fc2_b.start()
    d_fc2_a.second()
    fc2_full.append(fc2_b.whole())
    columns = heads_full[0].shape[1]
    first, second = slice(0, columns), slice(columns, 2 * columns)
    qkv_end = 3 * half - columns
    everything = slice(None)
    branch_products = (
        [attended, activated],
        [heads_full[1], *fc2_full],
        [
            (0, everything, 0, slice(qkv_end, columns)),
            (1, first, 1, everything),
            (1, second, 2, everything),
        ],
    )
    far, *partials = segment(
        [
            *half_rows(branch_kernel, "branch", 1, *branch_products),
            *sums_of((all_normed, qkv_grad), (all_grad, attended)),
        ],
        d_fc2_a,
        d_fc2_b,
    )
    d_heads_a, d_heads_b = as_sums(partials)
    d_heads_a.start()
    d_fc2_b.second()
    d_fc2_a.third()
    branch_got = to_core(far)
    (branch_kept,) = half_rows(branch_kernel, "branch", 0, *branch_products)
    pre_grad, pre_sums = hidden_back(all_grad, fc2_full, slope)
    branch_got, branch_kept, pre_grad, pre_sums, d_heads_b.given = segment(
        [branch_got, branch_kept, pre_grad, pre_sums, d_heads_b.given],
        d_heads_a,
        d_fc2_a,
        d_fc2_b,
    )
    d_heads_b.start()
    d_heads_a.second()
    left, left_given, right, right_given = link_stage(branch_kept, branch_got)
    branch_state = [left, to_y(left_given), right, to_low(right_given)]
    *branch_state, given_a, given_b, kept_a, kept_b = segment(
        [*branch_state, *sums_of((all_normed, pre_grad))], d_heads_a, d_heads_b, d_fc2_b
    )
    d_fc1_a, d_fc1_b = as_sums([given_a, given_b, kept_a, kept_b])
    d_fc1_a.start()
    d_heads_b.second()
    left, left_given, right, right_given = last_stage(*branch_state)
    branch_state = [left, to_low(left_given), right, to_y(right_given)]
    grad_products = (
        [qkv_grad, pre_grad],
        [*heads_full, *fc1_full],
        [
            (0, first, 0, everything),
            (0, slice(columns, 3 * half), 1, slice(0, qkv_end)),
            (1, first, 2, everything),
            (1, second, 3, everything),
        ],
        token_pieces,
    )
    far, far_sums, d_fc1_b.given, *branch_state = segment(
        [
            *half_rows(token_grad_kernel, "token_grad", 1, *grad_products),
            d_fc1_b.given,
            *branch_state,
        ],
        d_fc1_a,
        d_heads_a,
        d_heads_b,
        d_fc2_b,
    )
    d_fc1_b.start()
    d_fc1_a.second()
    d_heads_a.third()
    d_fc2_b.third()
    got = to_core(far)
    kept, near_sums = half_rows(token_grad_kernel, "token_grad", 0, *grad_products)
    output = row_result(
        output_kernel, "output", *branch_state, tokens, dense_bias[None], fc2_bias[None]
    )
    got, kept, near_sums, output = segment(
        [got, kept, near_sums, output], d_fc1_a, d_fc1_b, d_heads_a, d_heads_b, d_fc2_b
    )
    d_fc1_b.second()
    left, left_given, right, right_given = link_stage(kept, got)
    grad_state = [left, to_y(left_given), right, to_low(right_given)]
    sums = (near_sums + far_sums).reshape(2 * D)
    sums_got = to_core(sums)
    fc2_weight_grad = final_grad(low_at, *d_fc2_a.halves(), *d_fc2_b.halves())
    here = jnp.concatenate([jnp.sum(qkv_sums, axis=(0, 1)), pre_sums[0]])
    fc2_weight_grad, here, sums, sums_got, *grad_state = segment(
        [fc2_weight_grad, here, sums, sums_got, *grad_state], d_fc1_a, d_fc1_b, d_heads_b
    )
    left, left_given, right, right_given = last_stage(*grad_state)
    grad_state = [left, to_low(left_given), right, to_y(right_given)]
    d_fc1_a.third()
    d_fc1_b.third()
    d_heads_b.third()
    sums, *grad_state = segment(
        [sums + sums_got, *grad_state], d_fc1_a, d_fc1_b, d_heads_b
    )
    sums_got = [to_low(sums), to_y(sums), swap_both(sums, "zl", 1, "t", 2)]
    bias_got = to_low(here)
    input_grad = row_result(
        input_grad_kernel, "input_grad", *grad_state, tokens, out_grad, ln_gain[None]
    )
    fc1_weight_grad = final_grad(low_at, *d_fc1_a.halves(), *d_fc1_b.halves())
    input_grad, fc1_weight_grad, sums, bias_got, *sums_got = sync(
        input_grad, fc1_weight_grad, sums, bias_got, *sums_got
    )
    sums = jnp.concatenate([sum(sums_got, sums), grad_sums[0], here, bias_got])
    if pairwise:
        sums_got = [to_high(sums), to_x(sums), swap_both(sums, "zh", 1, "x", 1)]
    else:
        sums_got = [lax.psum(sums, ("zh", "x")) - sums]
    q, k, v, dense_weight_grad = final_heads(low_at, *d_heads_a.halves(), *d_heads_b.halves())
    qkv_weight_grad = jnp.stack([q, k, v], axis=1)
    qkv_weight_grad, dense_weight_grad, sums, *sums_got = sync(
        qkv_weight_grad, dense_weight_grad, sums, *sums_got
    )
    sums = sum(sums_got, sums)
    both = sums[3 * D :].reshape(2, here.shape[0])
    both = jnp.where(low_at == 0, both, both[::-1])
    qkv_bias_grad = (
        both[:, : 3 * half].reshape(2, pairs, 3, pair).transpose(2, 0, 1, 3).reshape(3, 2 * half)
    )
    return (
        output,
        input_grad,
        sums[:D],
        sums[D : 2 * D],
        qkv_weight_grad,
        qkv_bias_grad,
        dense_weight_grad,
        sums[2 * D : 3 * D],
        fc1_weight_grad,
        both[:, 3 * half :].reshape(2 * hidden),
        fc2_weight_grad,
        sums[2 * D : 3 * D],
    )


def solution(mesh):
    dp, tensor = mesh.shape["dp"], mesh.shape["tensor"]
    rows = ("zh", "zl", "x")
    everywhere = (*rows, "t")
    split = Mesh(np.asarray(mesh.devices).reshape(dp // 4, 2, 2, tensor), everywhere)
    return jax.shard_map(
        body,
        mesh=split,
        in_specs=(
            P(everywhere, None),
            P(everywhere, None),
            P(rows, None),
            P(),
            P(),
            P(rows, None, "t"),
            P(None, "t"),
            P(rows, "t"),
            P(),
            P(rows, "t"),
            P("t"),
            P(rows, "t"),
            P(),
        ),
        out_specs=(
            P(everywhere, None),
            P(everywhere, None),
            P(),
            P(),
            P(rows, None, "t"),
            P(None, "t"),
            P(rows, "t"),
            P(),
            P(rows, "t"),
            P("t"),
            P(rows, "t"),
            P(),
        ),
        check_vma=False,
    )
```

```python
import functools
import math

import jax
import jax.numpy as jnp
import numpy as np
from jax import lax
from jax.experimental import pallas as pl
from jax.experimental.pallas import tpu as pltpu
from jax.sharding import Mesh
from jax.sharding import PartitionSpec as P

D = 2048
H = 32
ROT = 32
LEN = 1024
LONGEST = LEN // 3
HEAD = D // H
QB = 128
BACK = -(-(LONGEST - 1) // QB)

EPSILON = 1e-05
GELU_SCALE = math.sqrt(2.0 / math.pi)
GELU_CUBIC = 0.044715
MASK_VALUE = -1e30
ROPE_BASE = 10000.0
LOW = jnp.bfloat16
FULL = jnp.float32


def gelu_both(pre_gelu):
    square = pre_gelu * pre_gelu
    tangent = jnp.tanh(GELU_SCALE * pre_gelu * (1.0 + GELU_CUBIC * square))
    value = 0.5 * pre_gelu * (1.0 + tangent)
    slope = 0.5 * (1.0 + tangent) + 0.5 * pre_gelu * (1.0 - tangent * tangent) * GELU_SCALE * (
        1.0 + 3.0 * GELU_CUBIC * square
    )
    return value, slope


def rotary_lanes():
    half = ROT // 2
    inverse = ROPE_BASE ** (-(2.0 * np.arange(half)) / ROT)
    angles = np.arange(LEN)[:, None] * inverse[None, :]
    rest = np.zeros((LEN, HEAD - ROT))
    cosine = np.concatenate([np.cos(angles), np.cos(angles), rest + 1.0], axis=1)
    sine = np.concatenate([-np.sin(angles), np.sin(angles), rest], axis=1)
    return tuple(jnp.asarray(np.tile(table, (1, 2)), FULL) for table in (cosine, sine))


def matmul(left, right, left_dim, right_dim):
    return lax.dot_general(
        left, right, (((left_dim,), (right_dim,)), ((), ())), preferred_element_type=FULL
    )


def attention_kernel(
    place_ref, proj_ref, grad_ref, start_ref, cos_ref, sin_ref, att_ref, dqkv_ref, sums_ref,
    q_st, g_st, k_low, v_low, k_turn, v_turn, dk_sum, dv_sum, dq_sum,
):
    pair = 2 * HEAD
    scale = 1.0 / math.sqrt(HEAD)
    part_rows = proj_ref.shape[3]
    parts = LEN // part_rows
    lane = lax.broadcasted_iota(jnp.int32, (part_rows, pair), 1)
    first = lane < HEAD
    near = lane % HEAD < ROT // 2
    y_at, core_at = place_ref[0], place_ref[1]

    def where_is(part):
        return (part % 2) ^ core_at, (part // 2) ^ y_at

    def partner(x):
        return jnp.where(near, pltpu.roll(x, pair - ROT // 2, 1), pltpu.roll(x, ROT // 2, 1))

    per_part = part_rows // QB
    for part in range(parts):
        core, y = where_is(part)
        rows = slice(part * part_rows, (part + 1) * part_rows)
        cosine, sine = cos_ref[rows, :], sin_ref[rows, :]
        projected = proj_ref[core, y, 0]
        q = projected[:, 0:pair]
        k = projected[:, pair : 2 * pair]
        v = projected[:, 2 * pair : 3 * pair]
        q = (q * cosine + partner(q) * sine) * scale
        k = k * cosine + partner(k) * sine
        g = grad_ref[core, y, 0].astype(FULL)
        zero = jnp.zeros_like(q)
        for stacked, whole in ((q_st, q), (g_st, g)):
            for head, own in enumerate(
                (jnp.where(first, whole, zero), jnp.where(first, zero, whole))
            ):
                stacked[
                    part * per_part : (part + 1) * per_part, head * QB : (head + 1) * QB, :
                ] = own.astype(LOW).reshape(per_part, QB, pair)
        k_low[rows, :] = k.astype(LOW)
        v_low[rows, :] = v.astype(LOW)
        k_turn[:, rows] = k.T.astype(LOW)
        v_turn[:, rows] = v.T.astype(LOW)
    dk_sum[...] = jnp.zeros_like(dk_sum)
    dv_sum[...] = jnp.zeros_like(dv_sum)
    upper = lax.broadcasted_iota(jnp.int32, (pair, QB), 0) < HEAD
    for block in range(LEN // QB):
        begin = max(0, block - BACK) * QB
        keys = slice(begin, (block + 1) * QB)
        rows = slice(block * QB, (block + 1) * QB)
        width = (block + 1) * QB - begin
        key_at = begin + lax.broadcasted_iota(jnp.int32, (width, QB), 0)
        query_at = block * QB + lax.broadcasted_iota(jnp.int32, (width, QB), 1)
        allowed = (key_at >= start_ref[0, block : block + 1, :]) & (key_at <= query_at)
        allowed = jnp.concatenate([allowed, allowed], axis=1)
        queries, grads = q_st[block], g_st[block]
        scores = jnp.where(allowed, matmul(k_low[keys], queries, 1, 1), MASK_VALUE)
        powers = jnp.exp(scores - jnp.max(scores, axis=0, keepdims=True))
        probs = powers * (1.0 / jnp.sum(powers, axis=0, keepdims=True))
        probs_low = probs.astype(LOW)
        prob_grad = matmul(v_low[keys], grads, 1, 1)
        row_dot = jnp.sum(probs * prob_grad, axis=0, keepdims=True)
        score_grad = (probs * (prob_grad - row_dot)).astype(LOW)
        dv_sum[keys] += matmul(probs_low, grads, 1, 0)
        dk_sum[keys] += matmul(score_grad, queries, 1, 0)
        turned = matmul(v_turn[:, keys], probs_low, 1, 0)
        core, y = where_is(block // per_part)
        here = slice((block % per_part) * QB, (block % per_part + 1) * QB)
        att_ref[core, y, 0, here, :] = jnp.where(upper, turned[:, :QB], turned[:, QB:]).T.astype(LOW)
        turned = matmul(k_turn[:, keys], score_grad, 1, 0)
        dq_sum[rows, :] = jnp.where(upper, turned[:, :QB], turned[:, QB:]).T
    totals = [jnp.zeros((1, pair), FULL)] * 3
    for part in range(parts):
        core, y = where_is(part)
        rows = slice(part * part_rows, (part + 1) * part_rows)
        cosine, sine = cos_ref[rows, :], sin_ref[rows, :]
        dq, dk = dq_sum[rows, :] * scale, dk_sum[rows, :]
        grads = (
            dq * cosine - partner(dq) * sine,
            dk * cosine - partner(dk) * sine,
            dv_sum[rows, :],
        )
        for at, grad in enumerate(grads):
            dqkv_ref[core, y, 0, :, at * pair : (at + 1) * pair] = grad.astype(LOW)
            totals[at] = totals[at] + jnp.sum(grad, axis=0, keepdims=True)
    for at, total in enumerate(totals):
        sums_ref[0, :, at * pair : (at + 1) * pair] = total


def attention(projected, grads, starts, place):
    rows, width = projected.shape
    seqs, pair = rows // LEN, 2 * HEAD
    pairs = width // (3 * pair)
    part_rows = rows // 8
    cosine, sine = rotary_lanes()
    table = pl.BlockSpec((LEN, pair), lambda s, h, place: (0, 0))

    def block(columns):
        return pl.BlockSpec((2, 2, 1, part_rows, columns), lambda s, h, place: (0, 0, s, 0, h))

    def view(columns):
        return (2, 2, seqs, part_rows, columns)

    attended, grad, sums = pl.pallas_call(
        attention_kernel,
        grid_spec=pltpu.PrefetchScalarGridSpec(
            num_scalar_prefetch=1,
            grid=(seqs, pairs),
            in_specs=[
                block(3 * pair),
                block(pair),
                pl.BlockSpec((1, LEN // QB, QB), lambda s, h, place: (s, 0, 0)),
                table,
                table,
            ],
            out_specs=[
                block(pair),
                block(3 * pair),
                pl.BlockSpec((1, 1, 3 * pair), lambda s, h, place: (s, 0, h)),
            ],
            scratch_shapes=[
                pltpu.VMEM((LEN // QB, 2 * QB, pair), LOW),
                pltpu.VMEM((LEN // QB, 2 * QB, pair), LOW),
                pltpu.VMEM((LEN, pair), LOW),
                pltpu.VMEM((LEN, pair), LOW),
                pltpu.VMEM((pair, LEN), LOW),
                pltpu.VMEM((pair, LEN), LOW),
                pltpu.VMEM((LEN, pair), FULL),
                pltpu.VMEM((LEN, pair), FULL),
                pltpu.VMEM((LEN, pair), FULL),
            ],
        ),
        out_shape=[
            jax.ShapeDtypeStruct(view(pairs * pair), LOW),
            jax.ShapeDtypeStruct(view(width), LOW),
            jax.ShapeDtypeStruct((seqs, 1, width), FULL),
        ],
        compiler_params=pltpu.CompilerParams(vmem_limit_bytes=58 << 20),
        cost_estimate=pl.CostEstimate(
            flops=seqs * LEN * QB * (BACK + 1) * pair // 8,
            transcendentals=0,
            bytes_accessed=rows * width // 8,
        ),
        name="attention_both_ways",
    )(
        place,
        projected.reshape(view(width)),
        grads.reshape(view(pairs * pair)),
        starts.reshape(seqs, LEN // QB, QB),
        cosine,
        sine,
    )
    return attended.reshape(rows, pairs * pair), grad.reshape(rows, width), sums


def swap(value, axis, bit):
    return lax.ppermute(value, axis, [(i, i ^ bit) for i in range(lax.axis_size(axis))])


def swap_both(value, axis, bit, other_axis, other_bit):
    inner = lax.axis_size(other_axis)
    pairs = [
        (i, ((i // inner) ^ bit) * inner + ((i % inner) ^ other_bit))
        for i in range(lax.axis_size(axis) * inner)
    ]
    return lax.ppermute(value, (axis, other_axis), pairs)


def normalize_rows(token_rows):
    values = token_rows.astype(FULL)
    centered = values - jnp.mean(values, axis=-1, keepdims=True)
    inv_std = lax.rsqrt(jnp.mean(centered * centered, axis=-1, keepdims=True) + EPSILON)
    return centered * inv_std, inv_std


def row_blocks(columns, rows):
    return pl.BlockSpec((rows, columns), lambda i, *_: (i, 0))


def resident(*shape):
    return pl.BlockSpec(shape, lambda i, *_: (0,) * len(shape), pipeline_mode=pl.Buffered(1))


def like(*shape, dtype=LOW):
    return jax.ShapeDtypeStruct(shape, dtype)


def run_kernel(
    kernel, steps, in_specs, out_specs, out_shape, name, *operands, scalars=(), room=None
):
    if scalars:
        scalars = (jnp.stack([jnp.asarray(scalar, jnp.int32) for scalar in scalars]),)
    return pl.pallas_call(
        kernel,
        grid_spec=pltpu.PrefetchScalarGridSpec(
            num_scalar_prefetch=len(scalars),
            grid=(steps,),
            in_specs=in_specs,
            out_specs=out_specs,
        ),
        out_shape=out_shape,
        compiler_params=pltpu.CompilerParams(vmem_limit_bytes=(room or (52 if steps > 1 else 32)) << 20),
        cost_estimate=pl.CostEstimate(flops=1 << 24, transcendentals=0, bytes_accessed=1 << 18),
        name=name,
    )(*scalars, *operands)


def whole(*values):
    return [resident(*value.shape) for value in values]


def halves_kernel(low_ref, *refs):
    count = len(refs) // 3
    for source, mine, given in zip(refs[:count], refs[count : 2 * count], refs[2 * count :]):
        columns = mine.shape[1]
        for target, at in ((mine, low_ref[0]), (given, 1 - low_ref[0])):
            target[...] = source[:, pl.ds(pl.multiple_of(at * columns, columns), columns)]


def halves_of(low_at, *weights):
    outs = [like(weight.shape[0], weight.shape[1] // 2) for weight in weights] * 2
    found = run_kernel(
        halves_kernel, 1, whole(*weights), whole(*outs), outs, "halves", *weights, scalars=[low_at]
    )
    return found[: len(weights)], found[len(weights) :]


def heads_halves_kernel(low_ref, q_ref, k_ref, v_ref, dense_ref, mine_ref, given_ref):
    pair = 2 * HEAD
    half = dense_ref.shape[1] // 2
    for target, at in ((mine_ref, low_ref[0]), (given_ref, 1 - low_ref[0])):
        for which in range(half // pair):
            columns = pl.ds(pl.multiple_of(at * half + which * pair, pair), pair)
            for part, source in enumerate((q_ref, k_ref, v_ref)):
                begin = (3 * which + part) * pair
                target[:, begin : begin + pair] = source[:, columns]
        target[:, 3 * half :] = dense_ref[:, pl.ds(pl.multiple_of(at * half, half), half)]


def heads_halves(low_at, qkv_weight, dense_weight):
    operands = (*(qkv_weight[:, part] for part in range(3)), dense_weight)
    out = like(dense_weight.shape[0], 2 * dense_weight.shape[1])
    return run_kernel(
        heads_halves_kernel,
        1,
        whole(*operands),
        whole(out, out),
        [out, out],
        "heads_halves",
        *operands,
        scalars=[low_at],
    )


def shard_kernel(low_ref, mine_ref, got_ref, *shard_refs):
    rows, columns = mine_ref.shape[0], shard_refs[0].shape[1]
    for source, at in ((mine_ref, low_ref[0]), (got_ref, 1 - low_ref[0])):
        for which, shard_ref in enumerate(shard_refs):
            here = slice(which * columns, (which + 1) * columns)
            shard_ref[pl.ds(pl.multiple_of(at * rows, rows), rows), :] = source[:, here]


def shards_of(low_at, mine, got):
    out = like(2 * mine.shape[0], mine.shape[1] // 2)
    return run_kernel(
        shard_kernel,
        1,
        whole(mine, got),
        whole(out, out),
        [out, out],
        "shards",
        mine,
        got,
        scalars=[low_at],
    )


def place_kernel(at_ref, *refs):
    *pieces, full = refs
    rows = pieces[0].shape[0] // 2
    for at, piece in enumerate(pieces):
        slot = 4 * (at_ref[0] ^ (at // 2)) + (at_ref[1] ^ (at % 2))
        for low in (0, 1):
            begin = pl.multiple_of((slot + 2 * low) * rows, rows)
            full[pl.ds(begin, rows), :] = piece[low * rows : (low + 1) * rows, :]


def place_pieces(high_at, x_at, *pieces):
    rows, columns = pieces[0].shape
    steps = 2
    block = pl.BlockSpec((rows, columns // steps), lambda i, *_: (0, i))
    return run_kernel(
        place_kernel,
        steps,
        [block] * 4,
        pl.BlockSpec((4 * rows, columns // steps), lambda i, *_: (0, i)),
        like(4 * rows, columns),
        "place_pieces",
        *pieces,
        scalars=[high_at, x_at],
    )


def from_piece(pieces, use):
    for at, piece in enumerate(pieces):

        @pl.when(pl.program_id(0) == at)
        def _(piece=piece):
            use(piece)


def normalize_kernel(*refs):
    *pieces, gain_ref, shift_ref, normed_ref, mean_ref, inv_std_ref = refs

    def use(piece):
        values = piece[...].astype(FULL)
        mean = jnp.mean(values, axis=-1, keepdims=True)
        centered = values - mean
        inv_std = lax.rsqrt(jnp.mean(centered * centered, axis=-1, keepdims=True) + EPSILON)
        normed_ref[...] = (centered * inv_std * gain_ref[...] + shift_ref[...]).astype(LOW)
        mean_ref[...] = mean
        inv_std_ref[...] = inv_std

    from_piece(pieces, use)


def normalize_all(pieces, gain, shift):
    step, width = pieces[0].shape
    return run_kernel(
        normalize_kernel,
        len(pieces),
        whole(*pieces, gain, shift),
        [row_blocks(width, step), row_blocks(1, step), row_blocks(1, step)],
        [like(step * len(pieces), width)] + [like(step * len(pieces), 1, dtype=FULL)] * 2,
        "normalize_all",
        *pieces,
        gain,
        shift,
    )


def stack_kernel(*refs):
    *pieces, whole_ref, sums_ref = refs

    @pl.when(pl.program_id(0) == 0)
    def _():
        sums_ref[...] = jnp.zeros_like(sums_ref)

    def use(piece):
        whole_ref[...] = piece[...]
        sums_ref[...] += jnp.sum(piece[...].astype(FULL), axis=0, keepdims=True)

    from_piece(pieces, use)


def stack_pieces(pieces):
    step, width = pieces[0].shape
    return run_kernel(
        stack_kernel,
        len(pieces),
        whole(*pieces),
        [row_blocks(width, step), resident(1, width)],
        [like(step * len(pieces), width), like(1, width, dtype=FULL)],
        "stack_pieces",
        *pieces,
    )


def column_parts(width, count):
    return [slice(at * width // count, (at + 1) * width // count) for at in range(count)]


def hidden_kernel(normed_ref, *refs):
    *weight_refs, bias_ref, activated_ref, slope_ref = refs
    for weight_ref, here in zip(weight_refs, column_parts(bias_ref.shape[1], len(weight_refs))):
        pre_gelu = matmul(normed_ref[...], weight_ref[...], 1, 0) + bias_ref[:, here]
        value, slope = gelu_both(pre_gelu)
        activated_ref[:, here] = value.astype(LOW)
        slope_ref[:, here] = slope.astype(LOW)


def hidden_forward(normed, weights, bias):
    rows, columns, step = normed.shape[0], bias.shape[1], 256
    return run_kernel(
        hidden_kernel,
        rows // step,
        [row_blocks(normed.shape[1], step), *whole(*weights, bias)],
        [row_blocks(columns, step)] * 2,
        [like(rows, columns)] * 2,
        "hidden_forward",
        normed,
        *weights,
        bias,
    )


def hidden_back_kernel(grad_ref, *refs):
    *weight_refs, slope_ref, pre_grad_ref, sums_ref = refs

    @pl.when(pl.program_id(0) == 0)
    def _():
        sums_ref[...] = jnp.zeros_like(sums_ref)

    for weight_ref, here in zip(weight_refs, column_parts(slope_ref.shape[1], len(weight_refs))):
        pre_grad = matmul(grad_ref[...], weight_ref[...], 1, 0) * slope_ref[:, here].astype(FULL)
        pre_grad_ref[:, here] = pre_grad.astype(LOW)
        sums_ref[:, here] += jnp.sum(pre_grad, axis=0, keepdims=True)


def hidden_back(grad, weights, slope):
    rows, columns, step = grad.shape[0], slope.shape[1], 256
    return run_kernel(
        hidden_back_kernel,
        rows // step,
        [row_blocks(grad.shape[1], step), *whole(*weights), row_blocks(columns, step)],
        [row_blocks(columns, step), resident(1, columns)],
        [like(rows, columns), like(1, columns, dtype=FULL)],
        "hidden_back",
        grad,
        *weights,
        slope,
    )


def heads_kernel(normed_ref, grad_ref, left_ref, right_ref, bias_ref, projected_ref, back_ref):
    columns = left_ref.shape[1]
    split = projected_ref.shape[1] - columns
    projected_ref[:, :columns] = (
        matmul(normed_ref[...], left_ref[...], 1, 0) + bias_ref[:, :columns]
    )
    projected_ref[:, columns:] = (
        matmul(normed_ref[...], right_ref[:, :split], 1, 0) + bias_ref[:, columns:]
    )
    back_ref[...] = matmul(grad_ref[...], right_ref[:, split:], 1, 0).astype(LOW)


def heads_inputs(normed, grad, weights, bias):
    rows, split, step = normed.shape[0], bias.shape[1], 256
    columns = sum(weight.shape[1] for weight in weights) - split
    return run_kernel(
        heads_kernel,
        rows // step,
        [
            row_blocks(normed.shape[1], step),
            row_blocks(grad.shape[1], step),
            *whole(*weights, bias),
        ],
        [row_blocks(split, step), row_blocks(columns, step)],
        [like(rows, split, dtype=FULL), like(rows, columns)],
        "heads_inputs",
        normed,
        grad,
        *weights,
        bias,
    )


def products_of(lefts, rights):
    values = [matmul(left[...], right[...], 0, 0).astype(LOW) for left, right in zip(lefts, rights)]
    return values[0] if len(values) == 1 else jnp.concatenate(values, axis=1)


def weight_grad_kernel(count, x_ref, *refs):
    lefts, rights, outs = refs[:count], refs[count : 2 * count], refs[2 * count :]
    value = products_of(lefts, rights)
    columns = outs[0].shape[1]
    for first, targets in ((True, outs[:2]), (False, outs[2:])):

        @pl.when((pl.program_id(0) < 4) == first)
        def _(targets=targets):
            for which, target in enumerate(targets):
                target[...] = value[:, which * columns : (which + 1) * columns]


def weight_grad(x_at, *products):
    lefts, rights = zip(*products)
    tokens, width = lefts[0].shape
    columns, step = sum(right.shape[1] for right in rights) // 2, width // 8

    def rows_of(i, x_ref):
        return (0, (i % 4) * 2 + jnp.where(i < 4, 1 - x_ref[0], x_ref[0]))

    return run_kernel(
        functools.partial(weight_grad_kernel, len(products)),
        8,
        [pl.BlockSpec((tokens, step), rows_of)] * len(products) + whole(*rights),
        [pl.BlockSpec((step, columns), lambda i, *_: (jnp.minimum(i, 3), 0))] * 2
        + [pl.BlockSpec((step, columns), lambda i, *_: (jnp.maximum(i - 4, 0), 0))] * 2,
        [like(width // 2, columns)] * 4,
        "weight_grad",
        *lefts,
        *rights,
        scalars=[x_at],
    )


def weight_grad_plain_kernel(count, *refs):
    lefts, rights, outs = refs[:count], refs[count : 2 * count], refs[2 * count :]
    value = products_of(lefts, rights)
    for out_ref, here in zip(outs, column_parts(value.shape[1], 2)):
        out_ref[...] = value[:, here]


def weight_grad_plain(*products):
    lefts, rights = zip(*products)
    tokens, width = lefts[0].shape
    columns, step = sum(right.shape[1] for right in rights) // 2, 256
    return run_kernel(
        functools.partial(weight_grad_plain_kernel, len(products)),
        width // step,
        [pl.BlockSpec((tokens, step), lambda i, *_: (0, i))] * len(products) + whole(*rights),
        [row_blocks(columns, step)] * 2,
        [like(width, columns)] * 2,
        "weight_grad",
        *lefts,
        *rights,
    )


def fold_kernel(at_ref, kept_ref, got_ref, mine_ref, given_ref):
    rows = mine_ref.shape[0]
    for target, at in ((mine_ref, at_ref[0]), (given_ref, 1 - at_ref[0])):
        here = pl.ds(pl.multiple_of(at * rows, rows), rows)
        target[...] = (kept_ref[here, :].astype(FULL) + got_ref[here, :].astype(FULL)).astype(LOW)


def fold(at, kept, got):
    out = like(kept.shape[0] // 2, kept.shape[1])
    return run_kernel(
        fold_kernel, 1, whole(kept, got), whole(out, out), [out, out], "fold", kept, got, scalars=[at]
    )


def final_kernel(low_ref, *refs):
    *pairs, out_ref = refs
    columns = pairs[0].shape[1]
    for which in (0, 1):
        for source, at in ((pairs[2 * which], low_ref[0]), (pairs[2 * which + 1], 1 - low_ref[0])):
            begin = pl.multiple_of((2 * at + which) * columns, columns)
            out_ref[:, pl.ds(begin, columns)] = source[...].astype(FULL)


def final_grad(low_at, *pairs):
    out = like(pairs[0].shape[0], 4 * pairs[0].shape[1], dtype=FULL)
    return run_kernel(
        final_kernel,
        1,
        whole(*pairs),
        resident(*out.shape),
        out,
        "final_grad",
        *pairs,
        scalars=[low_at],
        room=58,
    )


def final_heads_kernel(low_ref, *refs):
    pairs, (q_ref, k_ref, v_ref, dense_ref) = refs[:4], refs[4:]
    pair = 2 * HEAD
    half = dense_ref.shape[1] // 2
    for own, at in ((0, low_ref[0]), (1, 1 - low_ref[0])):
        source = jnp.concatenate([pairs[own][...], pairs[2 + own][...]], axis=1).astype(FULL)
        for which in range(half // pair):
            columns = pl.ds(pl.multiple_of(at * half + which * pair, pair), pair)
            for part, target in enumerate((q_ref, k_ref, v_ref)):
                begin = (3 * which + part) * pair
                target[:, columns] = source[:, begin : begin + pair]
        dense_ref[:, pl.ds(pl.multiple_of(at * half, half), half)] = source[:, 3 * half :]


def final_heads(low_at, *pairs):
    out = like(pairs[0].shape[0], pairs[0].shape[1], dtype=FULL)
    return run_kernel(
        final_heads_kernel,
        1,
        whole(*pairs),
        whole(*[out] * 4),
        [out] * 4,
        "final_heads",
        *pairs,
        scalars=[low_at],
        room=58,
    )


def sum_of_products(left_refs, right_refs, terms):
    total = None
    for left_at, left_columns, right_at, right_columns in terms:
        product = matmul(left_refs[left_at][:, left_columns], right_refs[right_at][:, right_columns], 1, 1)
        total = product if total is None else total + product
    return total


def branch_kernel(counts, terms, *refs):
    lefts, rights = refs[: counts[0]], refs[counts[0] : sum(counts)]
    refs[-1][...] = sum_of_products(lefts, rights, terms).astype(LOW)


def token_grad_kernel(counts, terms, *refs):
    lefts, rights = refs[: counts[0]], refs[counts[0] : sum(counts)]
    pieces, (mean_ref, inv_std_ref, out_ref, sums_ref) = refs[sum(counts) : -4], refs[-4:]

    @pl.when(pl.program_id(0) == 0)
    def _():
        sums_ref[...] = jnp.zeros_like(sums_ref)

    grad = sum_of_products(lefts, rights, terms)
    out_ref[...] = grad.astype(LOW)
    sums_ref[1:2, :] += jnp.sum(grad, axis=0, keepdims=True)

    def use(piece):
        x_hat = (piece[...].astype(FULL) - mean_ref[...]) * inv_std_ref[...]
        sums_ref[0:1, :] += jnp.sum(grad * x_hat, axis=0, keepdims=True)

    from_piece(pieces, use)


def half_rows(kernel, name, far, lefts, rights, terms, pieces=(), row_stats=()):
    rows, width = lefts[0].shape[0], rights[0].shape[0]
    step = rows // 8
    pieces = pieces[4 * far : 4 * far + 4]
    sums = [like(2, width, dtype=FULL)] if pieces else []
    return run_kernel(
        functools.partial(kernel, (len(lefts), len(rights)), terms),
        4,
        [pl.BlockSpec((step, left.shape[1]), lambda i, *_: (i + 4 * far, 0)) for left in lefts]
        + whole(*rights, *pieces)
        + [pl.BlockSpec((step, 1), lambda i, *_: (i + 4 * far, 0)) for _ in row_stats],
        [row_blocks(width, step), *whole(*sums)],
        [like(4 * step, width)] + sums,
        name,
        *lefts,
        *rights,
        *pieces,
        *row_stats,
    )


def to_links(held, left_ref, left_given_ref, right_ref, right_given_ref):
    columns = left_ref.shape[1]

    for at in range(4):

        @pl.when(pl.program_id(0) == at)
        def _(y=at // 2, low=at % 2):
            left = left_given_ref if y else left_ref
            left[...] = held[:, :columns]
            right = right_given_ref if low else right_ref
            right[...] = held[:, columns:]


def links(step, width):
    columns = width * 11 // 16
    specs = [
        pl.BlockSpec((step, columns), lambda i, *_: (jnp.minimum(i, 1), 0)),
        pl.BlockSpec((step, columns), lambda i, *_: (jnp.maximum(i - 2, 0), 0)),
        pl.BlockSpec((step, width - columns), lambda i, *_: (i // 2, 0)),
        pl.BlockSpec((step, width - columns), lambda i, *_: (i // 2, 0)),
    ]
    return specs, [like(2 * step, columns)] * 2 + [like(2 * step, width - columns)] * 2


def link_kernel(kept_ref, got_ref, *outs):
    to_links((kept_ref[...].astype(FULL) + got_ref[...].astype(FULL)).astype(LOW), *outs)


def link_stage(kept, got):
    rows, width = kept.shape
    specs, outs = links(rows // 4, width)
    return run_kernel(
        link_kernel,
        4,
        [row_blocks(width, rows // 4)] * 2,
        specs,
        outs,
        "link_stage",
        kept,
        got,
    )


def last_kernel(left_ref, left_got_ref, right_ref, right_got_ref, *outs):
    rows = outs[0].shape[0]
    pairs = ((left_ref, left_got_ref), (right_ref, right_got_ref))
    for at, (kept_ref, got_ref) in enumerate(pairs):
        total = (kept_ref[...].astype(FULL) + got_ref[...].astype(FULL)).astype(LOW)
        outs[2 * at][...] = total[:rows]
        outs[2 * at + 1][...] = total[rows:]


def last_stage(*values):
    outs = [like(value.shape[0] // 2, value.shape[1]) for value in values]
    return run_kernel(last_kernel, 1, whole(*values), whole(*outs), outs, "last_stage", *values)


def joined(refs):
    left, left_got, right, right_got = (ref[...].astype(FULL) for ref in refs)
    return jnp.concatenate([left + left_got, right + right_got], axis=1)


def output_kernel(*refs):
    tokens_ref, dense_bias_ref, fc2_bias_ref, output_ref = refs[4:]
    total = tokens_ref[...].astype(FULL) + joined(refs[:4])
    output_ref[...] = (total + dense_bias_ref[...] + fc2_bias_ref[...]).astype(LOW)


def input_grad_kernel(*refs):
    tokens_ref, out_grad_ref, gain_ref, grad_ref = refs[4:]
    x_hat, inv_std = normalize_rows(tokens_ref[...])
    scaled = joined(refs[:4]) * gain_ref[...]
    token_grad = inv_std * (
        scaled
        - jnp.mean(scaled, axis=-1, keepdims=True)
        - x_hat * jnp.mean(scaled * x_hat, axis=-1, keepdims=True)
    )
    grad_ref[...] = (out_grad_ref[...].astype(FULL) + token_grad).astype(LOW)


def row_result(kernel, name, *operands):
    out = like(*operands[4].shape)
    return run_kernel(
        kernel, 1, whole(*operands), resident(*out.shape), out, name, *operands, room=58
    )


def body(
    tokens,
    out_grad,
    segments,
    ln_gain,
    ln_bias,
    qkv_weight,
    qkv_bias,
    dense_weight,
    dense_bias,
    fc1_weight,
    fc1_bias,
    fc2_weight,
    fc2_bias,
):
    low_at, high_at, x_at = lax.axis_index("zl"), lax.axis_index("zh"), lax.axis_index("x")
    t_at = lax.axis_index("t")
    pairwise = lax.axis_size("zh") == 2
    place = jnp.stack([t_at // 2, t_at % 2]).astype(jnp.int32)
    weight_rows = qkv_weight.shape[0]
    pair = 2 * HEAD
    half = dense_weight.shape[1] // 2
    pairs = half // pair
    hidden = fc1_weight.shape[1] // 2

    before = [()]

    def sync(*values):
        before[0] = lax.optimization_barrier((values, before[0]))[0]
        return before[0]

    def to_low(value):
        return swap(value, "zl", 1)

    def to_high(value):
        return swap(value, "zh", 1)

    def to_x(value):
        return swap(value, "x", 1)

    def to_y(value):
        return swap(value, "t", 2)

    def to_core(value):
        return swap(value, "t", 1)

    class Gather:
        def __init__(self, shard):
            self.own = shard
            self.moving = []

        def start(self):
            if pairwise:
                self.moving = [to_high(self.own), to_x(self.own)]
            else:
                rows, columns = self.own.shape
                gathered = lax.all_gather(self.own, ("zh", "x"), axis=0, tiled=True)
                natural = gathered.reshape(-1, 2, 2, rows // 2, columns).transpose(0, 2, 1, 3, 4)
                self.moving = [natural.reshape(-1, columns)]

        def forward(self):
            if pairwise:
                self.high, self.x = self.moving
                self.moving = [to_x(self.high)]

        def whole(self):
            if pairwise:
                return place_pieces(high_at, x_at, self.own, self.x, self.high, self.moving[0])
            return self.moving[0]

    class Sum:
        def __init__(self, given, kept):
            self.given, self.kept = given, kept
            self.moving = []

        def start(self):
            if pairwise:
                self.moving = [to_x(self.given)]
            else:
                rows, columns = self.given.shape
                blocks = self.given.reshape(-1, 2, 2, weight_rows, columns)
                ordered = blocks.transpose(0, 2, 1, 3, 4).reshape(rows, columns)
                self.moving = [
                    lax.psum_scatter(
                        ordered.astype(FULL), ("zh", "x"), scatter_dimension=0, tiled=True
                    )
                ]

        def second(self):
            if pairwise:
                self.kept, given = fold(high_at, self.kept, self.moving[0])
                self.moving = [to_high(given)]

        def third(self):
            other = self.kept if pairwise else jnp.zeros_like(self.moving[0])
            self.kept, given = fold(low_at, other, self.moving[0])
            self.moving = [to_low(given)]

        def halves(self):
            return [self.kept, self.moving[0]]

    def segment(values, *transfers):
        tied = sync(*values, *[piece for transfer in transfers for piece in transfer.moving])
        at = len(values)
        for transfer in transfers:
            many = len(transfer.moving)
            transfer.moving = list(tied[at : at + many])
            at += many
        return tied[: len(values)]

    def gathers_of(mine, got):
        return [Gather(shard) for shard in sync(*shards_of(low_at, mine, got))]

    def sums_of(*products):
        if pairwise:
            given_a, given_b, kept_a, kept_b = weight_grad(x_at, *products)
        else:
            given_a, given_b = weight_grad_plain(*products)
            kept_a = kept_b = given_a
        return [given_a, given_b, kept_a, kept_b]

    def as_sums(tied):
        return [Sum(tied[0], tied[2]), Sum(tied[1], tied[3])]

    (fc1_mine,), (fc1_given,) = halves_of(low_at, fc1_weight)
    fc1_given, tokens, out_grad, segments, qkv_weight, dense_weight, fc2_weight = sync(
        fc1_given, tokens, out_grad, segments, qkv_weight, dense_weight, fc2_weight
    )
    got = to_low(fc1_given)
    tokens_core, grad_core = to_core(tokens), to_core(out_grad)
    heads_mine, heads_given = heads_halves(low_at, qkv_weight, dense_weight)
    (fc2_mine,), (fc2_given,) = halves_of(low_at, fc2_weight)
    got, tokens_core, grad_core, heads_given, fc2_given, tokens, out_grad, segments = sync(
        got, tokens_core, grad_core, heads_given, fc2_given, tokens, out_grad, segments
    )
    fc1_a, fc1_b = gathers_of(fc1_mine, got)
    tokens, out_grad, segments, heads_given, fc2_given = sync(
        tokens, out_grad, segments, heads_given, fc2_given
    )
    fc1_a.start()
    tokens_low, tokens_y, segments_low = to_low(tokens), to_y(tokens), to_low(segments)
    tokens_low, tokens_y, segments_low, heads_given, fc1_b.own, fc2_given, out_grad = segment(
        [tokens_low, tokens_y, segments_low, heads_given, fc1_b.own, fc2_given, out_grad], fc1_a
    )
    fc1_a.forward()
    fc1_b.start()
    tokens_both, got = to_y(tokens_low), to_low(heads_given)
    all_segments = jnp.concatenate([segments, segments_low])
    starts = jnp.sum(
        (all_segments[:, None, :] < all_segments[:, :, None]).astype(jnp.int32), axis=2
    )
    tokens_both, got, starts, fc2_given, out_grad, tokens_low, tokens_y = segment(
        [tokens_both, got, starts, fc2_given, out_grad, tokens_low, tokens_y], fc1_a, fc1_b
    )
    tokens_low_core, tokens_y_core = to_core(tokens_low), to_core(tokens_y)
    tokens_both_core = to_core(tokens_both)
    shards = shards_of(low_at, heads_mine, got)
    tokens_low_core, tokens_y_core, tokens_both_core, fc2_given, out_grad, *shards = sync(
        tokens_low_core, tokens_y_core, tokens_both_core, fc2_given, out_grad, *shards
    )
    heads_a, heads_b = (Gather(shard) for shard in shards)
    fc1_b.forward()
    heads_a.start()
    grad_low, grad_y = to_low(out_grad), to_y(out_grad)
    token_pieces = [
        tokens,
        tokens_low,
        tokens_y,
        tokens_both,
        tokens_core,
        tokens_low_core,
        tokens_y_core,
        tokens_both_core,
    ]
    all_normed, *row_stats = normalize_all(token_pieces, ln_gain[None], ln_bias[None])
    fc1_full = [fc1_a.whole()]
    all_normed, fc1_full[0], grad_low, grad_y, heads_b.own, fc2_given = segment(
        [all_normed, fc1_full[0], grad_low, grad_y, heads_b.own, fc2_given], fc1_b, heads_a
    )
    heads_a.forward()
    heads_b.start()
    grad_both, got = to_y(grad_low), to_low(fc2_given)
    fc1_full.append(fc1_b.whole())
    bias = lax.dynamic_slice_in_dim(fc1_bias, low_at * hidden, hidden, 0)[None]
    activated, slope = hidden_forward(all_normed, fc1_full, bias)
    activated, slope, grad_both, got, grad_low, grad_y = segment(
        [activated, slope, grad_both, got, grad_low, grad_y], heads_a, heads_b
    )
    grad_low_core, grad_y_core = to_core(grad_low), to_core(grad_y)
    grad_both_core = to_core(grad_both)
    grad_low_core, grad_y_core, grad_both_core, *shards = sync(
        grad_low_core, grad_y_core, grad_both_core, *shards_of(low_at, fc2_mine, got)
    )
    fc2_a, fc2_b = (Gather(shard) for shard in shards)
    heads_b.forward()
    fc2_a.start()
    all_grad, grad_sums = stack_pieces(
        [
            out_grad,
            grad_low,
            grad_y,
            grad_both,
            grad_core,
            grad_low_core,
            grad_y_core,
            grad_both_core,
        ]
    )
    heads_full = [heads_a.whole()]
    all_grad, heads_full[0], *partials, fc2_b.own = segment(
        [all_grad, heads_full[0], *sums_of((all_grad, activated)), fc2_b.own], heads_b, fc2_a
    )
    d_fc2_a, d_fc2_b = as_sums(partials)
    fc2_a.forward()
    fc2_b.start()
    heads_full.append(heads_b.whole())
    bias = lax.dynamic_slice_in_dim(qkv_bias, low_at * half, half, 1)
    bias = bias.reshape(3, pairs, pair).transpose(1, 0, 2).reshape(1, 3 * half)
    projected, back = heads_inputs(all_normed, all_grad, heads_full, bias)
    projected, back, d_fc2_a.given, d_fc2_b.given = segment(
        [projected, back, d_fc2_a.given, d_fc2_b.given], fc2_a, fc2_b
    )
    fc2_b.forward()
    d_fc2_a.start()
    attended, qkv_grad, qkv_sums = attention(projected, back, starts, place)
    fc2_full = [fc2_a.whole()]
    attended, qkv_grad, qkv_sums, fc2_full[0], d_fc2_b.given = segment(
        [attended, qkv_grad, qkv_sums, fc2_full[0], d_fc2_b.given], fc2_b, d_fc2_a
    )
    d_fc2_b.start()
    d_fc2_a.second()
    fc2_full.append(fc2_b.whole())
    columns = heads_full[0].shape[1]
    first, second = slice(0, columns), slice(columns, 2 * columns)
    qkv_end = 3 * half - columns
    everything = slice(None)
    branch_products = (
        [attended, activated],
        [heads_full[1], *fc2_full],
        [
            (0, everything, 0, slice(qkv_end, columns)),
            (1, first, 1, everything),
            (1, second, 2, everything),
        ],
    )
    far, *partials = segment(
        [
            *half_rows(branch_kernel, "branch", 1, *branch_products),
            *sums_of((all_normed, qkv_grad), (all_grad, attended)),
        ],
        d_fc2_a,
        d_fc2_b,
    )
    d_heads_a, d_heads_b = as_sums(partials)
    d_heads_a.start()
    d_fc2_b.second()
    d_fc2_a.third()
    branch_got = to_core(far)
    (branch_kept,) = half_rows(branch_kernel, "branch", 0, *branch_products)
    pre_grad, pre_sums = hidden_back(all_grad, fc2_full, slope)
    branch_got, branch_kept, pre_grad, pre_sums, d_heads_b.given = segment(
        [branch_got, branch_kept, pre_grad, pre_sums, d_heads_b.given],
        d_heads_a,
        d_fc2_a,
        d_fc2_b,
    )
    d_heads_b.start()
    d_heads_a.second()
    d_fc2_b.third()
    left, left_given, right, right_given = link_stage(branch_kept, branch_got)
    branch_state = [left, to_y(left_given), right, to_low(right_given)]
    *branch_state, given_a, given_b, kept_a, kept_b = segment(
        [*branch_state, *sums_of((all_normed, pre_grad))], d_heads_a, d_heads_b, d_fc2_b
    )
    d_fc1_a, d_fc1_b = as_sums([given_a, given_b, kept_a, kept_b])
    d_fc1_a.start()
    d_heads_b.second()
    left, left_given, right, right_given = last_stage(*branch_state)
    branch_state = [left, to_low(left_given), right, to_y(right_given)]
    grad_products = (
        [qkv_grad, pre_grad],
        [*heads_full, *fc1_full],
        [
            (0, first, 0, everything),
            (0, slice(columns, 3 * half), 1, slice(0, qkv_end)),
            (1, first, 2, everything),
            (1, second, 3, everything),
        ],
        token_pieces,
        row_stats,
    )
    here = jnp.concatenate([jnp.sum(qkv_sums, axis=(0, 1)), pre_sums[0]])
    bias_got = to_low(here)
    far, far_sums, d_fc1_b.given, here, bias_got, *branch_state = segment(
        [
            *half_rows(token_grad_kernel, "token_grad", 1, *grad_products),
            d_fc1_b.given,
            here,
            bias_got,
            *branch_state,
        ],
        d_fc1_a,
        d_heads_a,
        d_heads_b,
    )
    d_fc1_b.start()
    d_fc1_a.second()
    d_heads_a.third()
    d_heads_b.third()
    got = to_core(far)
    kept, near_sums = half_rows(token_grad_kernel, "token_grad", 0, *grad_products)
    output = row_result(
        output_kernel, "output", *branch_state, tokens, dense_bias[None], fc2_bias[None]
    )
    got, kept, near_sums, output = segment(
        [got, kept, near_sums, output], d_fc1_a, d_fc1_b, d_heads_a, d_heads_b
    )
    d_fc1_b.second()
    d_fc1_a.third()
    left, left_given, right, right_given = link_stage(kept, got)
    grad_state = [left, to_y(left_given), right, to_low(right_given)]
    sums = (near_sums + far_sums).reshape(2 * D)
    sums_got = to_core(sums)
    fc2_weight_grad = final_grad(low_at, *d_fc2_a.halves(), *d_fc2_b.halves())
    q, k, v, dense_weight_grad = final_heads(low_at, *d_heads_a.halves(), *d_heads_b.halves())
    qkv_weight_grad = jnp.stack([q, k, v], axis=1)
    fc2_weight_grad, qkv_weight_grad, dense_weight_grad, sums, sums_got, *grad_state = segment(
        [fc2_weight_grad, qkv_weight_grad, dense_weight_grad, sums, sums_got, *grad_state],
        d_fc1_a,
        d_fc1_b,
    )
    sums = sums + sums_got
    sums_got = [to_low(sums), to_y(sums), swap_both(sums, "zl", 1, "t", 2)]
    left, left_given, right, right_given = last_stage(*grad_state)
    grad_state = [left, to_low(left_given), right, to_y(right_given)]
    d_fc1_b.third()
    sums, *states = segment([sums, *sums_got, *grad_state], d_fc1_b)
    sums = jnp.concatenate([sum(states[:3], sums), grad_sums[0], here, bias_got])
    if pairwise:
        sums_got = [to_high(sums), to_x(sums), swap_both(sums, "zh", 1, "x", 1)]
    else:
        sums_got = [lax.psum(sums, ("zh", "x")) - sums]
    input_grad = row_result(
        input_grad_kernel, "input_grad", *states[3:], tokens, out_grad, ln_gain[None]
    )
    fc1_weight_grad = final_grad(low_at, *d_fc1_a.halves(), *d_fc1_b.halves())
    input_grad, fc1_weight_grad, sums, *sums_got = sync(
        input_grad, fc1_weight_grad, sums, *sums_got
    )
    sums = sum(sums_got, sums)
    both = sums[3 * D :].reshape(2, here.shape[0])
    both = jnp.where(low_at == 0, both, both[::-1])
    qkv_bias_grad = (
        both[:, : 3 * half].reshape(2, pairs, 3, pair).transpose(2, 0, 1, 3).reshape(3, 2 * half)
    )
    return (
        output,
        input_grad,
        sums[:D],
        sums[D : 2 * D],
        qkv_weight_grad,
        qkv_bias_grad,
        dense_weight_grad,
        sums[2 * D : 3 * D],
        fc1_weight_grad,
        both[:, 3 * half :].reshape(2 * hidden),
        fc2_weight_grad,
        sums[2 * D : 3 * D],
    )


def solution(mesh):
    dp, tensor = mesh.shape["dp"], mesh.shape["tensor"]
    rows = ("zh", "zl", "x")
    everywhere = (*rows, "t")
    split = Mesh(np.asarray(mesh.devices).reshape(dp // 4, 2, 2, tensor), everywhere)
    return jax.shard_map(
        body,
        mesh=split,
        in_specs=(
            P(everywhere, None),
            P(everywhere, None),
            P(rows, None),
            P(),
            P(),
            P(rows, None, "t"),
            P(None, "t"),
            P(rows, "t"),
            P(),
            P(rows, "t"),
            P("t"),
            P(rows, "t"),
            P(),
        ),
        out_specs=(
            P(everywhere, None),
            P(everywhere, None),
            P(),
            P(),
            P(rows, None, "t"),
            P(None, "t"),
            P(rows, "t"),
            P(),
            P(rows, "t"),
            P("t"),
            P(rows, "t"),
            P(),
        ),
        check_vma=False,
    )
```

```python
import functools
import math

import jax
import jax.numpy as jnp
import numpy as np
from jax import lax
from jax.experimental import pallas as pl
from jax.experimental.pallas import tpu as pltpu
from jax.sharding import Mesh
from jax.sharding import PartitionSpec as P

D = 2048
H = 32
ROT = 32
LEN = 1024
LONGEST = LEN // 3
HEAD = D // H
QB = 128
BACK = -(-(LONGEST - 1) // QB)

EPSILON = 1e-05
GELU_SCALE = math.sqrt(2.0 / math.pi)
GELU_CUBIC = 0.044715
MASK_VALUE = -1e30
ROPE_BASE = 10000.0
LOW = jnp.bfloat16
FULL = jnp.float32


def gelu_both(pre_gelu):
    square = pre_gelu * pre_gelu
    tangent = jnp.tanh(GELU_SCALE * pre_gelu * (1.0 + GELU_CUBIC * square))
    value = 0.5 * pre_gelu * (1.0 + tangent)
    slope = 0.5 * (1.0 + tangent) + 0.5 * pre_gelu * (1.0 - tangent * tangent) * GELU_SCALE * (
        1.0 + 3.0 * GELU_CUBIC * square
    )
    return value, slope


def rotary_lanes():
    half = ROT // 2
    inverse = ROPE_BASE ** (-(2.0 * np.arange(half)) / ROT)
    angles = np.arange(LEN)[:, None] * inverse[None, :]
    rest = np.zeros((LEN, HEAD - ROT))
    cosine = np.concatenate([np.cos(angles), np.cos(angles), rest + 1.0], axis=1)
    sine = np.concatenate([-np.sin(angles), np.sin(angles), rest], axis=1)
    return tuple(jnp.asarray(np.tile(table, (1, 2)), FULL) for table in (cosine, sine))


def matmul(left, right, left_dim, right_dim):
    return lax.dot_general(
        left, right, (((left_dim,), (right_dim,)), ((), ())), preferred_element_type=FULL
    )


def attention_kernel(
    place_ref, proj_ref, grad_ref, start_ref, cos_ref, sin_ref, att_ref, dqkv_ref, sums_ref,
    q_st, g_st, k_low, v_low, k_turn, v_turn, dk_sum, dv_sum, dq_sum,
):
    pair = 2 * HEAD
    scale = 1.0 / math.sqrt(HEAD)
    part_rows = proj_ref.shape[3]
    parts = LEN // part_rows
    lane = lax.broadcasted_iota(jnp.int32, (part_rows, pair), 1)
    first = lane < HEAD
    near = lane % HEAD < ROT // 2
    y_at, core_at = place_ref[0], place_ref[1]

    def where_is(part):
        return (part % 2) ^ core_at, (part // 2) ^ y_at

    def partner(x):
        return jnp.where(near, pltpu.roll(x, pair - ROT // 2, 1), pltpu.roll(x, ROT // 2, 1))

    per_part = part_rows // QB
    for part in range(parts):
        core, y = where_is(part)
        rows = slice(part * part_rows, (part + 1) * part_rows)
        cosine, sine = cos_ref[rows, :], sin_ref[rows, :]
        projected = proj_ref[core, y, 0]
        q = projected[:, 0:pair]
        k = projected[:, pair : 2 * pair]
        v = projected[:, 2 * pair : 3 * pair]
        q = (q * cosine + partner(q) * sine) * scale
        k = k * cosine + partner(k) * sine
        g = grad_ref[core, y, 0].astype(FULL)
        zero = jnp.zeros_like(q)
        for stacked, whole in ((q_st, q), (g_st, g)):
            for head, own in enumerate(
                (jnp.where(first, whole, zero), jnp.where(first, zero, whole))
            ):
                stacked[
                    part * per_part : (part + 1) * per_part, head * QB : (head + 1) * QB, :
                ] = own.astype(LOW).reshape(per_part, QB, pair)
        k_low[rows, :] = k.astype(LOW)
        v_low[rows, :] = v.astype(LOW)
        k_turn[:, rows] = k.T.astype(LOW)
        v_turn[:, rows] = v.T.astype(LOW)
    dk_sum[...] = jnp.zeros_like(dk_sum)
    dv_sum[...] = jnp.zeros_like(dv_sum)
    upper = lax.broadcasted_iota(jnp.int32, (pair, QB), 0) < HEAD
    for block in range(LEN // QB):
        begin = max(0, block - BACK) * QB
        keys = slice(begin, (block + 1) * QB)
        rows = slice(block * QB, (block + 1) * QB)
        width = (block + 1) * QB - begin
        key_at = begin + lax.broadcasted_iota(jnp.int32, (width, QB), 0)
        query_at = block * QB + lax.broadcasted_iota(jnp.int32, (width, QB), 1)
        allowed = (key_at >= start_ref[0, block : block + 1, :]) & (key_at <= query_at)
        allowed = jnp.concatenate([allowed, allowed], axis=1)
        queries, grads = q_st[block], g_st[block]
        scores = jnp.where(allowed, matmul(k_low[keys], queries, 1, 1), MASK_VALUE)
        powers = jnp.exp(scores - jnp.max(scores, axis=0, keepdims=True))
        probs = powers * (1.0 / jnp.sum(powers, axis=0, keepdims=True))
        probs_low = probs.astype(LOW)
        prob_grad = matmul(v_low[keys], grads, 1, 1)
        row_dot = jnp.sum(probs * prob_grad, axis=0, keepdims=True)
        score_grad = (probs * (prob_grad - row_dot)).astype(LOW)
        dv_sum[keys] += matmul(probs_low, grads, 1, 0)
        dk_sum[keys] += matmul(score_grad, queries, 1, 0)
        turned = matmul(v_turn[:, keys], probs_low, 1, 0)
        core, y = where_is(block // per_part)
        here = slice((block % per_part) * QB, (block % per_part + 1) * QB)
        att_ref[core, y, 0, here, :] = jnp.where(upper, turned[:, :QB], turned[:, QB:]).T.astype(LOW)
        turned = matmul(k_turn[:, keys], score_grad, 1, 0)
        dq_sum[rows, :] = jnp.where(upper, turned[:, :QB], turned[:, QB:]).T
    totals = [jnp.zeros((1, pair), FULL)] * 3
    for part in range(parts):
        core, y = where_is(part)
        rows = slice(part * part_rows, (part + 1) * part_rows)
        cosine, sine = cos_ref[rows, :], sin_ref[rows, :]
        dq, dk = dq_sum[rows, :] * scale, dk_sum[rows, :]
        grads = (
            dq * cosine - partner(dq) * sine,
            dk * cosine - partner(dk) * sine,
            dv_sum[rows, :],
        )
        for at, grad in enumerate(grads):
            dqkv_ref[core, y, 0, :, at * pair : (at + 1) * pair] = grad.astype(LOW)
            totals[at] = totals[at] + jnp.sum(grad, axis=0, keepdims=True)
    for at, total in enumerate(totals):
        sums_ref[0, :, at * pair : (at + 1) * pair] = total


def attention(projected, grads, starts, place):
    rows, width = projected.shape
    seqs, pair = rows // LEN, 2 * HEAD
    pairs = width // (3 * pair)
    part_rows = rows // 8
    cosine, sine = rotary_lanes()
    table = pl.BlockSpec((LEN, pair), lambda s, h, place: (0, 0))

    def block(columns):
        return pl.BlockSpec((2, 2, 1, part_rows, columns), lambda s, h, place: (0, 0, s, 0, h))

    def view(columns):
        return (2, 2, seqs, part_rows, columns)

    attended, grad, sums = pl.pallas_call(
        attention_kernel,
        grid_spec=pltpu.PrefetchScalarGridSpec(
            num_scalar_prefetch=1,
            grid=(seqs, pairs),
            in_specs=[
                block(3 * pair),
                block(pair),
                pl.BlockSpec((1, LEN // QB, QB), lambda s, h, place: (s, 0, 0)),
                table,
                table,
            ],
            out_specs=[
                block(pair),
                block(3 * pair),
                pl.BlockSpec((1, 1, 3 * pair), lambda s, h, place: (s, 0, h)),
            ],
            scratch_shapes=[
                pltpu.VMEM((LEN // QB, 2 * QB, pair), LOW),
                pltpu.VMEM((LEN // QB, 2 * QB, pair), LOW),
                pltpu.VMEM((LEN, pair), LOW),
                pltpu.VMEM((LEN, pair), LOW),
                pltpu.VMEM((pair, LEN), LOW),
                pltpu.VMEM((pair, LEN), LOW),
                pltpu.VMEM((LEN, pair), FULL),
                pltpu.VMEM((LEN, pair), FULL),
                pltpu.VMEM((LEN, pair), FULL),
            ],
        ),
        out_shape=[
            jax.ShapeDtypeStruct(view(pairs * pair), LOW),
            jax.ShapeDtypeStruct(view(width), LOW),
            jax.ShapeDtypeStruct((seqs, 1, width), FULL),
        ],
        compiler_params=pltpu.CompilerParams(vmem_limit_bytes=58 << 20),
        cost_estimate=pl.CostEstimate(
            flops=seqs * LEN * QB * (BACK + 1) * pair // 8,
            transcendentals=0,
            bytes_accessed=rows * width // 8,
        ),
        name="attention_both_ways",
    )(
        place,
        projected.reshape(view(width)),
        grads.reshape(view(pairs * pair)),
        starts.reshape(seqs, LEN // QB, QB),
        cosine,
        sine,
    )
    return attended.reshape(rows, pairs * pair), grad.reshape(rows, width), sums


def swap(value, axis, bit):
    return lax.ppermute(value, axis, [(i, i ^ bit) for i in range(lax.axis_size(axis))])


def swap_both(value, axis, bit, other_axis, other_bit):
    inner = lax.axis_size(other_axis)
    pairs = [
        (i, ((i // inner) ^ bit) * inner + ((i % inner) ^ other_bit))
        for i in range(lax.axis_size(axis) * inner)
    ]
    return lax.ppermute(value, (axis, other_axis), pairs)


def normalize_rows(token_rows):
    values = token_rows.astype(FULL)
    centered = values - jnp.mean(values, axis=-1, keepdims=True)
    inv_std = lax.rsqrt(jnp.mean(centered * centered, axis=-1, keepdims=True) + EPSILON)
    return centered * inv_std, inv_std


def row_blocks(columns, rows):
    return pl.BlockSpec((rows, columns), lambda i, *_: (i, 0))


def resident(*shape):
    return pl.BlockSpec(shape, lambda i, *_: (0,) * len(shape), pipeline_mode=pl.Buffered(1))


def like(*shape, dtype=LOW):
    return jax.ShapeDtypeStruct(shape, dtype)


def run_kernel(
    kernel, steps, in_specs, out_specs, out_shape, name, *operands, scalars=(), room=None
):
    if scalars:
        scalars = (jnp.stack([jnp.asarray(scalar, jnp.int32) for scalar in scalars]),)
    return pl.pallas_call(
        kernel,
        grid_spec=pltpu.PrefetchScalarGridSpec(
            num_scalar_prefetch=len(scalars),
            grid=(steps,),
            in_specs=in_specs,
            out_specs=out_specs,
        ),
        out_shape=out_shape,
        compiler_params=pltpu.CompilerParams(vmem_limit_bytes=(room or (52 if steps > 1 else 32)) << 20),
        cost_estimate=pl.CostEstimate(flops=1 << 24, transcendentals=0, bytes_accessed=1 << 18),
        name=name,
    )(*scalars, *operands)


def whole(*values):
    return [resident(*value.shape) for value in values]


def halves_kernel(low_ref, *refs):
    count = len(refs) // 3
    for source, mine, given in zip(refs[:count], refs[count : 2 * count], refs[2 * count :]):
        columns = mine.shape[1]
        for target, at in ((mine, low_ref[0]), (given, 1 - low_ref[0])):
            target[...] = source[:, pl.ds(pl.multiple_of(at * columns, columns), columns)]


def halves_of(low_at, *weights):
    outs = [like(weight.shape[0], weight.shape[1] // 2) for weight in weights] * 2
    found = run_kernel(
        halves_kernel, 1, whole(*weights), whole(*outs), outs, "halves", *weights, scalars=[low_at]
    )
    return found[: len(weights)], found[len(weights) :]


def heads_halves_kernel(low_ref, q_ref, k_ref, v_ref, dense_ref, mine_ref, given_ref):
    pair = 2 * HEAD
    half = dense_ref.shape[1] // 2
    for target, at in ((mine_ref, low_ref[0]), (given_ref, 1 - low_ref[0])):
        for which in range(half // pair):
            columns = pl.ds(pl.multiple_of(at * half + which * pair, pair), pair)
            for part, source in enumerate((q_ref, k_ref, v_ref)):
                begin = (3 * which + part) * pair
                target[:, begin : begin + pair] = source[:, columns]
        target[:, 3 * half :] = dense_ref[:, pl.ds(pl.multiple_of(at * half, half), half)]


def heads_halves(low_at, qkv_weight, dense_weight):
    operands = (*(qkv_weight[:, part] for part in range(3)), dense_weight)
    out = like(dense_weight.shape[0], 2 * dense_weight.shape[1])
    return run_kernel(
        heads_halves_kernel,
        1,
        whole(*operands),
        whole(out, out),
        [out, out],
        "heads_halves",
        *operands,
        scalars=[low_at],
    )


def shard_kernel(low_ref, mine_ref, got_ref, *shard_refs):
    rows, columns = mine_ref.shape[0], shard_refs[0].shape[1]
    for source, at in ((mine_ref, low_ref[0]), (got_ref, 1 - low_ref[0])):
        for which, shard_ref in enumerate(shard_refs):
            here = slice(which * columns, (which + 1) * columns)
            shard_ref[pl.ds(pl.multiple_of(at * rows, rows), rows), :] = source[:, here]


def shards_of(low_at, mine, got):
    out = like(2 * mine.shape[0], mine.shape[1] // 2)
    return run_kernel(
        shard_kernel,
        1,
        whole(mine, got),
        whole(out, out),
        [out, out],
        "shards",
        mine,
        got,
        scalars=[low_at],
    )


def place_kernel(at_ref, *refs):
    *pieces, full = refs
    rows = pieces[0].shape[0] // 2
    for at, piece in enumerate(pieces):
        slot = 4 * (at_ref[0] ^ (at // 2)) + (at_ref[1] ^ (at % 2))
        for low in (0, 1):
            begin = pl.multiple_of((slot + 2 * low) * rows, rows)
            full[pl.ds(begin, rows), :] = piece[low * rows : (low + 1) * rows, :]


def place_pieces(high_at, x_at, *pieces):
    rows, columns = pieces[0].shape
    steps = 2
    block = pl.BlockSpec((rows, columns // steps), lambda i, *_: (0, i))
    return run_kernel(
        place_kernel,
        steps,
        [block] * 4,
        pl.BlockSpec((4 * rows, columns // steps), lambda i, *_: (0, i)),
        like(4 * rows, columns),
        "place_pieces",
        *pieces,
        scalars=[high_at, x_at],
    )


def from_piece(pieces, use):
    for at, piece in enumerate(pieces):

        @pl.when(pl.program_id(0) == at)
        def _(piece=piece):
            use(piece)


def normalize_kernel(*refs):
    *pieces, gain_ref, shift_ref, normed_ref, mean_ref, inv_std_ref = refs

    def use(piece):
        values = piece[...].astype(FULL)
        mean = jnp.mean(values, axis=-1, keepdims=True)
        centered = values - mean
        inv_std = lax.rsqrt(jnp.mean(centered * centered, axis=-1, keepdims=True) + EPSILON)
        normed_ref[...] = (centered * inv_std * gain_ref[...] + shift_ref[...]).astype(LOW)
        mean_ref[...] = mean
        inv_std_ref[...] = inv_std

    from_piece(pieces, use)


def normalize_all(pieces, gain, shift):
    step, width = pieces[0].shape
    return run_kernel(
        normalize_kernel,
        len(pieces),
        whole(*pieces, gain, shift),
        [row_blocks(width, step), row_blocks(1, step), row_blocks(1, step)],
        [like(step * len(pieces), width)] + [like(step * len(pieces), 1, dtype=FULL)] * 2,
        "normalize_all",
        *pieces,
        gain,
        shift,
    )


def stack_kernel(*refs):
    *pieces, whole_ref, sums_ref = refs

    @pl.when(pl.program_id(0) == 0)
    def _():
        sums_ref[...] = jnp.zeros_like(sums_ref)

    def use(piece):
        whole_ref[...] = piece[...]
        sums_ref[...] += jnp.sum(piece[...].astype(FULL), axis=0, keepdims=True)

    from_piece(pieces, use)


def stack_pieces(pieces):
    step, width = pieces[0].shape
    return run_kernel(
        stack_kernel,
        len(pieces),
        whole(*pieces),
        [row_blocks(width, step), resident(1, width)],
        [like(step * len(pieces), width), like(1, width, dtype=FULL)],
        "stack_pieces",
        *pieces,
    )


def column_parts(width, count):
    return [slice(at * width // count, (at + 1) * width // count) for at in range(count)]


def hidden_kernel(normed_ref, *refs):
    *weight_refs, bias_ref, activated_ref, slope_ref = refs
    for weight_ref, here in zip(weight_refs, column_parts(bias_ref.shape[1], len(weight_refs))):
        pre_gelu = matmul(normed_ref[...], weight_ref[...], 1, 0) + bias_ref[:, here]
        value, slope = gelu_both(pre_gelu)
        activated_ref[:, here] = value.astype(LOW)
        slope_ref[:, here] = slope.astype(LOW)


def hidden_forward(normed, weights, bias):
    rows, columns, step = normed.shape[0], bias.shape[1], 256
    return run_kernel(
        hidden_kernel,
        rows // step,
        [row_blocks(normed.shape[1], step), *whole(*weights, bias)],
        [row_blocks(columns, step)] * 2,
        [like(rows, columns)] * 2,
        "hidden_forward",
        normed,
        *weights,
        bias,
    )


def hidden_back_kernel(grad_ref, *refs):
    *weight_refs, slope_ref, pre_grad_ref, sums_ref = refs

    @pl.when(pl.program_id(0) == 0)
    def _():
        sums_ref[...] = jnp.zeros_like(sums_ref)

    for weight_ref, here in zip(weight_refs, column_parts(slope_ref.shape[1], len(weight_refs))):
        pre_grad = matmul(grad_ref[...], weight_ref[...], 1, 0) * slope_ref[:, here].astype(FULL)
        pre_grad_ref[:, here] = pre_grad.astype(LOW)
        sums_ref[:, here] += jnp.sum(pre_grad, axis=0, keepdims=True)


def hidden_back(grad, weights, slope):
    rows, columns, step = grad.shape[0], slope.shape[1], 256
    return run_kernel(
        hidden_back_kernel,
        rows // step,
        [row_blocks(grad.shape[1], step), *whole(*weights), row_blocks(columns, step)],
        [row_blocks(columns, step), resident(1, columns)],
        [like(rows, columns), like(1, columns, dtype=FULL)],
        "hidden_back",
        grad,
        *weights,
        slope,
    )


def heads_kernel(normed_ref, grad_ref, left_ref, right_ref, bias_ref, projected_ref, back_ref):
    columns = left_ref.shape[1]
    split = projected_ref.shape[1] - columns
    projected_ref[:, :columns] = (
        matmul(normed_ref[...], left_ref[...], 1, 0) + bias_ref[:, :columns]
    )
    projected_ref[:, columns:] = (
        matmul(normed_ref[...], right_ref[:, :split], 1, 0) + bias_ref[:, columns:]
    )
    back_ref[...] = matmul(grad_ref[...], right_ref[:, split:], 1, 0).astype(LOW)


def heads_inputs(normed, grad, weights, bias):
    rows, split, step = normed.shape[0], bias.shape[1], 256
    columns = sum(weight.shape[1] for weight in weights) - split
    return run_kernel(
        heads_kernel,
        rows // step,
        [
            row_blocks(normed.shape[1], step),
            row_blocks(grad.shape[1], step),
            *whole(*weights, bias),
        ],
        [row_blocks(split, step), row_blocks(columns, step)],
        [like(rows, split, dtype=FULL), like(rows, columns)],
        "heads_inputs",
        normed,
        grad,
        *weights,
        bias,
    )


def products_of(lefts, rights):
    values = [matmul(left[...], right[...], 0, 0).astype(LOW) for left, right in zip(lefts, rights)]
    return values[0] if len(values) == 1 else jnp.concatenate(values, axis=1)


def weight_grad_kernel(count, x_ref, *refs):
    lefts, rights, outs = refs[:count], refs[count : 2 * count], refs[2 * count :]
    value = products_of(lefts, rights)
    columns = outs[0].shape[1]
    for first, targets in ((True, outs[:2]), (False, outs[2:])):

        @pl.when((pl.program_id(0) < 4) == first)
        def _(targets=targets):
            for which, target in enumerate(targets):
                target[...] = value[:, which * columns : (which + 1) * columns]


def weight_grad(x_at, *products):
    lefts, rights = zip(*products)
    tokens, width = lefts[0].shape
    columns, step = sum(right.shape[1] for right in rights) // 2, width // 8

    def rows_of(i, x_ref):
        return (0, (i % 4) * 2 + jnp.where(i < 4, 1 - x_ref[0], x_ref[0]))

    return run_kernel(
        functools.partial(weight_grad_kernel, len(products)),
        8,
        [pl.BlockSpec((tokens, step), rows_of)] * len(products) + whole(*rights),
        [pl.BlockSpec((step, columns), lambda i, *_: (jnp.minimum(i, 3), 0))] * 2
        + [pl.BlockSpec((step, columns), lambda i, *_: (jnp.maximum(i - 4, 0), 0))] * 2,
        [like(width // 2, columns)] * 4,
        "weight_grad",
        *lefts,
        *rights,
        scalars=[x_at],
    )


def weight_grad_plain_kernel(count, *refs):
    lefts, rights, outs = refs[:count], refs[count : 2 * count], refs[2 * count :]
    value = products_of(lefts, rights)
    for out_ref, here in zip(outs, column_parts(value.shape[1], 2)):
        out_ref[...] = value[:, here]


def weight_grad_plain(*products):
    lefts, rights = zip(*products)
    tokens, width = lefts[0].shape
    columns, step = sum(right.shape[1] for right in rights) // 2, 256
    return run_kernel(
        functools.partial(weight_grad_plain_kernel, len(products)),
        width // step,
        [pl.BlockSpec((tokens, step), lambda i, *_: (0, i))] * len(products) + whole(*rights),
        [row_blocks(columns, step)] * 2,
        [like(width, columns)] * 2,
        "weight_grad",
        *lefts,
        *rights,
    )


def fold_kernel(at_ref, kept_ref, got_ref, mine_ref, given_ref):
    rows = mine_ref.shape[0]
    for target, at in ((mine_ref, at_ref[0]), (given_ref, 1 - at_ref[0])):
        here = pl.ds(pl.multiple_of(at * rows, rows), rows)
        target[...] = (kept_ref[here, :].astype(FULL) + got_ref[here, :].astype(FULL)).astype(LOW)


def fold(at, kept, got):
    out = like(kept.shape[0] // 2, kept.shape[1])
    return run_kernel(
        fold_kernel, 1, whole(kept, got), whole(out, out), [out, out], "fold", kept, got, scalars=[at]
    )


def final_kernel(low_ref, *refs):
    *pairs, out_ref = refs
    columns = pairs[0].shape[1]
    for which in (0, 1):
        for source, at in ((pairs[2 * which], low_ref[0]), (pairs[2 * which + 1], 1 - low_ref[0])):
            begin = pl.multiple_of((2 * at + which) * columns, columns)
            out_ref[:, pl.ds(begin, columns)] = source[...].astype(FULL)


def final_grad(low_at, *pairs):
    out = like(pairs[0].shape[0], 4 * pairs[0].shape[1], dtype=FULL)
    return run_kernel(
        final_kernel,
        1,
        whole(*pairs),
        resident(*out.shape),
        out,
        "final_grad",
        *pairs,
        scalars=[low_at],
        room=58,
    )


def final_heads_kernel(low_ref, *refs):
    pairs, (q_ref, k_ref, v_ref, dense_ref) = refs[:4], refs[4:]
    pair = 2 * HEAD
    half = dense_ref.shape[1] // 2
    for own, at in ((0, low_ref[0]), (1, 1 - low_ref[0])):
        source = jnp.concatenate([pairs[own][...], pairs[2 + own][...]], axis=1).astype(FULL)
        for which in range(half // pair):
            columns = pl.ds(pl.multiple_of(at * half + which * pair, pair), pair)
            for part, target in enumerate((q_ref, k_ref, v_ref)):
                begin = (3 * which + part) * pair
                target[:, columns] = source[:, begin : begin + pair]
        dense_ref[:, pl.ds(pl.multiple_of(at * half, half), half)] = source[:, 3 * half :]


def final_heads(low_at, *pairs):
    out = like(pairs[0].shape[0], pairs[0].shape[1], dtype=FULL)
    return run_kernel(
        final_heads_kernel,
        1,
        whole(*pairs),
        whole(*[out] * 4),
        [out] * 4,
        "final_heads",
        *pairs,
        scalars=[low_at],
        room=58,
    )


def sum_of_products(left_refs, right_refs, terms):
    total = None
    for left_at, left_columns, right_at, right_columns in terms:
        product = matmul(left_refs[left_at][:, left_columns], right_refs[right_at][:, right_columns], 1, 1)
        total = product if total is None else total + product
    return total


def branch_kernel(counts, terms, *refs):
    lefts, rights = refs[: counts[0]], refs[counts[0] : sum(counts)]
    refs[-1][...] = sum_of_products(lefts, rights, terms).astype(LOW)


def token_grad_kernel(counts, terms, *refs):
    lefts, rights = refs[: counts[0]], refs[counts[0] : sum(counts)]
    pieces, (mean_ref, inv_std_ref, out_ref, sums_ref) = refs[sum(counts) : -4], refs[-4:]
    grad = sum_of_products(lefts, rights, terms)
    out_ref[...] = grad.astype(LOW)
    sums_ref[1:2, :] = jnp.sum(grad, axis=0, keepdims=True)
    step = pieces[0].shape[0]
    total = None
    for at, piece in enumerate(pieces):
        rows = slice(at * step, (at + 1) * step)
        x_hat = (piece[...].astype(FULL) - mean_ref[rows, :]) * inv_std_ref[rows, :]
        part = jnp.sum(grad[rows, :] * x_hat, axis=0, keepdims=True)
        total = part if total is None else total + part
    sums_ref[0:1, :] = total


def branch_rows(far, lefts, rights, terms):
    rows, width, step = lefts[0].shape[0] // 2, rights[0].shape[0], 256
    blocks = rows // step
    return run_kernel(
        functools.partial(branch_kernel, (len(lefts), len(rights)), terms),
        blocks,
        [
            pl.BlockSpec((step, left.shape[1]), lambda i, *_: (i + blocks * far, 0))
            for left in lefts
        ]
        + whole(*rights),
        row_blocks(width, step),
        like(rows, width),
        "branch",
        *lefts,
        *rights,
    )


def token_grad(far, lefts, rights, terms, pieces, row_stats):
    rows, width = lefts[0].shape[0] // 2, rights[0].shape[0]
    step = 256
    pieces = pieces[4 * far : 4 * far + 4]

    def kept(columns):
        return pl.BlockSpec((rows, columns), lambda i, *_: (far, 0), pipeline_mode=pl.Buffered(1))

    def along_width(height):
        return pl.BlockSpec((height, step), lambda i, *_: (0, i))

    return run_kernel(
        functools.partial(token_grad_kernel, (len(lefts), len(rights)), terms),
        width // step,
        [kept(left.shape[1]) for left in lefts]
        + [row_blocks(right.shape[1], step) for right in rights]
        + [along_width(piece.shape[0]) for piece in pieces]
        + [kept(1) for _ in row_stats],
        [along_width(rows), along_width(2)],
        [like(rows, width), like(2, width, dtype=FULL)],
        "token_grad",
        *lefts,
        *rights,
        *pieces,
        *row_stats,
    )


def to_links(held, left_ref, left_given_ref, right_ref, right_given_ref):
    columns = left_ref.shape[1]

    for at in range(4):

        @pl.when(pl.program_id(0) == at)
        def _(y=at // 2, low=at % 2):
            left = left_given_ref if y else left_ref
            left[...] = held[:, :columns]
            right = right_given_ref if low else right_ref
            right[...] = held[:, columns:]


def links(step, width, sixteenths):
    columns = width * sixteenths // 16
    specs = [
        pl.BlockSpec((step, columns), lambda i, *_: (jnp.minimum(i, 1), 0)),
        pl.BlockSpec((step, columns), lambda i, *_: (jnp.maximum(i - 2, 0), 0)),
        pl.BlockSpec((step, width - columns), lambda i, *_: (i // 2, 0)),
        pl.BlockSpec((step, width - columns), lambda i, *_: (i // 2, 0)),
    ]
    return specs, [like(2 * step, columns)] * 2 + [like(2 * step, width - columns)] * 2


def link_kernel(kept_ref, got_ref, *outs):
    to_links((kept_ref[...].astype(FULL) + got_ref[...].astype(FULL)).astype(LOW), *outs)


def link_stage(kept, got, sixteenths):
    rows, width = kept.shape
    specs, outs = links(rows // 4, width, sixteenths)
    return run_kernel(
        link_kernel,
        4,
        [row_blocks(width, rows // 4)] * 2,
        specs,
        outs,
        "link_stage",
        kept,
        got,
    )


def last_kernel(left_ref, left_got_ref, right_ref, right_got_ref, *outs):
    rows = outs[0].shape[0]
    pairs = ((left_ref, left_got_ref), (right_ref, right_got_ref))
    for at, (kept_ref, got_ref) in enumerate(pairs):
        total = (kept_ref[...].astype(FULL) + got_ref[...].astype(FULL)).astype(LOW)
        outs[2 * at][...] = total[:rows]
        outs[2 * at + 1][...] = total[rows:]


def last_stage(*values):
    outs = [like(value.shape[0] // 2, value.shape[1]) for value in values]
    return run_kernel(last_kernel, 1, whole(*values), whole(*outs), outs, "last_stage", *values)


def joined(refs):
    left, left_got, right, right_got = (ref[...].astype(FULL) for ref in refs)
    return jnp.concatenate([left + left_got, right + right_got], axis=1)


def output_kernel(*refs):
    tokens_ref, dense_bias_ref, fc2_bias_ref, output_ref = refs[4:]
    total = tokens_ref[...].astype(FULL) + joined(refs[:4])
    output_ref[...] = (total + dense_bias_ref[...] + fc2_bias_ref[...]).astype(LOW)


def input_grad_kernel(*refs):
    tokens_ref, out_grad_ref, gain_ref, grad_ref = refs[4:]
    x_hat, inv_std = normalize_rows(tokens_ref[...])
    scaled = joined(refs[:4]) * gain_ref[...]
    token_grad = inv_std * (
        scaled
        - jnp.mean(scaled, axis=-1, keepdims=True)
        - x_hat * jnp.mean(scaled * x_hat, axis=-1, keepdims=True)
    )
    grad_ref[...] = (out_grad_ref[...].astype(FULL) + token_grad).astype(LOW)


def row_result(kernel, name, *operands):
    out = like(*operands[4].shape)
    return run_kernel(
        kernel, 1, whole(*operands), resident(*out.shape), out, name, *operands, room=58
    )


def body(
    tokens,
    out_grad,
    segments,
    ln_gain,
    ln_bias,
    qkv_weight,
    qkv_bias,
    dense_weight,
    dense_bias,
    fc1_weight,
    fc1_bias,
    fc2_weight,
    fc2_bias,
):
    low_at, high_at, x_at = lax.axis_index("zl"), lax.axis_index("zh"), lax.axis_index("x")
    t_at = lax.axis_index("t")
    pairwise = lax.axis_size("zh") == 2
    place = jnp.stack([t_at // 2, t_at % 2]).astype(jnp.int32)
    weight_rows = qkv_weight.shape[0]
    pair = 2 * HEAD
    half = dense_weight.shape[1] // 2
    pairs = half // pair
    hidden = fc1_weight.shape[1] // 2

    before = [()]

    def sync(*values):
        before[0] = lax.optimization_barrier((values, before[0]))[0]
        return before[0]

    def to_low(value):
        return swap(value, "zl", 1)

    def to_high(value):
        return swap(value, "zh", 1)

    def to_x(value):
        return swap(value, "x", 1)

    def to_y(value):
        return swap(value, "t", 2)

    def to_core(value):
        return swap(value, "t", 1)

    class Gather:
        def __init__(self, shard):
            self.own = shard
            self.moving = []

        def start(self):
            if pairwise:
                self.moving = [to_high(self.own), to_x(self.own)]
            else:
                rows, columns = self.own.shape
                gathered = lax.all_gather(self.own, ("zh", "x"), axis=0, tiled=True)
                natural = gathered.reshape(-1, 2, 2, rows // 2, columns).transpose(0, 2, 1, 3, 4)
                self.moving = [natural.reshape(-1, columns)]

        def forward(self):
            if pairwise:
                self.high, self.x = self.moving
                self.moving = [to_x(self.high)]

        def whole(self):
            if pairwise:
                return place_pieces(high_at, x_at, self.own, self.x, self.high, self.moving[0])
            return self.moving[0]

    class Sum:
        def __init__(self, given, kept):
            self.given, self.kept = given, kept
            self.moving = []

        def start(self):
            if pairwise:
                self.moving = [to_x(self.given)]
            else:
                rows, columns = self.given.shape
                blocks = self.given.reshape(-1, 2, 2, weight_rows, columns)
                ordered = blocks.transpose(0, 2, 1, 3, 4).reshape(rows, columns)
                self.moving = [
                    lax.psum_scatter(
                        ordered.astype(FULL), ("zh", "x"), scatter_dimension=0, tiled=True
                    )
                ]

        def second(self):
            if pairwise:
                self.kept, given = fold(high_at, self.kept, self.moving[0])
                self.moving = [to_high(given)]

        def third(self):
            other = self.kept if pairwise else jnp.zeros_like(self.moving[0])
            self.kept, given = fold(low_at, other, self.moving[0])
            self.moving = [to_low(given)]

        def halves(self):
            return [self.kept, self.moving[0]]

    def segment(values, *transfers):
        tied = sync(*values, *[piece for transfer in transfers for piece in transfer.moving])
        at = len(values)
        for transfer in transfers:
            many = len(transfer.moving)
            transfer.moving = list(tied[at : at + many])
            at += many
        return tied[: len(values)]

    def gathers_of(mine, got):
        return [Gather(shard) for shard in sync(*shards_of(low_at, mine, got))]

    def sums_of(*products):
        if pairwise:
            given_a, given_b, kept_a, kept_b = weight_grad(x_at, *products)
        else:
            given_a, given_b = weight_grad_plain(*products)
            kept_a = kept_b = given_a
        return [given_a, given_b, kept_a, kept_b]

    def as_sums(tied):
        return [Sum(tied[0], tied[2]), Sum(tied[1], tied[3])]

    (fc1_mine,), (fc1_given,) = halves_of(low_at, fc1_weight)
    fc1_given, tokens, out_grad, segments, qkv_weight, dense_weight, fc2_weight = sync(
        fc1_given, tokens, out_grad, segments, qkv_weight, dense_weight, fc2_weight
    )
    got = to_low(fc1_given)
    tokens_core, grad_core = to_core(tokens), to_core(out_grad)
    heads_mine, heads_given = heads_halves(low_at, qkv_weight, dense_weight)
    (fc2_mine,), (fc2_given,) = halves_of(low_at, fc2_weight)
    got, tokens_core, grad_core, heads_given, fc2_given, tokens, out_grad, segments = sync(
        got, tokens_core, grad_core, heads_given, fc2_given, tokens, out_grad, segments
    )
    fc1_a, fc1_b = gathers_of(fc1_mine, got)
    tokens, out_grad, segments, heads_given, fc2_given = sync(
        tokens, out_grad, segments, heads_given, fc2_given
    )
    fc1_a.start()
    tokens_low, tokens_y, segments_low = to_low(tokens), to_y(tokens), to_low(segments)
    tokens_low, tokens_y, segments_low, heads_given, fc1_b.own, fc2_given, out_grad = segment(
        [tokens_low, tokens_y, segments_low, heads_given, fc1_b.own, fc2_given, out_grad], fc1_a
    )
    fc1_a.forward()
    fc1_b.start()
    tokens_both, got = to_y(tokens_low), to_low(heads_given)
    all_segments = jnp.concatenate([segments, segments_low])
    starts = jnp.sum(
        (all_segments[:, None, :] < all_segments[:, :, None]).astype(jnp.int32), axis=2
    )
    tokens_both, got, starts, fc2_given, out_grad, tokens_low, tokens_y = segment(
        [tokens_both, got, starts, fc2_given, out_grad, tokens_low, tokens_y], fc1_a, fc1_b
    )
    tokens_low_core, tokens_y_core = to_core(tokens_low), to_core(tokens_y)
    tokens_both_core = to_core(tokens_both)
    shards = shards_of(low_at, heads_mine, got)
    tokens_low_core, tokens_y_core, tokens_both_core, fc2_given, out_grad, *shards = sync(
        tokens_low_core, tokens_y_core, tokens_both_core, fc2_given, out_grad, *shards
    )
    heads_a, heads_b = (Gather(shard) for shard in shards)
    fc1_b.forward()
    heads_a.start()
    grad_low, grad_y = to_low(out_grad), to_y(out_grad)
    token_pieces = [
        tokens,
        tokens_low,
        tokens_y,
        tokens_both,
        tokens_core,
        tokens_low_core,
        tokens_y_core,
        tokens_both_core,
    ]
    all_normed, *row_stats = normalize_all(token_pieces, ln_gain[None], ln_bias[None])
    fc1_full = [fc1_a.whole()]
    all_normed, fc1_full[0], grad_low, grad_y, heads_b.own, fc2_given = segment(
        [all_normed, fc1_full[0], grad_low, grad_y, heads_b.own, fc2_given], fc1_b, heads_a
    )
    heads_a.forward()
    heads_b.start()
    grad_both, got = to_y(grad_low), to_low(fc2_given)
    fc1_full.append(fc1_b.whole())
    bias = lax.dynamic_slice_in_dim(fc1_bias, low_at * hidden, hidden, 0)[None]
    activated, slope = hidden_forward(all_normed, fc1_full, bias)
    activated, slope, grad_both, got, grad_low, grad_y = segment(
        [activated, slope, grad_both, got, grad_low, grad_y], heads_a, heads_b
    )
    grad_low_core, grad_y_core = to_core(grad_low), to_core(grad_y)
    grad_both_core = to_core(grad_both)
    heads_full = [heads_a.whole()]
    heads_full[0], grad_low_core, grad_y_core, grad_both_core, *shards = sync(
        heads_full[0],
        grad_low_core,
        grad_y_core,
        grad_both_core,
        *shards_of(low_at, fc2_mine, got),
    )
    fc2_a, fc2_b = (Gather(shard) for shard in shards)
    heads_b.forward()
    fc2_a.start()
    all_grad, grad_sums = stack_pieces(
        [
            out_grad,
            grad_low,
            grad_y,
            grad_both,
            grad_core,
            grad_low_core,
            grad_y_core,
            grad_both_core,
        ]
    )
    all_grad, *partials, fc2_b.own = segment(
        [all_grad, *sums_of((all_grad, activated)), fc2_b.own], heads_b, fc2_a
    )
    d_fc2_a, d_fc2_b = as_sums(partials)
    fc2_a.forward()
    fc2_b.start()
    heads_full.append(heads_b.whole())
    bias = lax.dynamic_slice_in_dim(qkv_bias, low_at * half, half, 1)
    bias = bias.reshape(3, pairs, pair).transpose(1, 0, 2).reshape(1, 3 * half)
    projected, back = heads_inputs(all_normed, all_grad, heads_full, bias)
    projected, back, d_fc2_a.given, d_fc2_b.given = segment(
        [projected, back, d_fc2_a.given, d_fc2_b.given], fc2_a, fc2_b
    )
    fc2_b.forward()
    d_fc2_a.start()
    attended, qkv_grad, qkv_sums = attention(projected, back, starts, place)
    fc2_full = [fc2_a.whole()]
    attended, qkv_grad, qkv_sums, fc2_full[0], d_fc2_b.given = segment(
        [attended, qkv_grad, qkv_sums, fc2_full[0], d_fc2_b.given], fc2_b, d_fc2_a
    )
    d_fc2_b.start()
    d_fc2_a.second()
    fc2_full.append(fc2_b.whole())
    columns = heads_full[0].shape[1]
    first, second = slice(0, columns), slice(columns, 2 * columns)
    qkv_end = 3 * half - columns
    everything = slice(None)
    branch_products = (
        [attended, activated],
        [heads_full[1], *fc2_full],
        [
            (0, everything, 0, slice(qkv_end, columns)),
            (1, first, 1, everything),
            (1, second, 2, everything),
        ],
    )
    far, *partials = segment(
        [
            branch_rows(1, *branch_products),
            *sums_of((all_normed, qkv_grad), (all_grad, attended)),
        ],
        d_fc2_a,
        d_fc2_b,
    )
    d_heads_a, d_heads_b = as_sums(partials)
    d_heads_a.start()
    d_fc2_b.second()
    d_fc2_a.third()
    branch_got = to_core(far)
    branch_kept = branch_rows(0, *branch_products)
    pre_grad, pre_sums = hidden_back(all_grad, fc2_full, slope)
    branch_got, branch_kept, pre_grad, pre_sums, d_heads_b.given = segment(
        [branch_got, branch_kept, pre_grad, pre_sums, d_heads_b.given],
        d_heads_a,
        d_fc2_a,
        d_fc2_b,
    )
    d_heads_b.start()
    d_heads_a.second()
    d_fc2_b.third()
    left, left_given, right, right_given = link_stage(branch_kept, branch_got, 11)
    branch_state = [left, to_y(left_given), right, to_low(right_given)]
    grad_products = (
        [qkv_grad, pre_grad],
        [*heads_full, *fc1_full],
        [
            (0, first, 0, everything),
            (0, slice(columns, 3 * half), 1, slice(0, qkv_end)),
            (1, first, 2, everything),
            (1, second, 3, everything),
        ],
        token_pieces,
        row_stats,
    )
    far, far_sums, given_a, given_b, kept_a, kept_b, *branch_state = segment(
        [*token_grad(1, *grad_products), *sums_of((all_normed, pre_grad)), *branch_state],
        d_heads_a,
        d_heads_b,
        d_fc2_b,
    )
    d_fc1_a, d_fc1_b = as_sums([given_a, given_b, kept_a, kept_b])
    d_fc1_a.start()
    d_heads_b.second()
    got = to_core(far)
    left, left_given, right, right_given = last_stage(*branch_state)
    branch_state = [left, to_low(left_given), right, to_y(right_given)]
    kept, near_sums = token_grad(0, *grad_products)
    got, kept, near_sums, d_fc1_b.given, *branch_state = segment(
        [got, kept, near_sums, d_fc1_b.given, *branch_state], d_fc1_a, d_heads_a, d_heads_b
    )
    d_fc1_b.start()
    d_fc1_a.second()
    left, left_given, right, right_given = link_stage(kept, got, 10)
    grad_state = [left, to_y(left_given), right, to_low(right_given)]
    output = row_result(
        output_kernel, "output", *branch_state, tokens, dense_bias[None], fc2_bias[None]
    )
    fc2_weight_grad = final_grad(low_at, *d_fc2_a.halves(), *d_fc2_b.halves())
    sums = (near_sums + far_sums).reshape(2 * D)
    sums_got = to_core(sums)
    here = jnp.concatenate([jnp.sum(qkv_sums, axis=(0, 1)), pre_sums[0]])
    output, fc2_weight_grad, sums, sums_got, here, *grad_state = segment(
        [output, fc2_weight_grad, sums, sums_got, here, *grad_state],
        d_fc1_a,
        d_fc1_b,
        d_heads_a,
        d_heads_b,
    )
    d_fc1_b.second()
    d_heads_a.third()
    left, left_given, right, right_given = last_stage(*grad_state)
    grad_state = [left, to_low(left_given), right, to_y(right_given)]
    sums = sums + sums_got
    sums_got = to_y(sums)
    sums, sums_got, here, *grad_state = segment(
        [sums, sums_got, here, *grad_state], d_fc1_a, d_fc1_b, d_heads_a, d_heads_b
    )
    d_fc1_a.third()
    d_fc1_b.third()
    d_heads_b.third()
    packed = jnp.concatenate([sums + sums_got, here])
    packed_got = to_low(packed)
    input_grad = row_result(
        input_grad_kernel, "input_grad", *grad_state, tokens, out_grad, ln_gain[None]
    )
    input_grad, packed, packed_got = segment(
        [input_grad, packed, packed_got], d_fc1_a, d_fc1_b, d_heads_b
    )
    sums = jnp.concatenate(
        [packed[: 2 * D] + packed_got[: 2 * D], grad_sums[0], packed[2 * D :], packed_got[2 * D :]]
    )
    if pairwise:
        sums_got = [to_high(sums), to_x(sums), swap_both(sums, "zh", 1, "x", 1)]
    else:
        sums_got = [lax.psum(sums, ("zh", "x")) - sums]
    q, k, v, dense_weight_grad = final_heads(low_at, *d_heads_a.halves(), *d_heads_b.halves())
    qkv_weight_grad = jnp.stack([q, k, v], axis=1)
    fc1_weight_grad = final_grad(low_at, *d_fc1_a.halves(), *d_fc1_b.halves())
    qkv_weight_grad, dense_weight_grad, fc1_weight_grad, sums, *sums_got = sync(
        qkv_weight_grad, dense_weight_grad, fc1_weight_grad, sums, *sums_got
    )
    sums = sum(sums_got, sums)
    both = sums[3 * D :].reshape(2, here.shape[0])
    both = jnp.where(low_at == 0, both, both[::-1])
    qkv_bias_grad = (
        both[:, : 3 * half].reshape(2, pairs, 3, pair).transpose(2, 0, 1, 3).reshape(3, 2 * half)
    )
    return (
        output,
        input_grad,
        sums[:D],
        sums[D : 2 * D],
        qkv_weight_grad,
        qkv_bias_grad,
        dense_weight_grad,
        sums[2 * D : 3 * D],
        fc1_weight_grad,
        both[:, 3 * half :].reshape(2 * hidden),
        fc2_weight_grad,
        sums[2 * D : 3 * D],
    )


def solution(mesh):
    dp, tensor = mesh.shape["dp"], mesh.shape["tensor"]
    rows = ("zh", "zl", "x")
    everywhere = (*rows, "t")
    split = Mesh(np.asarray(mesh.devices).reshape(dp // 4, 2, 2, tensor), everywhere)
    return jax.shard_map(
        body,
        mesh=split,
        in_specs=(
            P(everywhere, None),
            P(everywhere, None),
            P(rows, None),
            P(),
            P(),
            P(rows, None, "t"),
            P(None, "t"),
            P(rows, "t"),
            P(),
            P(rows, "t"),
            P("t"),
            P(rows, "t"),
            P(),
        ),
        out_specs=(
            P(everywhere, None),
            P(everywhere, None),
            P(),
            P(),
            P(rows, None, "t"),
            P(None, "t"),
            P(rows, "t"),
            P(),
            P(rows, "t"),
            P("t"),
            P(rows, "t"),
            P(),
        ),
        check_vma=False,
    )
```

```python
import functools
import math

import jax
import jax.numpy as jnp
import numpy as np
from jax import lax
from jax.experimental import pallas as pl
from jax.experimental.pallas import tpu as pltpu
from jax.sharding import Mesh
from jax.sharding import PartitionSpec as P

D = 2048
H = 32
ROT = 32
LEN = 1024
LONGEST = LEN // 3
HEAD = D // H
QB = 128
BACK = -(-(LONGEST - 1) // QB)

EPSILON = 1e-05
GELU_SCALE = math.sqrt(2.0 / math.pi)
GELU_CUBIC = 0.044715
MASK_VALUE = -1e30
ROPE_BASE = 10000.0
LOW = jnp.bfloat16
FULL = jnp.float32


def gelu_both(pre_gelu):
    square = pre_gelu * pre_gelu
    tangent = jnp.tanh(GELU_SCALE * pre_gelu * (1.0 + GELU_CUBIC * square))
    value = 0.5 * pre_gelu * (1.0 + tangent)
    slope = 0.5 * (1.0 + tangent) + 0.5 * pre_gelu * (1.0 - tangent * tangent) * GELU_SCALE * (
        1.0 + 3.0 * GELU_CUBIC * square
    )
    return value, slope


def rotary_lanes():
    half = ROT // 2
    inverse = ROPE_BASE ** (-(2.0 * np.arange(half)) / ROT)
    angles = np.arange(LEN)[:, None] * inverse[None, :]
    rest = np.zeros((LEN, HEAD - ROT))
    cosine = np.concatenate([np.cos(angles), np.cos(angles), rest + 1.0], axis=1)
    sine = np.concatenate([-np.sin(angles), np.sin(angles), rest], axis=1)
    return tuple(jnp.asarray(np.tile(table, (1, 2)), FULL) for table in (cosine, sine))


def matmul(left, right, left_dim, right_dim):
    return lax.dot_general(
        left, right, (((left_dim,), (right_dim,)), ((), ())), preferred_element_type=FULL
    )


def attention_kernel(
    place_ref, proj_ref, grad_ref, start_ref, cos_ref, sin_ref, att_ref, dqkv_ref, sums_ref,
    q_st, g_st, k_low, v_low, k_turn, v_turn, dk_sum, dv_sum, dq_sum,
):
    pair = 2 * HEAD
    scale = 1.0 / math.sqrt(HEAD)
    part_rows = proj_ref.shape[3]
    parts = LEN // part_rows
    lane = lax.broadcasted_iota(jnp.int32, (part_rows, pair), 1)
    first = lane < HEAD
    near = lane % HEAD < ROT // 2
    y_at, core_at = place_ref[0], place_ref[1]

    def where_is(part):
        return (part % 2) ^ core_at, (part // 2) ^ y_at

    def partner(x):
        return jnp.where(near, pltpu.roll(x, pair - ROT // 2, 1), pltpu.roll(x, ROT // 2, 1))

    per_part = part_rows // QB
    for part in range(parts):
        core, y = where_is(part)
        rows = slice(part * part_rows, (part + 1) * part_rows)
        cosine, sine = cos_ref[rows, :], sin_ref[rows, :]
        projected = proj_ref[core, y, 0]
        q = projected[:, 0:pair]
        k = projected[:, pair : 2 * pair]
        v = projected[:, 2 * pair : 3 * pair]
        q = (q * cosine + partner(q) * sine) * scale
        k = k * cosine + partner(k) * sine
        g = grad_ref[core, y, 0].astype(FULL)
        zero = jnp.zeros_like(q)
        for stacked, whole in ((q_st, q), (g_st, g)):
            for head, own in enumerate(
                (jnp.where(first, whole, zero), jnp.where(first, zero, whole))
            ):
                stacked[
                    part * per_part : (part + 1) * per_part, head * QB : (head + 1) * QB, :
                ] = own.astype(LOW).reshape(per_part, QB, pair)
        k_low[rows, :] = k.astype(LOW)
        v_low[rows, :] = v.astype(LOW)
        k_turn[:, rows] = k.T.astype(LOW)
        v_turn[:, rows] = v.T.astype(LOW)
    dk_sum[...] = jnp.zeros_like(dk_sum)
    dv_sum[...] = jnp.zeros_like(dv_sum)
    upper = lax.broadcasted_iota(jnp.int32, (pair, QB), 0) < HEAD
    for block in range(LEN // QB):
        begin = max(0, block - BACK) * QB
        keys = slice(begin, (block + 1) * QB)
        rows = slice(block * QB, (block + 1) * QB)
        width = (block + 1) * QB - begin
        key_at = begin + lax.broadcasted_iota(jnp.int32, (width, QB), 0)
        query_at = block * QB + lax.broadcasted_iota(jnp.int32, (width, QB), 1)
        allowed = (key_at >= start_ref[0, block : block + 1, :]) & (key_at <= query_at)
        allowed = jnp.concatenate([allowed, allowed], axis=1)
        queries, grads = q_st[block], g_st[block]
        scores = jnp.where(allowed, matmul(k_low[keys], queries, 1, 1), MASK_VALUE)
        powers = jnp.exp(scores - jnp.max(scores, axis=0, keepdims=True))
        probs = powers * (1.0 / jnp.sum(powers, axis=0, keepdims=True))
        probs_low = probs.astype(LOW)
        prob_grad = matmul(v_low[keys], grads, 1, 1)
        row_dot = jnp.sum(probs * prob_grad, axis=0, keepdims=True)
        score_grad = (probs * (prob_grad - row_dot)).astype(LOW)
        dv_sum[keys] += matmul(probs_low, grads, 1, 0)
        dk_sum[keys] += matmul(score_grad, queries, 1, 0)
        turned = matmul(v_turn[:, keys], probs_low, 1, 0)
        core, y = where_is(block // per_part)
        here = slice((block % per_part) * QB, (block % per_part + 1) * QB)
        att_ref[core, y, 0, here, :] = jnp.where(upper, turned[:, :QB], turned[:, QB:]).T.astype(LOW)
        turned = matmul(k_turn[:, keys], score_grad, 1, 0)
        dq_sum[rows, :] = jnp.where(upper, turned[:, :QB], turned[:, QB:]).T
    totals = [jnp.zeros((1, pair), FULL)] * 3
    for part in range(parts):
        core, y = where_is(part)
        rows = slice(part * part_rows, (part + 1) * part_rows)
        cosine, sine = cos_ref[rows, :], sin_ref[rows, :]
        dq, dk = dq_sum[rows, :] * scale, dk_sum[rows, :]
        grads = (
            dq * cosine - partner(dq) * sine,
            dk * cosine - partner(dk) * sine,
            dv_sum[rows, :],
        )
        for at, grad in enumerate(grads):
            dqkv_ref[core, y, 0, :, at * pair : (at + 1) * pair] = grad.astype(LOW)
            totals[at] = totals[at] + jnp.sum(grad, axis=0, keepdims=True)
    for at, total in enumerate(totals):
        sums_ref[0, :, at * pair : (at + 1) * pair] = total


def attention(projected, grads, starts, place):
    rows, width = projected.shape
    seqs, pair = rows // LEN, 2 * HEAD
    pairs = width // (3 * pair)
    part_rows = rows // 8
    cosine, sine = rotary_lanes()
    table = pl.BlockSpec((LEN, pair), lambda s, h, place: (0, 0))

    def block(columns):
        return pl.BlockSpec((2, 2, 1, part_rows, columns), lambda s, h, place: (0, 0, s, 0, h))

    def view(columns):
        return (2, 2, seqs, part_rows, columns)

    attended, grad, sums = pl.pallas_call(
        attention_kernel,
        grid_spec=pltpu.PrefetchScalarGridSpec(
            num_scalar_prefetch=1,
            grid=(seqs, pairs),
            in_specs=[
                block(3 * pair),
                block(pair),
                pl.BlockSpec((1, LEN // QB, QB), lambda s, h, place: (s, 0, 0)),
                table,
                table,
            ],
            out_specs=[
                block(pair),
                block(3 * pair),
                pl.BlockSpec((1, 1, 3 * pair), lambda s, h, place: (s, 0, h)),
            ],
            scratch_shapes=[
                pltpu.VMEM((LEN // QB, 2 * QB, pair), LOW),
                pltpu.VMEM((LEN // QB, 2 * QB, pair), LOW),
                pltpu.VMEM((LEN, pair), LOW),
                pltpu.VMEM((LEN, pair), LOW),
                pltpu.VMEM((pair, LEN), LOW),
                pltpu.VMEM((pair, LEN), LOW),
                pltpu.VMEM((LEN, pair), FULL),
                pltpu.VMEM((LEN, pair), FULL),
                pltpu.VMEM((LEN, pair), FULL),
            ],
        ),
        out_shape=[
            jax.ShapeDtypeStruct(view(pairs * pair), LOW),
            jax.ShapeDtypeStruct(view(width), LOW),
            jax.ShapeDtypeStruct((seqs, 1, width), FULL),
        ],
        compiler_params=pltpu.CompilerParams(vmem_limit_bytes=58 << 20),
        cost_estimate=pl.CostEstimate(
            flops=seqs * LEN * QB * (BACK + 1) * pair // 8,
            transcendentals=0,
            bytes_accessed=rows * width // 8,
        ),
        name="attention_both_ways",
    )(
        place,
        projected.reshape(view(width)),
        grads.reshape(view(pairs * pair)),
        starts.reshape(seqs, LEN // QB, QB),
        cosine,
        sine,
    )
    return attended.reshape(rows, pairs * pair), grad.reshape(rows, width), sums


def swap(value, axis, bit):
    return lax.ppermute(value, axis, [(i, i ^ bit) for i in range(lax.axis_size(axis))])


def swap_both(value, axis, bit, other_axis, other_bit):
    inner = lax.axis_size(other_axis)
    pairs = [
        (i, ((i // inner) ^ bit) * inner + ((i % inner) ^ other_bit))
        for i in range(lax.axis_size(axis) * inner)
    ]
    return lax.ppermute(value, (axis, other_axis), pairs)


def normalize_rows(token_rows):
    values = token_rows.astype(FULL)
    centered = values - jnp.mean(values, axis=-1, keepdims=True)
    inv_std = lax.rsqrt(jnp.mean(centered * centered, axis=-1, keepdims=True) + EPSILON)
    return centered * inv_std, inv_std


def row_blocks(columns, rows):
    return pl.BlockSpec((rows, columns), lambda i, *_: (i, 0))


def resident(*shape):
    return pl.BlockSpec(shape, lambda i, *_: (0,) * len(shape), pipeline_mode=pl.Buffered(1))


def like(*shape, dtype=LOW):
    return jax.ShapeDtypeStruct(shape, dtype)


def run_kernel(
    kernel, steps, in_specs, out_specs, out_shape, name, *operands, scalars=(), room=None
):
    if scalars:
        scalars = (jnp.stack([jnp.asarray(scalar, jnp.int32) for scalar in scalars]),)
    return pl.pallas_call(
        kernel,
        grid_spec=pltpu.PrefetchScalarGridSpec(
            num_scalar_prefetch=len(scalars),
            grid=(steps,),
            in_specs=in_specs,
            out_specs=out_specs,
        ),
        out_shape=out_shape,
        compiler_params=pltpu.CompilerParams(vmem_limit_bytes=(room or (52 if steps > 1 else 32)) << 20),
        cost_estimate=pl.CostEstimate(flops=1 << 24, transcendentals=0, bytes_accessed=1 << 18),
        name=name,
    )(*scalars, *operands)


def whole(*values):
    return [resident(*value.shape) for value in values]


def halves_kernel(low_ref, *refs):
    count = len(refs) // 3
    for source, mine, given in zip(refs[:count], refs[count : 2 * count], refs[2 * count :]):
        columns = mine.shape[1]
        for target, at in ((mine, low_ref[0]), (given, 1 - low_ref[0])):
            target[...] = source[:, pl.ds(pl.multiple_of(at * columns, columns), columns)]


def halves_of(low_at, *weights):
    outs = [like(weight.shape[0], weight.shape[1] // 2) for weight in weights] * 2
    found = run_kernel(
        halves_kernel, 1, whole(*weights), whole(*outs), outs, "halves", *weights, scalars=[low_at]
    )
    return found[: len(weights)], found[len(weights) :]


def heads_halves_kernel(low_ref, q_ref, k_ref, v_ref, dense_ref, mine_ref, given_ref):
    pair = 2 * HEAD
    half = dense_ref.shape[1] // 2
    for target, at in ((mine_ref, low_ref[0]), (given_ref, 1 - low_ref[0])):
        for which in range(half // pair):
            columns = pl.ds(pl.multiple_of(at * half + which * pair, pair), pair)
            for part, source in enumerate((q_ref, k_ref, v_ref)):
                begin = (3 * which + part) * pair
                target[:, begin : begin + pair] = source[:, columns]
        target[:, 3 * half :] = dense_ref[:, pl.ds(pl.multiple_of(at * half, half), half)]


def heads_halves(low_at, qkv_weight, dense_weight):
    operands = (*(qkv_weight[:, part] for part in range(3)), dense_weight)
    out = like(dense_weight.shape[0], 2 * dense_weight.shape[1])
    return run_kernel(
        heads_halves_kernel,
        1,
        whole(*operands),
        whole(out, out),
        [out, out],
        "heads_halves",
        *operands,
        scalars=[low_at],
    )


def shard_kernel(low_ref, mine_ref, got_ref, *shard_refs):
    rows, columns = mine_ref.shape[0], shard_refs[0].shape[1]
    for source, at in ((mine_ref, low_ref[0]), (got_ref, 1 - low_ref[0])):
        for which, shard_ref in enumerate(shard_refs):
            here = slice(which * columns, (which + 1) * columns)
            shard_ref[pl.ds(pl.multiple_of(at * rows, rows), rows), :] = source[:, here]


def shards_of(low_at, mine, got):
    out = like(2 * mine.shape[0], mine.shape[1] // 2)
    return run_kernel(
        shard_kernel,
        1,
        whole(mine, got),
        whole(out, out),
        [out, out],
        "shards",
        mine,
        got,
        scalars=[low_at],
    )


def place_kernel(at_ref, *refs):
    *pieces, full = refs
    rows = pieces[0].shape[0] // 2
    for at, piece in enumerate(pieces):
        slot = 4 * (at_ref[0] ^ (at // 2)) + (at_ref[1] ^ (at % 2))
        for low in (0, 1):
            begin = pl.multiple_of((slot + 2 * low) * rows, rows)
            full[pl.ds(begin, rows), :] = piece[low * rows : (low + 1) * rows, :]


def place_pieces(high_at, x_at, *pieces):
    rows, columns = pieces[0].shape
    steps = 2
    block = pl.BlockSpec((rows, columns // steps), lambda i, *_: (0, i))
    return run_kernel(
        place_kernel,
        steps,
        [block] * 4,
        pl.BlockSpec((4 * rows, columns // steps), lambda i, *_: (0, i)),
        like(4 * rows, columns),
        "place_pieces",
        *pieces,
        scalars=[high_at, x_at],
    )


def from_piece(pieces, use):
    for at, piece in enumerate(pieces):

        @pl.when(pl.program_id(0) == at)
        def _(piece=piece):
            use(piece)


def normalize_kernel(*refs):
    *pieces, gain_ref, shift_ref, normed_ref, mean_ref, inv_std_ref = refs

    def use(piece):
        values = piece[...].astype(FULL)
        mean = jnp.mean(values, axis=-1, keepdims=True)
        centered = values - mean
        inv_std = lax.rsqrt(jnp.mean(centered * centered, axis=-1, keepdims=True) + EPSILON)
        normed_ref[...] = (centered * inv_std * gain_ref[...] + shift_ref[...]).astype(LOW)
        mean_ref[...] = mean
        inv_std_ref[...] = inv_std

    from_piece(pieces, use)


def normalize_all(pieces, gain, shift):
    step, width = pieces[0].shape
    return run_kernel(
        normalize_kernel,
        len(pieces),
        whole(*pieces, gain, shift),
        [row_blocks(width, step), row_blocks(1, step), row_blocks(1, step)],
        [like(step * len(pieces), width)] + [like(step * len(pieces), 1, dtype=FULL)] * 2,
        "normalize_all",
        *pieces,
        gain,
        shift,
    )


def stack_kernel(*refs):
    *pieces, whole_ref, sums_ref = refs

    @pl.when(pl.program_id(0) == 0)
    def _():
        sums_ref[...] = jnp.zeros_like(sums_ref)

    def use(piece):
        whole_ref[...] = piece[...]
        sums_ref[...] += jnp.sum(piece[...].astype(FULL), axis=0, keepdims=True)

    from_piece(pieces, use)


def stack_pieces(pieces):
    step, width = pieces[0].shape
    return run_kernel(
        stack_kernel,
        len(pieces),
        whole(*pieces),
        [row_blocks(width, step), resident(1, width)],
        [like(step * len(pieces), width), like(1, width, dtype=FULL)],
        "stack_pieces",
        *pieces,
    )


def column_parts(width, count):
    return [slice(at * width // count, (at + 1) * width // count) for at in range(count)]


def hidden_kernel(normed_ref, *refs):
    *weight_refs, bias_ref, activated_ref, slope_ref = refs
    for weight_ref, here in zip(weight_refs, column_parts(bias_ref.shape[1], len(weight_refs))):
        pre_gelu = matmul(normed_ref[...], weight_ref[...], 1, 0) + bias_ref[:, here]
        value, slope = gelu_both(pre_gelu)
        activated_ref[:, here] = value.astype(LOW)
        slope_ref[:, here] = slope.astype(LOW)


def hidden_forward(normed, weights, bias):
    rows, columns, step = normed.shape[0], bias.shape[1], 512
    return run_kernel(
        hidden_kernel,
        rows // step,
        [row_blocks(normed.shape[1], step), *whole(*weights, bias)],
        [row_blocks(columns, step)] * 2,
        [like(rows, columns)] * 2,
        "hidden_forward",
        normed,
        *weights,
        bias,
    )


def hidden_back_kernel(grad_ref, *refs):
    *weight_refs, slope_ref, pre_grad_ref, sums_ref = refs

    @pl.when(pl.program_id(0) == 0)
    def _():
        sums_ref[...] = jnp.zeros_like(sums_ref)

    for weight_ref, here in zip(weight_refs, column_parts(slope_ref.shape[1], len(weight_refs))):
        pre_grad = matmul(grad_ref[...], weight_ref[...], 1, 0) * slope_ref[:, here].astype(FULL)
        pre_grad_ref[:, here] = pre_grad.astype(LOW)
        sums_ref[:, here] += jnp.sum(pre_grad, axis=0, keepdims=True)


def hidden_back(grad, weights, slope):
    rows, columns, step = grad.shape[0], slope.shape[1], 512
    return run_kernel(
        hidden_back_kernel,
        rows // step,
        [row_blocks(grad.shape[1], step), *whole(*weights), row_blocks(columns, step)],
        [row_blocks(columns, step), resident(1, columns)],
        [like(rows, columns), like(1, columns, dtype=FULL)],
        "hidden_back",
        grad,
        *weights,
        slope,
    )


def heads_kernel(normed_ref, grad_ref, left_ref, right_ref, bias_ref, projected_ref, back_ref):
    columns = left_ref.shape[1]
    split = projected_ref.shape[1] - columns
    projected_ref[:, :columns] = (
        matmul(normed_ref[...], left_ref[...], 1, 0) + bias_ref[:, :columns]
    )
    projected_ref[:, columns:] = (
        matmul(normed_ref[...], right_ref[:, :split], 1, 0) + bias_ref[:, columns:]
    )
    back_ref[...] = matmul(grad_ref[...], right_ref[:, split:], 1, 0).astype(LOW)


def heads_inputs(normed, grad, weights, bias):
    rows, split, step = normed.shape[0], bias.shape[1], 512
    columns = sum(weight.shape[1] for weight in weights) - split
    return run_kernel(
        heads_kernel,
        rows // step,
        [
            row_blocks(normed.shape[1], step),
            row_blocks(grad.shape[1], step),
            *whole(*weights, bias),
        ],
        [row_blocks(split, step), row_blocks(columns, step)],
        [like(rows, split, dtype=FULL), like(rows, columns)],
        "heads_inputs",
        normed,
        grad,
        *weights,
        bias,
    )


def products_of(lefts, rights):
    values = [matmul(left[...], right[...], 0, 0).astype(LOW) for left, right in zip(lefts, rights)]
    return values[0] if len(values) == 1 else jnp.concatenate(values, axis=1)


def weight_grad_kernel(count, x_ref, *refs):
    lefts, rights, outs = refs[:count], refs[count : 2 * count], refs[2 * count :]
    value = products_of(lefts, rights)
    columns = outs[0].shape[1]
    for first, targets in ((True, outs[:2]), (False, outs[2:])):

        @pl.when((pl.program_id(0) < 4) == first)
        def _(targets=targets):
            for which, target in enumerate(targets):
                target[...] = value[:, which * columns : (which + 1) * columns]


def weight_grad(x_at, *products):
    lefts, rights = zip(*products)
    tokens, width = lefts[0].shape
    columns, step = sum(right.shape[1] for right in rights) // 2, width // 8

    def rows_of(i, x_ref):
        return (0, (i % 4) * 2 + jnp.where(i < 4, 1 - x_ref[0], x_ref[0]))

    return run_kernel(
        functools.partial(weight_grad_kernel, len(products)),
        8,
        [pl.BlockSpec((tokens, step), rows_of)] * len(products) + whole(*rights),
        [pl.BlockSpec((step, columns), lambda i, *_: (jnp.minimum(i, 3), 0))] * 2
        + [pl.BlockSpec((step, columns), lambda i, *_: (jnp.maximum(i - 4, 0), 0))] * 2,
        [like(width // 2, columns)] * 4,
        "weight_grad",
        *lefts,
        *rights,
        scalars=[x_at],
    )


def weight_grad_plain_kernel(count, *refs):
    lefts, rights, outs = refs[:count], refs[count : 2 * count], refs[2 * count :]
    value = products_of(lefts, rights)
    for out_ref, here in zip(outs, column_parts(value.shape[1], 2)):
        out_ref[...] = value[:, here]


def weight_grad_plain(*products):
    lefts, rights = zip(*products)
    tokens, width = lefts[0].shape
    columns, step = sum(right.shape[1] for right in rights) // 2, 256
    return run_kernel(
        functools.partial(weight_grad_plain_kernel, len(products)),
        width // step,
        [pl.BlockSpec((tokens, step), lambda i, *_: (0, i))] * len(products) + whole(*rights),
        [row_blocks(columns, step)] * 2,
        [like(width, columns)] * 2,
        "weight_grad",
        *lefts,
        *rights,
    )


def fold_kernel(at_ref, kept_ref, got_ref, mine_ref, given_ref):
    rows = mine_ref.shape[0]
    for target, at in ((mine_ref, at_ref[0]), (given_ref, 1 - at_ref[0])):
        here = pl.ds(pl.multiple_of(at * rows, rows), rows)
        target[...] = (kept_ref[here, :].astype(FULL) + got_ref[here, :].astype(FULL)).astype(LOW)


def fold(at, kept, got):
    out = like(kept.shape[0] // 2, kept.shape[1])
    return run_kernel(
        fold_kernel, 1, whole(kept, got), whole(out, out), [out, out], "fold", kept, got, scalars=[at]
    )


def final_kernel(low_ref, *refs):
    *pairs, out_ref = refs
    columns = pairs[0].shape[1]
    for which in (0, 1):
        for source, at in ((pairs[2 * which], low_ref[0]), (pairs[2 * which + 1], 1 - low_ref[0])):
            begin = pl.multiple_of((2 * at + which) * columns, columns)
            out_ref[:, pl.ds(begin, columns)] = source[...].astype(FULL)


def final_grad(low_at, *pairs):
    out = like(pairs[0].shape[0], 4 * pairs[0].shape[1], dtype=FULL)
    return run_kernel(
        final_kernel,
        1,
        whole(*pairs),
        resident(*out.shape),
        out,
        "final_grad",
        *pairs,
        scalars=[low_at],
        room=58,
    )


def final_heads_kernel(low_ref, *refs):
    pairs, (qkv_ref, dense_ref) = refs[:4], refs[4:]
    pair = 2 * HEAD
    half = dense_ref.shape[1] // 2
    for own, at in ((0, low_ref[0]), (1, 1 - low_ref[0])):
        source = jnp.concatenate([pairs[own][...], pairs[2 + own][...]], axis=1).astype(FULL)
        for which in range(half // pair):
            columns = pl.ds(pl.multiple_of(at * half + which * pair, pair), pair)
            for part in range(3):
                begin = (3 * which + part) * pair
                qkv_ref[part, :, columns] = source[:, begin : begin + pair]
        dense_ref[:, pl.ds(pl.multiple_of(at * half, half), half)] = source[:, 3 * half :]


def final_heads(low_at, *pairs):
    rows, columns = pairs[0].shape
    outs = [like(3, rows, columns, dtype=FULL), like(rows, columns, dtype=FULL)]
    return run_kernel(
        final_heads_kernel,
        1,
        whole(*pairs),
        whole(*outs),
        outs,
        "final_heads",
        *pairs,
        scalars=[low_at],
        room=58,
    )


def sum_of_products(left_refs, right_refs, terms):
    total = None
    for left_at, left_columns, right_at, right_columns in terms:
        product = matmul(left_refs[left_at][:, left_columns], right_refs[right_at][:, right_columns], 1, 1)
        total = product if total is None else total + product
    return total


def branch_kernel(counts, terms, *refs):
    lefts, rights = refs[: counts[0]], refs[counts[0] : sum(counts)]
    refs[-1][...] = sum_of_products(lefts, rights, terms).astype(LOW)


def token_grad_kernel(counts, terms, *refs):
    lefts, rights = refs[: counts[0]], refs[counts[0] : sum(counts)]
    pieces, (mean_ref, inv_std_ref, out_ref, sums_ref) = refs[sum(counts) : -4], refs[-4:]
    grad = sum_of_products(lefts, rights, terms)
    out_ref[...] = grad.astype(LOW)
    sums_ref[1:2, :] = jnp.sum(grad, axis=0, keepdims=True)
    step = pieces[0].shape[0]
    total = None
    for at, piece in enumerate(pieces):
        rows = slice(at * step, (at + 1) * step)
        x_hat = (piece[...].astype(FULL) - mean_ref[rows, :]) * inv_std_ref[rows, :]
        part = jnp.sum(grad[rows, :] * x_hat, axis=0, keepdims=True)
        total = part if total is None else total + part
    sums_ref[0:1, :] = total


def branch_rows(far, lefts, rights, terms):
    rows, width, step = lefts[0].shape[0] // 2, rights[0].shape[0], 256
    blocks = rows // step
    return run_kernel(
        functools.partial(branch_kernel, (len(lefts), len(rights)), terms),
        blocks,
        [
            pl.BlockSpec((step, left.shape[1]), lambda i, *_: (i + blocks * far, 0))
            for left in lefts
        ]
        + whole(*rights),
        row_blocks(width, step),
        like(rows, width),
        "branch",
        *lefts,
        *rights,
    )


def token_grad(far, lefts, rights, terms, pieces, row_stats):
    rows, width = lefts[0].shape[0] // 2, rights[0].shape[0]
    step = 256
    pieces = pieces[4 * far : 4 * far + 4]

    def kept(columns):
        return pl.BlockSpec((rows, columns), lambda i, *_: (far, 0), pipeline_mode=pl.Buffered(1))

    def along_width(height):
        return pl.BlockSpec((height, step), lambda i, *_: (0, i))

    return run_kernel(
        functools.partial(token_grad_kernel, (len(lefts), len(rights)), terms),
        width // step,
        [kept(left.shape[1]) for left in lefts]
        + [row_blocks(right.shape[1], step) for right in rights]
        + [along_width(piece.shape[0]) for piece in pieces]
        + [kept(1) for _ in row_stats],
        [along_width(rows), along_width(2)],
        [like(rows, width), like(2, width, dtype=FULL)],
        "token_grad",
        *lefts,
        *rights,
        *pieces,
        *row_stats,
    )


def to_links(held, left_ref, left_given_ref, right_ref, right_given_ref):
    columns = left_ref.shape[1]

    for at in range(4):

        @pl.when(pl.program_id(0) == at)
        def _(y=at // 2, low=at % 2):
            left = left_given_ref if y else left_ref
            left[...] = held[:, :columns]
            right = right_given_ref if low else right_ref
            right[...] = held[:, columns:]


def links(step, width, sixteenths):
    columns = width * sixteenths // 16
    specs = [
        pl.BlockSpec((step, columns), lambda i, *_: (jnp.minimum(i, 1), 0)),
        pl.BlockSpec((step, columns), lambda i, *_: (jnp.maximum(i - 2, 0), 0)),
        pl.BlockSpec((step, width - columns), lambda i, *_: (i // 2, 0)),
        pl.BlockSpec((step, width - columns), lambda i, *_: (i // 2, 0)),
    ]
    return specs, [like(2 * step, columns)] * 2 + [like(2 * step, width - columns)] * 2


def link_kernel(kept_ref, got_ref, *outs):
    to_links((kept_ref[...].astype(FULL) + got_ref[...].astype(FULL)).astype(LOW), *outs)


def link_stage(kept, got, sixteenths):
    rows, width = kept.shape
    specs, outs = links(rows // 4, width, sixteenths)
    return run_kernel(
        link_kernel,
        4,
        [row_blocks(width, rows // 4)] * 2,
        specs,
        outs,
        "link_stage",
        kept,
        got,
    )


def last_kernel(left_ref, left_got_ref, right_ref, right_got_ref, *outs):
    rows = outs[0].shape[0]
    pairs = ((left_ref, left_got_ref), (right_ref, right_got_ref))
    for at, (kept_ref, got_ref) in enumerate(pairs):
        total = (kept_ref[...].astype(FULL) + got_ref[...].astype(FULL)).astype(LOW)
        outs[2 * at][...] = total[:rows]
        outs[2 * at + 1][...] = total[rows:]


def last_stage(*values):
    outs = [like(value.shape[0] // 2, value.shape[1]) for value in values]
    return run_kernel(last_kernel, 1, whole(*values), whole(*outs), outs, "last_stage", *values)


def joined(refs):
    left, left_got, right, right_got = (ref[...].astype(FULL) for ref in refs)
    return jnp.concatenate([left + left_got, right + right_got], axis=1)


def output_kernel(*refs):
    tokens_ref, dense_bias_ref, fc2_bias_ref, output_ref = refs[4:]
    total = tokens_ref[...].astype(FULL) + joined(refs[:4])
    output_ref[...] = (total + dense_bias_ref[...] + fc2_bias_ref[...]).astype(LOW)


def input_grad_kernel(*refs):
    tokens_ref, out_grad_ref, gain_ref, grad_ref = refs[4:]
    x_hat, inv_std = normalize_rows(tokens_ref[...])
    scaled = joined(refs[:4]) * gain_ref[...]
    token_grad = inv_std * (
        scaled
        - jnp.mean(scaled, axis=-1, keepdims=True)
        - x_hat * jnp.mean(scaled * x_hat, axis=-1, keepdims=True)
    )
    grad_ref[...] = (out_grad_ref[...].astype(FULL) + token_grad).astype(LOW)


def row_result(kernel, name, *operands):
    out = like(*operands[4].shape)
    return run_kernel(
        kernel, 1, whole(*operands), resident(*out.shape), out, name, *operands, room=58
    )


def body(
    tokens,
    out_grad,
    segments,
    ln_gain,
    ln_bias,
    qkv_weight,
    qkv_bias,
    dense_weight,
    dense_bias,
    fc1_weight,
    fc1_bias,
    fc2_weight,
    fc2_bias,
):
    low_at, high_at, x_at = lax.axis_index("zl"), lax.axis_index("zh"), lax.axis_index("x")
    t_at = lax.axis_index("t")
    pairwise = lax.axis_size("zh") == 2
    place = jnp.stack([t_at // 2, t_at % 2]).astype(jnp.int32)
    weight_rows = qkv_weight.shape[0]
    pair = 2 * HEAD
    half = dense_weight.shape[1] // 2
    pairs = half // pair
    hidden = fc1_weight.shape[1] // 2

    before = [()]

    def sync(*values):
        before[0] = lax.optimization_barrier((values, before[0]))[0]
        return before[0]

    def to_low(value):
        return swap(value, "zl", 1)

    def to_high(value):
        return swap(value, "zh", 1)

    def to_x(value):
        return swap(value, "x", 1)

    def to_y(value):
        return swap(value, "t", 2)

    def to_core(value):
        return swap(value, "t", 1)

    class Gather:
        def __init__(self, shard):
            self.own = shard
            self.moving = []

        def start(self):
            if pairwise:
                self.moving = [to_high(self.own), to_x(self.own)]
            else:
                rows, columns = self.own.shape
                gathered = lax.all_gather(self.own, ("zh", "x"), axis=0, tiled=True)
                natural = gathered.reshape(-1, 2, 2, rows // 2, columns).transpose(0, 2, 1, 3, 4)
                self.moving = [natural.reshape(-1, columns)]

        def forward(self):
            if pairwise:
                self.high, self.x = self.moving
                self.moving = [to_x(self.high)]

        def whole(self):
            if pairwise:
                return place_pieces(high_at, x_at, self.own, self.x, self.high, self.moving[0])
            return self.moving[0]

    class Sum:
        def __init__(self, given, kept):
            self.given, self.kept = given, kept
            self.moving = []

        def start(self):
            if pairwise:
                self.moving = [to_x(self.given)]
            else:
                rows, columns = self.given.shape
                blocks = self.given.reshape(-1, 2, 2, weight_rows, columns)
                ordered = blocks.transpose(0, 2, 1, 3, 4).reshape(rows, columns)
                self.moving = [
                    lax.psum_scatter(
                        ordered.astype(FULL), ("zh", "x"), scatter_dimension=0, tiled=True
                    )
                ]

        def second(self):
            if pairwise:
                self.kept, given = fold(high_at, self.kept, self.moving[0])
                self.moving = [to_high(given)]

        def third(self):
            other = self.kept if pairwise else jnp.zeros_like(self.moving[0])
            self.kept, given = fold(low_at, other, self.moving[0])
            self.moving = [to_low(given)]

        def halves(self):
            return [self.kept, self.moving[0]]

    def segment(values, *transfers):
        tied = sync(*values, *[piece for transfer in transfers for piece in transfer.moving])
        at = len(values)
        for transfer in transfers:
            many = len(transfer.moving)
            transfer.moving = list(tied[at : at + many])
            at += many
        return tied[: len(values)]

    def gathers_of(mine, got):
        return [Gather(shard) for shard in sync(*shards_of(low_at, mine, got))]

    def sums_of(*products):
        if pairwise:
            given_a, given_b, kept_a, kept_b = weight_grad(x_at, *products)
        else:
            given_a, given_b = weight_grad_plain(*products)
            kept_a = kept_b = given_a
        return [given_a, given_b, kept_a, kept_b]

    def as_sums(tied):
        return [Sum(tied[0], tied[2]), Sum(tied[1], tied[3])]

    (fc1_mine,), (fc1_given,) = halves_of(low_at, fc1_weight)
    fc1_given, tokens, out_grad, segments, qkv_weight, dense_weight, fc2_weight = sync(
        fc1_given, tokens, out_grad, segments, qkv_weight, dense_weight, fc2_weight
    )
    got = to_low(fc1_given)
    tokens_core, grad_core = to_core(tokens), to_core(out_grad)
    heads_mine, heads_given = heads_halves(low_at, qkv_weight, dense_weight)
    (fc2_mine,), (fc2_given,) = halves_of(low_at, fc2_weight)
    got, tokens_core, grad_core, heads_given, fc2_given, tokens, out_grad, segments = sync(
        got, tokens_core, grad_core, heads_given, fc2_given, tokens, out_grad, segments
    )
    fc1_a, fc1_b = gathers_of(fc1_mine, got)
    tokens, out_grad, segments, heads_given, fc2_given = sync(
        tokens, out_grad, segments, heads_given, fc2_given
    )
    fc1_a.start()
    tokens_low, tokens_y, segments_low = to_low(tokens), to_y(tokens), to_low(segments)
    tokens_low, tokens_y, segments_low, heads_given, fc1_b.own, fc2_given, out_grad = segment(
        [tokens_low, tokens_y, segments_low, heads_given, fc1_b.own, fc2_given, out_grad], fc1_a
    )
    fc1_a.forward()
    fc1_b.start()
    tokens_both, got = to_y(tokens_low), to_low(heads_given)
    all_segments = jnp.concatenate([segments, segments_low])
    starts = jnp.sum(
        (all_segments[:, None, :] < all_segments[:, :, None]).astype(jnp.int32), axis=2
    )
    tokens_both, got, starts, fc2_given, out_grad, tokens_low, tokens_y = segment(
        [tokens_both, got, starts, fc2_given, out_grad, tokens_low, tokens_y], fc1_a, fc1_b
    )
    tokens_low_core, tokens_y_core = to_core(tokens_low), to_core(tokens_y)
    tokens_both_core = to_core(tokens_both)
    shards = shards_of(low_at, heads_mine, got)
    tokens_low_core, tokens_y_core, tokens_both_core, fc2_given, out_grad, *shards = sync(
        tokens_low_core, tokens_y_core, tokens_both_core, fc2_given, out_grad, *shards
    )
    heads_a, heads_b = (Gather(shard) for shard in shards)
    fc1_b.forward()
    heads_a.start()
    grad_low, grad_y = to_low(out_grad), to_y(out_grad)
    token_pieces = [
        tokens,
        tokens_low,
        tokens_y,
        tokens_both,
        tokens_core,
        tokens_low_core,
        tokens_y_core,
        tokens_both_core,
    ]
    all_normed, *row_stats = normalize_all(token_pieces, ln_gain[None], ln_bias[None])
    fc1_full = [fc1_a.whole()]
    all_normed, fc1_full[0], grad_low, grad_y, heads_b.own, fc2_given = segment(
        [all_normed, fc1_full[0], grad_low, grad_y, heads_b.own, fc2_given], fc1_b, heads_a
    )
    heads_a.forward()
    heads_b.start()
    grad_both, got = to_y(grad_low), to_low(fc2_given)
    fc1_full.append(fc1_b.whole())
    bias = lax.dynamic_slice_in_dim(fc1_bias, low_at * hidden, hidden, 0)[None]
    activated, slope = hidden_forward(all_normed, fc1_full, bias)
    activated, slope, grad_both, got, grad_low, grad_y = segment(
        [activated, slope, grad_both, got, grad_low, grad_y], heads_a, heads_b
    )
    grad_low_core, grad_y_core = to_core(grad_low), to_core(grad_y)
    grad_both_core = to_core(grad_both)
    heads_full = [heads_a.whole()]
    heads_full[0], grad_low_core, grad_y_core, grad_both_core, *shards = sync(
        heads_full[0],
        grad_low_core,
        grad_y_core,
        grad_both_core,
        *shards_of(low_at, fc2_mine, got),
    )
    fc2_a, fc2_b = (Gather(shard) for shard in shards)
    heads_b.forward()
    fc2_a.start()
    all_grad, grad_sums = stack_pieces(
        [
            out_grad,
            grad_low,
            grad_y,
            grad_both,
            grad_core,
            grad_low_core,
            grad_y_core,
            grad_both_core,
        ]
    )
    all_grad, *partials, fc2_b.own = segment(
        [all_grad, *sums_of((all_grad, activated)), fc2_b.own], heads_b, fc2_a
    )
    d_fc2_a, d_fc2_b = as_sums(partials)
    fc2_a.forward()
    fc2_b.start()
    heads_full.append(heads_b.whole())
    bias = lax.dynamic_slice_in_dim(qkv_bias, low_at * half, half, 1)
    bias = bias.reshape(3, pairs, pair).transpose(1, 0, 2).reshape(1, 3 * half)
    projected, back = heads_inputs(all_normed, all_grad, heads_full, bias)
    projected, back, d_fc2_a.given, d_fc2_b.given = segment(
        [projected, back, d_fc2_a.given, d_fc2_b.given], fc2_a, fc2_b
    )
    fc2_b.forward()
    d_fc2_a.start()
    attended, qkv_grad, qkv_sums = attention(projected, back, starts, place)
    fc2_full = [fc2_a.whole()]
    attended, qkv_grad, qkv_sums, fc2_full[0], d_fc2_b.given = segment(
        [attended, qkv_grad, qkv_sums, fc2_full[0], d_fc2_b.given], fc2_b, d_fc2_a
    )
    d_fc2_b.start()
    d_fc2_a.second()
    fc2_full.append(fc2_b.whole())
    columns = heads_full[0].shape[1]
    first, second = slice(0, columns), slice(columns, 2 * columns)
    qkv_end = 3 * half - columns
    everything = slice(None)
    branch_products = (
        [attended, activated],
        [heads_full[1], *fc2_full],
        [
            (0, everything, 0, slice(qkv_end, columns)),
            (1, first, 1, everything),
            (1, second, 2, everything),
        ],
    )
    far, *partials = segment(
        [
            branch_rows(1, *branch_products),
            *sums_of((all_normed, qkv_grad), (all_grad, attended)),
        ],
        d_fc2_a,
        d_fc2_b,
    )
    d_heads_a, d_heads_b = as_sums(partials)
    d_heads_a.start()
    d_fc2_b.second()
    d_fc2_a.third()
    branch_got = to_core(far)
    branch_kept = branch_rows(0, *branch_products)
    pre_grad, pre_sums = hidden_back(all_grad, fc2_full, slope)
    branch_got, branch_kept, pre_grad, pre_sums, d_heads_b.given = segment(
        [branch_got, branch_kept, pre_grad, pre_sums, d_heads_b.given],
        d_heads_a,
        d_fc2_a,
        d_fc2_b,
    )
    d_heads_b.start()
    d_heads_a.second()
    d_fc2_b.third()
    left, left_given, right, right_given = link_stage(branch_kept, branch_got, 11)
    branch_state = [left, to_y(left_given), right, to_low(right_given)]
    grad_products = (
        [qkv_grad, pre_grad],
        [*heads_full, *fc1_full],
        [
            (0, first, 0, everything),
            (0, slice(columns, 3 * half), 1, slice(0, qkv_end)),
            (1, first, 2, everything),
            (1, second, 3, everything),
        ],
        token_pieces,
        row_stats,
    )
    far, far_sums, given_a, given_b, kept_a, kept_b, *branch_state = segment(
        [*token_grad(1, *grad_products), *sums_of((all_normed, pre_grad)), *branch_state],
        d_heads_a,
        d_heads_b,
        d_fc2_b,
    )
    d_fc1_a, d_fc1_b = as_sums([given_a, given_b, kept_a, kept_b])
    d_fc1_a.start()
    d_heads_b.second()
    got = to_core(far)
    left, left_given, right, right_given = last_stage(*branch_state)
    branch_state = [left, to_low(left_given), right, to_y(right_given)]
    kept, near_sums = token_grad(0, *grad_products)
    got, kept, near_sums, d_fc1_b.given, *branch_state = segment(
        [got, kept, near_sums, d_fc1_b.given, *branch_state], d_fc1_a, d_heads_a, d_heads_b
    )
    d_fc1_b.start()
    d_fc1_a.second()
    left, left_given, right, right_given = link_stage(kept, got, 10)
    grad_state = [left, to_y(left_given), right, to_low(right_given)]
    output = row_result(
        output_kernel, "output", *branch_state, tokens, dense_bias[None], fc2_bias[None]
    )
    fc2_weight_grad = final_grad(low_at, *d_fc2_a.halves(), *d_fc2_b.halves())
    sums = (near_sums + far_sums).reshape(2 * D)
    sums_got = to_core(sums)
    here = jnp.concatenate([jnp.sum(qkv_sums, axis=(0, 1)), pre_sums[0]])
    output, fc2_weight_grad, sums, sums_got, here, *grad_state = segment(
        [output, fc2_weight_grad, sums, sums_got, here, *grad_state],
        d_fc1_a,
        d_fc1_b,
        d_heads_a,
        d_heads_b,
    )
    d_fc1_b.second()
    d_heads_a.third()
    left, left_given, right, right_given = last_stage(*grad_state)
    grad_state = [left, to_low(left_given), right, to_y(right_given)]
    sums = sums + sums_got
    sums_got = to_y(sums)
    sums, sums_got, here, *grad_state = segment(
        [sums, sums_got, here, *grad_state], d_fc1_a, d_fc1_b, d_heads_a, d_heads_b
    )
    d_fc1_a.third()
    d_fc1_b.third()
    d_heads_b.third()
    packed = jnp.concatenate([sums + sums_got, here])
    packed_got = to_low(packed)
    input_grad = row_result(
        input_grad_kernel, "input_grad", *grad_state, tokens, out_grad, ln_gain[None]
    )
    input_grad, packed, packed_got = segment(
        [input_grad, packed, packed_got], d_fc1_a, d_fc1_b, d_heads_b
    )
    sums = jnp.concatenate(
        [packed[: 2 * D] + packed_got[: 2 * D], grad_sums[0], packed[2 * D :], packed_got[2 * D :]]
    )
    if pairwise:
        sums_got = [to_high(sums), to_x(sums), swap_both(sums, "zh", 1, "x", 1)]
    else:
        sums_got = [lax.psum(sums, ("zh", "x")) - sums]
    qkv_weight_grad, dense_weight_grad = final_heads(
        low_at, *d_heads_a.halves(), *d_heads_b.halves()
    )
    fc1_weight_grad = final_grad(low_at, *d_fc1_a.halves(), *d_fc1_b.halves())
    qkv_weight_grad, dense_weight_grad, fc1_weight_grad, sums, *sums_got = sync(
        qkv_weight_grad, dense_weight_grad, fc1_weight_grad, sums, *sums_got
    )
    sums = sum(sums_got, sums)
    both = sums[3 * D :].reshape(2, here.shape[0])
    both = jnp.where(low_at == 0, both, both[::-1])
    qkv_bias_grad = (
        both[:, : 3 * half].reshape(2, pairs, 3, pair).transpose(2, 0, 1, 3).reshape(3, 2 * half)
    )
    return (
        output,
        input_grad,
        sums[:D],
        sums[D : 2 * D],
        qkv_weight_grad.transpose(1, 0, 2),
        qkv_bias_grad,
        dense_weight_grad,
        sums[2 * D : 3 * D],
        fc1_weight_grad,
        both[:, 3 * half :].reshape(2 * hidden),
        fc2_weight_grad,
        sums[2 * D : 3 * D],
    )


def solution(mesh):
    dp, tensor = mesh.shape["dp"], mesh.shape["tensor"]
    rows = ("zh", "zl", "x")
    everywhere = (*rows, "t")
    split = Mesh(np.asarray(mesh.devices).reshape(dp // 4, 2, 2, tensor), everywhere)
    return jax.shard_map(
        body,
        mesh=split,
        in_specs=(
            P(everywhere, None),
            P(everywhere, None),
            P(rows, None),
            P(),
            P(),
            P(rows, None, "t"),
            P(None, "t"),
            P(rows, "t"),
            P(),
            P(rows, "t"),
            P("t"),
            P(rows, "t"),
            P(),
        ),
        out_specs=(
            P(everywhere, None),
            P(everywhere, None),
            P(),
            P(),
            P(rows, None, "t"),
            P(None, "t"),
            P(rows, "t"),
            P(),
            P(rows, "t"),
            P("t"),
            P(rows, "t"),
            P(),
        ),
        check_vma=False,
    )
```

```python
import functools
import math

import jax
import jax.numpy as jnp
import numpy as np
from jax import lax
from jax.experimental import pallas as pl
from jax.experimental.pallas import tpu as pltpu
from jax.sharding import Mesh
from jax.sharding import PartitionSpec as P

D = 2048
H = 32
ROT = 32
LEN = 1024
LONGEST = LEN // 3
HEAD = D // H
QB = 128
BACK = -(-(LONGEST - 1) // QB)

EPSILON = 1e-05
GELU_SCALE = math.sqrt(2.0 / math.pi)
GELU_CUBIC = 0.044715
MASK_VALUE = -1e30
ROPE_BASE = 10000.0
LOW = jnp.bfloat16
FULL = jnp.float32


def gelu_both(pre_gelu):
    square = pre_gelu * pre_gelu
    tangent = jnp.tanh(GELU_SCALE * pre_gelu * (1.0 + GELU_CUBIC * square))
    value = 0.5 * pre_gelu * (1.0 + tangent)
    slope = 0.5 * (1.0 + tangent) + 0.5 * pre_gelu * (1.0 - tangent * tangent) * GELU_SCALE * (
        1.0 + 3.0 * GELU_CUBIC * square
    )
    return value, slope


def rotary_lanes():
    half = ROT // 2
    inverse = ROPE_BASE ** (-(2.0 * np.arange(half)) / ROT)
    angles = np.arange(LEN)[:, None] * inverse[None, :]
    rest = np.zeros((LEN, HEAD - ROT))
    cosine = np.concatenate([np.cos(angles), np.cos(angles), rest + 1.0], axis=1)
    sine = np.concatenate([-np.sin(angles), np.sin(angles), rest], axis=1)
    return tuple(jnp.asarray(np.tile(table, (1, 2)), FULL) for table in (cosine, sine))


def matmul(left, right, left_dim, right_dim):
    return lax.dot_general(
        left, right, (((left_dim,), (right_dim,)), ((), ())), preferred_element_type=FULL
    )


def attention_kernel(
    place_ref, proj_ref, grad_ref, start_ref, cos_ref, sin_ref, att_ref, dqkv_ref, sums_ref,
    q_st, g_st, k_low, v_low, k_turn, v_turn, dk_sum, dv_sum, dq_sum,
):
    pair = 2 * HEAD
    scale = 1.0 / math.sqrt(HEAD)
    part_rows = proj_ref.shape[3]
    parts = LEN // part_rows
    lane = lax.broadcasted_iota(jnp.int32, (part_rows, pair), 1)
    first = lane < HEAD
    near = lane % HEAD < ROT // 2
    y_at, core_at = place_ref[0], place_ref[1]

    def where_is(part):
        return (part % 2) ^ core_at, (part // 2) ^ y_at

    def partner(x):
        return jnp.where(near, pltpu.roll(x, pair - ROT // 2, 1), pltpu.roll(x, ROT // 2, 1))

    per_part = part_rows // QB
    for part in range(parts):
        core, y = where_is(part)
        rows = slice(part * part_rows, (part + 1) * part_rows)
        cosine, sine = cos_ref[rows, :], sin_ref[rows, :]
        projected = proj_ref[core, y, 0]
        q = projected[:, 0:pair]
        k = projected[:, pair : 2 * pair]
        v = projected[:, 2 * pair : 3 * pair]
        q = (q * cosine + partner(q) * sine) * scale
        k = k * cosine + partner(k) * sine
        g = grad_ref[core, y, 0].astype(FULL)
        zero = jnp.zeros_like(q)
        for stacked, whole in ((q_st, q), (g_st, g)):
            for head, own in enumerate(
                (jnp.where(first, whole, zero), jnp.where(first, zero, whole))
            ):
                stacked[
                    part * per_part : (part + 1) * per_part, head * QB : (head + 1) * QB, :
                ] = own.astype(LOW).reshape(per_part, QB, pair)
        k_low[rows, :] = k.astype(LOW)
        v_low[rows, :] = v.astype(LOW)
        k_turn[:, rows] = k.T.astype(LOW)
        v_turn[:, rows] = v.T.astype(LOW)
    dk_sum[...] = jnp.zeros_like(dk_sum)
    dv_sum[...] = jnp.zeros_like(dv_sum)
    upper = lax.broadcasted_iota(jnp.int32, (pair, QB), 0) < HEAD
    for block in range(LEN // QB):
        begin = max(0, block - BACK) * QB
        keys = slice(begin, (block + 1) * QB)
        rows = slice(block * QB, (block + 1) * QB)
        width = (block + 1) * QB - begin
        key_at = begin + lax.broadcasted_iota(jnp.int32, (width, QB), 0)
        query_at = block * QB + lax.broadcasted_iota(jnp.int32, (width, QB), 1)
        allowed = (key_at >= start_ref[0, block : block + 1, :]) & (key_at <= query_at)
        allowed = jnp.concatenate([allowed, allowed], axis=1)
        queries, grads = q_st[block], g_st[block]
        scores = jnp.where(allowed, matmul(k_low[keys], queries, 1, 1), MASK_VALUE)
        powers = jnp.exp(scores - jnp.max(scores, axis=0, keepdims=True))
        probs = powers * (1.0 / jnp.sum(powers, axis=0, keepdims=True))
        probs_low = probs.astype(LOW)
        prob_grad = matmul(v_low[keys], grads, 1, 1)
        row_dot = jnp.sum(probs * prob_grad, axis=0, keepdims=True)
        score_grad = (probs * (prob_grad - row_dot)).astype(LOW)
        dv_sum[keys] += matmul(probs_low, grads, 1, 0)
        dk_sum[keys] += matmul(score_grad, queries, 1, 0)
        turned = matmul(v_turn[:, keys], probs_low, 1, 0)
        core, y = where_is(block // per_part)
        here = slice((block % per_part) * QB, (block % per_part + 1) * QB)
        att_ref[core, y, 0, here, :] = jnp.where(upper, turned[:, :QB], turned[:, QB:]).T.astype(LOW)
        turned = matmul(k_turn[:, keys], score_grad, 1, 0)
        dq_sum[rows, :] = jnp.where(upper, turned[:, :QB], turned[:, QB:]).T
    totals = [jnp.zeros((1, pair), FULL)] * 3
    for part in range(parts):
        core, y = where_is(part)
        rows = slice(part * part_rows, (part + 1) * part_rows)
        cosine, sine = cos_ref[rows, :], sin_ref[rows, :]
        dq, dk = dq_sum[rows, :] * scale, dk_sum[rows, :]
        grads = (
            dq * cosine - partner(dq) * sine,
            dk * cosine - partner(dk) * sine,
            dv_sum[rows, :],
        )
        for at, grad in enumerate(grads):
            dqkv_ref[core, y, 0, :, at * pair : (at + 1) * pair] = grad.astype(LOW)
            totals[at] = totals[at] + jnp.sum(grad, axis=0, keepdims=True)
    for at, total in enumerate(totals):
        sums_ref[0, :, at * pair : (at + 1) * pair] = total


def attention(projected, grads, starts, place):
    rows, width = projected.shape
    seqs, pair = rows // LEN, 2 * HEAD
    pairs = width // (3 * pair)
    part_rows = rows // 8
    cosine, sine = rotary_lanes()
    table = pl.BlockSpec((LEN, pair), lambda s, h, place: (0, 0))

    def block(columns):
        return pl.BlockSpec((2, 2, 1, part_rows, columns), lambda s, h, place: (0, 0, s, 0, h))

    def view(columns):
        return (2, 2, seqs, part_rows, columns)

    attended, grad, sums = pl.pallas_call(
        attention_kernel,
        grid_spec=pltpu.PrefetchScalarGridSpec(
            num_scalar_prefetch=1,
            grid=(seqs, pairs),
            in_specs=[
                block(3 * pair),
                block(pair),
                pl.BlockSpec((1, LEN // QB, QB), lambda s, h, place: (s, 0, 0)),
                table,
                table,
            ],
            out_specs=[
                block(pair),
                block(3 * pair),
                pl.BlockSpec((1, 1, 3 * pair), lambda s, h, place: (s, 0, h)),
            ],
            scratch_shapes=[
                pltpu.VMEM((LEN // QB, 2 * QB, pair), LOW),
                pltpu.VMEM((LEN // QB, 2 * QB, pair), LOW),
                pltpu.VMEM((LEN, pair), LOW),
                pltpu.VMEM((LEN, pair), LOW),
                pltpu.VMEM((pair, LEN), LOW),
                pltpu.VMEM((pair, LEN), LOW),
                pltpu.VMEM((LEN, pair), FULL),
                pltpu.VMEM((LEN, pair), FULL),
                pltpu.VMEM((LEN, pair), FULL),
            ],
        ),
        out_shape=[
            jax.ShapeDtypeStruct(view(pairs * pair), LOW),
            jax.ShapeDtypeStruct(view(width), LOW),
            jax.ShapeDtypeStruct((seqs, 1, width), FULL),
        ],
        compiler_params=pltpu.CompilerParams(vmem_limit_bytes=58 << 20),
        cost_estimate=pl.CostEstimate(
            flops=seqs * LEN * QB * (BACK + 1) * pair // 8,
            transcendentals=0,
            bytes_accessed=rows * width // 8,
        ),
        name="attention_both_ways",
    )(
        place,
        projected.reshape(view(width)),
        grads.reshape(view(pairs * pair)),
        starts.reshape(seqs, LEN // QB, QB),
        cosine,
        sine,
    )
    return attended.reshape(rows, pairs * pair), grad.reshape(rows, width), sums


def swap(value, axis, bit):
    return lax.ppermute(value, axis, [(i, i ^ bit) for i in range(lax.axis_size(axis))])


def swap_both(value, axis, bit, other_axis, other_bit):
    inner = lax.axis_size(other_axis)
    pairs = [
        (i, ((i // inner) ^ bit) * inner + ((i % inner) ^ other_bit))
        for i in range(lax.axis_size(axis) * inner)
    ]
    return lax.ppermute(value, (axis, other_axis), pairs)


def normalize_rows(token_rows):
    values = token_rows.astype(FULL)
    centered = values - jnp.mean(values, axis=-1, keepdims=True)
    inv_std = lax.rsqrt(jnp.mean(centered * centered, axis=-1, keepdims=True) + EPSILON)
    return centered * inv_std, inv_std


def row_blocks(columns, rows):
    return pl.BlockSpec((rows, columns), lambda i, *_: (i, 0))


def resident(*shape):
    return pl.BlockSpec(shape, lambda i, *_: (0,) * len(shape), pipeline_mode=pl.Buffered(1))


def like(*shape, dtype=LOW):
    return jax.ShapeDtypeStruct(shape, dtype)


def run_kernel(
    kernel, steps, in_specs, out_specs, out_shape, name, *operands, scalars=(), room=None
):
    if scalars:
        scalars = (jnp.stack([jnp.asarray(scalar, jnp.int32) for scalar in scalars]),)
    return pl.pallas_call(
        kernel,
        grid_spec=pltpu.PrefetchScalarGridSpec(
            num_scalar_prefetch=len(scalars),
            grid=(steps,),
            in_specs=in_specs,
            out_specs=out_specs,
        ),
        out_shape=out_shape,
        compiler_params=pltpu.CompilerParams(vmem_limit_bytes=(room or (52 if steps > 1 else 32)) << 20),
        cost_estimate=pl.CostEstimate(flops=1 << 24, transcendentals=0, bytes_accessed=1 << 18),
        name=name,
    )(*scalars, *operands)


def whole(*values):
    return [resident(*value.shape) for value in values]


def halves_kernel(low_ref, *refs):
    count = len(refs) // 3
    for source, mine, given in zip(refs[:count], refs[count : 2 * count], refs[2 * count :]):
        columns = mine.shape[1]
        for target, at in ((mine, low_ref[0]), (given, 1 - low_ref[0])):
            target[...] = source[:, pl.ds(pl.multiple_of(at * columns, columns), columns)]


def halves_of(low_at, *weights):
    outs = [like(weight.shape[0], weight.shape[1] // 2) for weight in weights] * 2
    found = run_kernel(
        halves_kernel, 1, whole(*weights), whole(*outs), outs, "halves", *weights, scalars=[low_at]
    )
    return found[: len(weights)], found[len(weights) :]


def heads_halves_kernel(low_ref, q_ref, k_ref, v_ref, dense_ref, mine_ref, given_ref):
    pair = 2 * HEAD
    half = dense_ref.shape[1] // 2
    for target, at in ((mine_ref, low_ref[0]), (given_ref, 1 - low_ref[0])):
        for which in range(half // pair):
            columns = pl.ds(pl.multiple_of(at * half + which * pair, pair), pair)
            for part, source in enumerate((q_ref, k_ref, v_ref)):
                begin = (3 * which + part) * pair
                target[:, begin : begin + pair] = source[:, columns]
        target[:, 3 * half :] = dense_ref[:, pl.ds(pl.multiple_of(at * half, half), half)]


def heads_halves(low_at, qkv_weight, dense_weight):
    operands = (*(qkv_weight[:, part] for part in range(3)), dense_weight)
    out = like(dense_weight.shape[0], 2 * dense_weight.shape[1])
    return run_kernel(
        heads_halves_kernel,
        1,
        whole(*operands),
        whole(out, out),
        [out, out],
        "heads_halves",
        *operands,
        scalars=[low_at],
    )


def shard_kernel(low_ref, mine_ref, got_ref, *shard_refs):
    rows, columns = mine_ref.shape[0], shard_refs[0].shape[1]
    for source, at in ((mine_ref, low_ref[0]), (got_ref, 1 - low_ref[0])):
        for which, shard_ref in enumerate(shard_refs):
            here = slice(which * columns, (which + 1) * columns)
            shard_ref[pl.ds(pl.multiple_of(at * rows, rows), rows), :] = source[:, here]


def shards_of(low_at, mine, got):
    out = like(2 * mine.shape[0], mine.shape[1] // 2)
    return run_kernel(
        shard_kernel,
        1,
        whole(mine, got),
        whole(out, out),
        [out, out],
        "shards",
        mine,
        got,
        scalars=[low_at],
    )


def place_kernel(at_ref, *refs):
    *pieces, full = refs
    rows = pieces[0].shape[0] // 2
    for at, piece in enumerate(pieces):
        slot = 4 * (at_ref[0] ^ (at // 2)) + (at_ref[1] ^ (at % 2))
        for low in (0, 1):
            begin = pl.multiple_of((slot + 2 * low) * rows, rows)
            full[pl.ds(begin, rows), :] = piece[low * rows : (low + 1) * rows, :]


def place_pieces(high_at, x_at, *pieces):
    rows, columns = pieces[0].shape
    steps = 4
    block = pl.BlockSpec((rows, columns // steps), lambda i, *_: (0, i))
    return run_kernel(
        place_kernel,
        steps,
        [block] * 4,
        pl.BlockSpec((4 * rows, columns // steps), lambda i, *_: (0, i)),
        like(4 * rows, columns),
        "place_pieces",
        *pieces,
        scalars=[high_at, x_at],
    )


def from_piece(pieces, use):
    for at, piece in enumerate(pieces):

        @pl.when(pl.program_id(0) == at)
        def _(piece=piece):
            use(piece)


def normalize_kernel(*refs):
    *pieces, gain_ref, shift_ref, normed_ref, mean_ref, inv_std_ref = refs

    def use(piece):
        values = piece[...].astype(FULL)
        mean = jnp.mean(values, axis=-1, keepdims=True)
        centered = values - mean
        inv_std = lax.rsqrt(jnp.mean(centered * centered, axis=-1, keepdims=True) + EPSILON)
        normed_ref[...] = (centered * inv_std * gain_ref[...] + shift_ref[...]).astype(LOW)
        mean_ref[...] = mean
        inv_std_ref[...] = inv_std

    from_piece(pieces, use)


def normalize_all(pieces, gain, shift):
    step, width = pieces[0].shape
    return run_kernel(
        normalize_kernel,
        len(pieces),
        whole(*pieces, gain, shift),
        [row_blocks(width, step), row_blocks(1, step), row_blocks(1, step)],
        [like(step * len(pieces), width)] + [like(step * len(pieces), 1, dtype=FULL)] * 2,
        "normalize_all",
        *pieces,
        gain,
        shift,
    )


def stack_kernel(*refs):
    *pieces, whole_ref, sums_ref = refs

    @pl.when(pl.program_id(0) == 0)
    def _():
        sums_ref[...] = jnp.zeros_like(sums_ref)

    def use(piece):
        whole_ref[...] = piece[...]
        sums_ref[...] += jnp.sum(piece[...].astype(FULL), axis=0, keepdims=True)

    from_piece(pieces, use)


def stack_pieces(pieces):
    step, width = pieces[0].shape
    return run_kernel(
        stack_kernel,
        len(pieces),
        whole(*pieces),
        [row_blocks(width, step), resident(1, width)],
        [like(step * len(pieces), width), like(1, width, dtype=FULL)],
        "stack_pieces",
        *pieces,
    )


def column_parts(width, count):
    return [slice(at * width // count, (at + 1) * width // count) for at in range(count)]


def hidden_kernel(normed_ref, *refs):
    *weight_refs, bias_ref, activated_ref, slope_ref = refs
    for weight_ref, here in zip(weight_refs, column_parts(bias_ref.shape[1], len(weight_refs))):
        pre_gelu = matmul(normed_ref[...], weight_ref[...], 1, 0) + bias_ref[:, here]
        value, slope = gelu_both(pre_gelu)
        activated_ref[:, here] = value.astype(LOW)
        slope_ref[:, here] = slope.astype(LOW)


def hidden_forward(normed, weights, bias):
    rows, columns, step = normed.shape[0], bias.shape[1], 512
    return run_kernel(
        hidden_kernel,
        rows // step,
        [row_blocks(normed.shape[1], step), *whole(*weights, bias)],
        [row_blocks(columns, step)] * 2,
        [like(rows, columns)] * 2,
        "hidden_forward",
        normed,
        *weights,
        bias,
    )


def hidden_back_kernel(grad_ref, *refs):
    *weight_refs, slope_ref, pre_grad_ref, sums_ref = refs

    @pl.when(pl.program_id(0) == 0)
    def _():
        sums_ref[...] = jnp.zeros_like(sums_ref)

    for weight_ref, here in zip(weight_refs, column_parts(slope_ref.shape[1], len(weight_refs))):
        pre_grad = matmul(grad_ref[...], weight_ref[...], 1, 0) * slope_ref[:, here].astype(FULL)
        pre_grad_ref[:, here] = pre_grad.astype(LOW)
        sums_ref[:, here] += jnp.sum(pre_grad, axis=0, keepdims=True)


def hidden_back(grad, weights, slope):
    rows, columns, step = grad.shape[0], slope.shape[1], 512
    return run_kernel(
        hidden_back_kernel,
        rows // step,
        [row_blocks(grad.shape[1], step), *whole(*weights), row_blocks(columns, step)],
        [row_blocks(columns, step), resident(1, columns)],
        [like(rows, columns), like(1, columns, dtype=FULL)],
        "hidden_back",
        grad,
        *weights,
        slope,
    )


def heads_kernel(normed_ref, grad_ref, left_ref, right_ref, bias_ref, projected_ref, back_ref):
    columns = left_ref.shape[1]
    split = projected_ref.shape[1] - columns
    projected_ref[:, :columns] = (
        matmul(normed_ref[...], left_ref[...], 1, 0) + bias_ref[:, :columns]
    )
    projected_ref[:, columns:] = (
        matmul(normed_ref[...], right_ref[:, :split], 1, 0) + bias_ref[:, columns:]
    )
    back_ref[...] = matmul(grad_ref[...], right_ref[:, split:], 1, 0).astype(LOW)


def heads_inputs(normed, grad, weights, bias):
    rows, split, step = normed.shape[0], bias.shape[1], 512
    columns = sum(weight.shape[1] for weight in weights) - split
    return run_kernel(
        heads_kernel,
        rows // step,
        [
            row_blocks(normed.shape[1], step),
            row_blocks(grad.shape[1], step),
            *whole(*weights, bias),
        ],
        [row_blocks(split, step), row_blocks(columns, step)],
        [like(rows, split, dtype=FULL), like(rows, columns)],
        "heads_inputs",
        normed,
        grad,
        *weights,
        bias,
    )


def products_of(lefts, rights):
    values = [matmul(left[...], right[...], 0, 0).astype(LOW) for left, right in zip(lefts, rights)]
    return values[0] if len(values) == 1 else jnp.concatenate(values, axis=1)


def weight_grad_kernel(count, x_ref, *refs):
    lefts, rights, outs = refs[:count], refs[count : 2 * count], refs[2 * count :]
    value = products_of(lefts, rights)
    columns = outs[0].shape[1]
    for first, targets in ((True, outs[:2]), (False, outs[2:])):

        @pl.when((pl.program_id(0) < 4) == first)
        def _(targets=targets):
            for which, target in enumerate(targets):
                target[...] = value[:, which * columns : (which + 1) * columns]


def weight_grad(x_at, *products):
    lefts, rights = zip(*products)
    tokens, width = lefts[0].shape
    columns, step = sum(right.shape[1] for right in rights) // 2, width // 8

    def rows_of(i, x_ref):
        return (0, (i % 4) * 2 + jnp.where(i < 4, 1 - x_ref[0], x_ref[0]))

    return run_kernel(
        functools.partial(weight_grad_kernel, len(products)),
        8,
        [pl.BlockSpec((tokens, step), rows_of)] * len(products) + whole(*rights),
        [pl.BlockSpec((step, columns), lambda i, *_: (jnp.minimum(i, 3), 0))] * 2
        + [pl.BlockSpec((step, columns), lambda i, *_: (jnp.maximum(i - 4, 0), 0))] * 2,
        [like(width // 2, columns)] * 4,
        "weight_grad",
        *lefts,
        *rights,
        scalars=[x_at],
    )


def weight_grad_plain_kernel(count, *refs):
    lefts, rights, outs = refs[:count], refs[count : 2 * count], refs[2 * count :]
    value = products_of(lefts, rights)
    for out_ref, here in zip(outs, column_parts(value.shape[1], 2)):
        out_ref[...] = value[:, here]


def weight_grad_plain(*products):
    lefts, rights = zip(*products)
    tokens, width = lefts[0].shape
    columns, step = sum(right.shape[1] for right in rights) // 2, 256
    return run_kernel(
        functools.partial(weight_grad_plain_kernel, len(products)),
        width // step,
        [pl.BlockSpec((tokens, step), lambda i, *_: (0, i))] * len(products) + whole(*rights),
        [row_blocks(columns, step)] * 2,
        [like(width, columns)] * 2,
        "weight_grad",
        *lefts,
        *rights,
    )


def fold_kernel(at_ref, kept_ref, got_ref, mine_ref, given_ref):
    rows = mine_ref.shape[0]
    for target, at in ((mine_ref, at_ref[0]), (given_ref, 1 - at_ref[0])):
        here = pl.ds(pl.multiple_of(at * rows, rows), rows)
        target[...] = (kept_ref[here, :].astype(FULL) + got_ref[here, :].astype(FULL)).astype(LOW)


def fold(at, kept, got):
    out = like(kept.shape[0] // 2, kept.shape[1])
    return run_kernel(
        fold_kernel, 1, whole(kept, got), whole(out, out), [out, out], "fold", kept, got, scalars=[at]
    )


def final_kernel(low_ref, *refs):
    *pairs, out_ref = refs
    columns = pairs[0].shape[1]
    for which in (0, 1):
        for source, at in ((pairs[2 * which], low_ref[0]), (pairs[2 * which + 1], 1 - low_ref[0])):
            begin = pl.multiple_of((2 * at + which) * columns, columns)
            out_ref[:, pl.ds(begin, columns)] = source[...].astype(FULL)


def final_grad(low_at, *pairs):
    out = like(pairs[0].shape[0], 4 * pairs[0].shape[1], dtype=FULL)
    return run_kernel(
        final_kernel,
        1,
        whole(*pairs),
        resident(*out.shape),
        out,
        "final_grad",
        *pairs,
        scalars=[low_at],
        room=58,
    )


def final_heads_kernel(low_ref, *refs):
    pairs, (qkv_ref, dense_ref) = refs[:4], refs[4:]
    pair = 2 * HEAD
    half = dense_ref.shape[1] // 2
    for own, at in ((0, low_ref[0]), (1, 1 - low_ref[0])):
        source = jnp.concatenate([pairs[own][...], pairs[2 + own][...]], axis=1).astype(FULL)
        for which in range(half // pair):
            columns = pl.ds(pl.multiple_of(at * half + which * pair, pair), pair)
            for part in range(3):
                begin = (3 * which + part) * pair
                qkv_ref[part, :, columns] = source[:, begin : begin + pair]
        dense_ref[:, pl.ds(pl.multiple_of(at * half, half), half)] = source[:, 3 * half :]


def final_heads(low_at, *pairs):
    rows, columns = pairs[0].shape
    outs = [like(3, rows, columns, dtype=FULL), like(rows, columns, dtype=FULL)]
    return run_kernel(
        final_heads_kernel,
        1,
        whole(*pairs),
        whole(*outs),
        outs,
        "final_heads",
        *pairs,
        scalars=[low_at],
        room=58,
    )


def sum_of_products(left_refs, right_refs, terms):
    total = None
    for left_at, left_columns, right_at, right_columns in terms:
        product = matmul(left_refs[left_at][:, left_columns], right_refs[right_at][:, right_columns], 1, 1)
        total = product if total is None else total + product
    return total


def branch_kernel(counts, terms, *refs):
    lefts, rights = refs[: counts[0]], refs[counts[0] : sum(counts)]
    refs[-1][...] = sum_of_products(lefts, rights, terms).astype(LOW)


def token_grad_kernel(counts, terms, *refs):
    lefts, rights = refs[: counts[0]], refs[counts[0] : sum(counts)]
    pieces, (mean_ref, inv_std_ref, out_ref, sums_ref) = refs[sum(counts) : -4], refs[-4:]
    grad = sum_of_products(lefts, rights, terms)
    out_ref[...] = grad.astype(LOW)
    sums_ref[1:2, :] = jnp.sum(grad, axis=0, keepdims=True)
    step = pieces[0].shape[0]
    total = None
    for at, piece in enumerate(pieces):
        rows = slice(at * step, (at + 1) * step)
        x_hat = (piece[...].astype(FULL) - mean_ref[rows, :]) * inv_std_ref[rows, :]
        part = jnp.sum(grad[rows, :] * x_hat, axis=0, keepdims=True)
        total = part if total is None else total + part
    sums_ref[0:1, :] = total


def branch_rows(far, lefts, rights, terms):
    rows, width, step = lefts[0].shape[0] // 2, rights[0].shape[0], 256
    blocks = rows // step
    return run_kernel(
        functools.partial(branch_kernel, (len(lefts), len(rights)), terms),
        blocks,
        [
            pl.BlockSpec((step, left.shape[1]), lambda i, *_: (i + blocks * far, 0))
            for left in lefts
        ]
        + whole(*rights),
        row_blocks(width, step),
        like(rows, width),
        "branch",
        *lefts,
        *rights,
    )


def token_grad(far, lefts, rights, terms, pieces, row_stats):
    rows, width = lefts[0].shape[0] // 2, rights[0].shape[0]
    step = 256
    pieces = pieces[4 * far : 4 * far + 4]

    def kept(columns):
        return pl.BlockSpec((rows, columns), lambda i, *_: (far, 0), pipeline_mode=pl.Buffered(1))

    def along_width(height):
        return pl.BlockSpec((height, step), lambda i, *_: (0, i))

    return run_kernel(
        functools.partial(token_grad_kernel, (len(lefts), len(rights)), terms),
        width // step,
        [kept(left.shape[1]) for left in lefts]
        + [row_blocks(right.shape[1], step) for right in rights]
        + [along_width(piece.shape[0]) for piece in pieces]
        + [kept(1) for _ in row_stats],
        [along_width(rows), along_width(2)],
        [like(rows, width), like(2, width, dtype=FULL)],
        "token_grad",
        *lefts,
        *rights,
        *pieces,
        *row_stats,
    )


def to_links(held, left_ref, left_given_ref, right_ref, right_given_ref):
    columns = left_ref.shape[1]

    for at in range(4):

        @pl.when(pl.program_id(0) == at)
        def _(y=at // 2, low=at % 2):
            left = left_given_ref if y else left_ref
            left[...] = held[:, :columns]
            right = right_given_ref if low else right_ref
            right[...] = held[:, columns:]


def links(step, width, sixteenths):
    columns = width * sixteenths // 16
    specs = [
        pl.BlockSpec((step, columns), lambda i, *_: (jnp.minimum(i, 1), 0)),
        pl.BlockSpec((step, columns), lambda i, *_: (jnp.maximum(i - 2, 0), 0)),
        pl.BlockSpec((step, width - columns), lambda i, *_: (i // 2, 0)),
        pl.BlockSpec((step, width - columns), lambda i, *_: (i // 2, 0)),
    ]
    return specs, [like(2 * step, columns)] * 2 + [like(2 * step, width - columns)] * 2


def link_kernel(kept_ref, got_ref, *outs):
    to_links((kept_ref[...].astype(FULL) + got_ref[...].astype(FULL)).astype(LOW), *outs)


def link_stage(kept, got, sixteenths):
    rows, width = kept.shape
    specs, outs = links(rows // 4, width, sixteenths)
    return run_kernel(
        link_kernel,
        4,
        [row_blocks(width, rows // 4)] * 2,
        specs,
        outs,
        "link_stage",
        kept,
        got,
    )


def last_kernel(left_ref, left_got_ref, right_ref, right_got_ref, *outs):
    rows = outs[0].shape[0]
    pairs = ((left_ref, left_got_ref), (right_ref, right_got_ref))
    for at, (kept_ref, got_ref) in enumerate(pairs):
        total = (kept_ref[...].astype(FULL) + got_ref[...].astype(FULL)).astype(LOW)
        outs[2 * at][...] = total[:rows]
        outs[2 * at + 1][...] = total[rows:]


def last_stage(*values):
    outs = [like(value.shape[0] // 2, value.shape[1]) for value in values]
    return run_kernel(last_kernel, 1, whole(*values), whole(*outs), outs, "last_stage", *values)


def joined(refs):
    left, left_got, right, right_got = (ref[...].astype(FULL) for ref in refs)
    return jnp.concatenate([left + left_got, right + right_got], axis=1)


def output_kernel(*refs):
    tokens_ref, dense_bias_ref, fc2_bias_ref, output_ref = refs[4:]
    total = tokens_ref[...].astype(FULL) + joined(refs[:4])
    output_ref[...] = (total + dense_bias_ref[...] + fc2_bias_ref[...]).astype(LOW)


def input_grad_kernel(*refs):
    tokens_ref, out_grad_ref, gain_ref, grad_ref = refs[4:]
    x_hat, inv_std = normalize_rows(tokens_ref[...])
    scaled = joined(refs[:4]) * gain_ref[...]
    token_grad = inv_std * (
        scaled
        - jnp.mean(scaled, axis=-1, keepdims=True)
        - x_hat * jnp.mean(scaled * x_hat, axis=-1, keepdims=True)
    )
    grad_ref[...] = (out_grad_ref[...].astype(FULL) + token_grad).astype(LOW)


def row_result(kernel, name, *operands):
    out = like(*operands[4].shape)
    return run_kernel(
        kernel, 1, whole(*operands), resident(*out.shape), out, name, *operands, room=58
    )


def body(
    tokens,
    out_grad,
    segments,
    ln_gain,
    ln_bias,
    qkv_weight,
    qkv_bias,
    dense_weight,
    dense_bias,
    fc1_weight,
    fc1_bias,
    fc2_weight,
    fc2_bias,
):
    low_at, high_at, x_at = lax.axis_index("zl"), lax.axis_index("zh"), lax.axis_index("x")
    t_at = lax.axis_index("t")
    pairwise = lax.axis_size("zh") == 2
    place = jnp.stack([t_at // 2, t_at % 2]).astype(jnp.int32)
    weight_rows = qkv_weight.shape[0]
    pair = 2 * HEAD
    half = dense_weight.shape[1] // 2
    pairs = half // pair
    hidden = fc1_weight.shape[1] // 2

    before = [()]

    def sync(*values):
        before[0] = lax.optimization_barrier((values, before[0]))[0]
        return before[0]

    def to_low(value):
        return swap(value, "zl", 1)

    def to_high(value):
        return swap(value, "zh", 1)

    def to_x(value):
        return swap(value, "x", 1)

    def to_y(value):
        return swap(value, "t", 2)

    def to_core(value):
        return swap(value, "t", 1)

    class Gather:
        def __init__(self, shard):
            self.own = shard
            self.moving = []

        def start(self):
            if pairwise:
                self.moving = [to_high(self.own), to_x(self.own)]
            else:
                rows, columns = self.own.shape
                gathered = lax.all_gather(self.own, ("zh", "x"), axis=0, tiled=True)
                natural = gathered.reshape(-1, 2, 2, rows // 2, columns).transpose(0, 2, 1, 3, 4)
                self.moving = [natural.reshape(-1, columns)]

        def forward(self):
            if pairwise:
                self.high, self.x = self.moving
                self.moving = [to_x(self.high)]

        def whole(self):
            if pairwise:
                return place_pieces(high_at, x_at, self.own, self.x, self.high, self.moving[0])
            return self.moving[0]

    class Sum:
        def __init__(self, given, kept):
            self.given, self.kept = given, kept
            self.moving = []

        def start(self):
            if pairwise:
                self.moving = [to_x(self.given)]
            else:
                rows, columns = self.given.shape
                blocks = self.given.reshape(-1, 2, 2, weight_rows, columns)
                ordered = blocks.transpose(0, 2, 1, 3, 4).reshape(rows, columns)
                self.moving = [
                    lax.psum_scatter(
                        ordered.astype(FULL), ("zh", "x"), scatter_dimension=0, tiled=True
                    )
                ]

        def second(self):
            if pairwise:
                self.kept, given = fold(high_at, self.kept, self.moving[0])
                self.moving = [to_high(given)]

        def third(self):
            other = self.kept if pairwise else jnp.zeros_like(self.moving[0])
            self.kept, given = fold(low_at, other, self.moving[0])
            self.moving = [to_low(given)]

        def halves(self):
            return [self.kept, self.moving[0]]

    def segment(values, *transfers):
        tied = sync(*values, *[piece for transfer in transfers for piece in transfer.moving])
        at = len(values)
        for transfer in transfers:
            many = len(transfer.moving)
            transfer.moving = list(tied[at : at + many])
            at += many
        return tied[: len(values)]

    def gathers_of(mine, got):
        return [Gather(shard) for shard in sync(*shards_of(low_at, mine, got))]

    def sums_of(*products):
        if pairwise:
            given_a, given_b, kept_a, kept_b = weight_grad(x_at, *products)
        else:
            given_a, given_b = weight_grad_plain(*products)
            kept_a = kept_b = given_a
        return [given_a, given_b, kept_a, kept_b]

    def as_sums(tied):
        return [Sum(tied[0], tied[2]), Sum(tied[1], tied[3])]

    (fc1_mine,), (fc1_given,) = halves_of(low_at, fc1_weight)
    fc1_given, tokens, out_grad, segments, qkv_weight, dense_weight, fc2_weight = sync(
        fc1_given, tokens, out_grad, segments, qkv_weight, dense_weight, fc2_weight
    )
    got = to_low(fc1_given)
    tokens_core, grad_core = to_core(tokens), to_core(out_grad)
    heads_mine, heads_given = heads_halves(low_at, qkv_weight, dense_weight)
    (fc2_mine,), (fc2_given,) = halves_of(low_at, fc2_weight)
    got, tokens_core, grad_core, heads_given, fc2_given, tokens, out_grad, segments = sync(
        got, tokens_core, grad_core, heads_given, fc2_given, tokens, out_grad, segments
    )
    fc1_a, fc1_b = gathers_of(fc1_mine, got)
    tokens, out_grad, segments, heads_given, fc2_given = sync(
        tokens, out_grad, segments, heads_given, fc2_given
    )
    fc1_a.start()
    tokens_low, tokens_y, segments_low = to_low(tokens), to_y(tokens), to_low(segments)
    tokens_low, tokens_y, segments_low, heads_given, fc1_b.own, fc2_given, out_grad = segment(
        [tokens_low, tokens_y, segments_low, heads_given, fc1_b.own, fc2_given, out_grad], fc1_a
    )
    fc1_a.forward()
    fc1_b.start()
    tokens_both, got = to_y(tokens_low), to_low(heads_given)
    all_segments = jnp.concatenate([segments, segments_low])
    starts = jnp.sum(
        (all_segments[:, None, :] < all_segments[:, :, None]).astype(jnp.int32), axis=2
    )
    tokens_both, got, starts, fc2_given, out_grad, tokens_low, tokens_y = segment(
        [tokens_both, got, starts, fc2_given, out_grad, tokens_low, tokens_y], fc1_a, fc1_b
    )
    tokens_low_core, tokens_y_core = to_core(tokens_low), to_core(tokens_y)
    tokens_both_core = to_core(tokens_both)
    shards = shards_of(low_at, heads_mine, got)
    tokens_low_core, tokens_y_core, tokens_both_core, fc2_given, out_grad, *shards = sync(
        tokens_low_core, tokens_y_core, tokens_both_core, fc2_given, out_grad, *shards
    )
    heads_a, heads_b = (Gather(shard) for shard in shards)
    fc1_b.forward()
    heads_a.start()
    grad_low, grad_y = to_low(out_grad), to_y(out_grad)
    token_pieces = [
        tokens,
        tokens_low,
        tokens_y,
        tokens_both,
        tokens_core,
        tokens_low_core,
        tokens_y_core,
        tokens_both_core,
    ]
    all_normed, *row_stats = normalize_all(token_pieces, ln_gain[None], ln_bias[None])
    fc1_full = [fc1_a.whole()]
    all_normed, fc1_full[0], grad_low, grad_y, heads_b.own, fc2_given = segment(
        [all_normed, fc1_full[0], grad_low, grad_y, heads_b.own, fc2_given], fc1_b, heads_a
    )
    heads_a.forward()
    heads_b.start()
    grad_both, got = to_y(grad_low), to_low(fc2_given)
    fc1_full.append(fc1_b.whole())
    bias = lax.dynamic_slice_in_dim(fc1_bias, low_at * hidden, hidden, 0)[None]
    activated, slope = hidden_forward(all_normed, fc1_full, bias)
    activated, slope, grad_both, got, grad_low, grad_y = segment(
        [activated, slope, grad_both, got, grad_low, grad_y], heads_a, heads_b
    )
    grad_low_core, grad_y_core = to_core(grad_low), to_core(grad_y)
    grad_both_core = to_core(grad_both)
    heads_full = [heads_a.whole()]
    heads_full[0], grad_low_core, grad_y_core, grad_both_core, *shards = sync(
        heads_full[0],
        grad_low_core,
        grad_y_core,
        grad_both_core,
        *shards_of(low_at, fc2_mine, got),
    )
    fc2_a, fc2_b = (Gather(shard) for shard in shards)
    heads_b.forward()
    fc2_a.start()
    all_grad, grad_sums = stack_pieces(
        [
            out_grad,
            grad_low,
            grad_y,
            grad_both,
            grad_core,
            grad_low_core,
            grad_y_core,
            grad_both_core,
        ]
    )
    all_grad, *partials, fc2_b.own = segment(
        [all_grad, *sums_of((all_grad, activated)), fc2_b.own], heads_b, fc2_a
    )
    d_fc2_a, d_fc2_b = as_sums(partials)
    fc2_a.forward()
    fc2_b.start()
    heads_full.append(heads_b.whole())
    bias = lax.dynamic_slice_in_dim(qkv_bias, low_at * half, half, 1)
    bias = bias.reshape(3, pairs, pair).transpose(1, 0, 2).reshape(1, 3 * half)
    projected, back = heads_inputs(all_normed, all_grad, heads_full, bias)
    projected, back, d_fc2_a.given, d_fc2_b.given = segment(
        [projected, back, d_fc2_a.given, d_fc2_b.given], fc2_a, fc2_b
    )
    fc2_b.forward()
    d_fc2_a.start()
    attended, qkv_grad, qkv_sums = attention(projected, back, starts, place)
    fc2_full = [fc2_a.whole()]
    attended, qkv_grad, qkv_sums, fc2_full[0], d_fc2_b.given = segment(
        [attended, qkv_grad, qkv_sums, fc2_full[0], d_fc2_b.given], fc2_b, d_fc2_a
    )
    d_fc2_b.start()
    d_fc2_a.second()
    fc2_full.append(fc2_b.whole())
    columns = heads_full[0].shape[1]
    first, second = slice(0, columns), slice(columns, 2 * columns)
    qkv_end = 3 * half - columns
    everything = slice(None)
    branch_products = (
        [attended, activated],
        [heads_full[1], *fc2_full],
        [
            (0, everything, 0, slice(qkv_end, columns)),
            (1, first, 1, everything),
            (1, second, 2, everything),
        ],
    )
    far, *partials = segment(
        [
            branch_rows(1, *branch_products),
            *sums_of((all_normed, qkv_grad), (all_grad, attended)),
        ],
        d_fc2_a,
        d_fc2_b,
    )
    d_heads_a, d_heads_b = as_sums(partials)
    d_heads_a.start()
    d_fc2_b.second()
    d_fc2_a.third()
    branch_got = to_core(far)
    branch_kept = branch_rows(0, *branch_products)
    pre_grad, pre_sums = hidden_back(all_grad, fc2_full, slope)
    branch_got, branch_kept, pre_grad, pre_sums, d_heads_b.given = segment(
        [branch_got, branch_kept, pre_grad, pre_sums, d_heads_b.given],
        d_heads_a,
        d_fc2_a,
        d_fc2_b,
    )
    d_heads_b.start()
    d_heads_a.second()
    d_fc2_b.third()
    left, left_given, right, right_given = link_stage(branch_kept, branch_got, 11)
    branch_state = [left, to_y(left_given), right, to_low(right_given)]
    grad_products = (
        [qkv_grad, pre_grad],
        [*heads_full, *fc1_full],
        [
            (0, first, 0, everything),
            (0, slice(columns, 3 * half), 1, slice(0, qkv_end)),
            (1, first, 2, everything),
            (1, second, 3, everything),
        ],
        token_pieces,
        row_stats,
    )
    far, far_sums, given_a, given_b, kept_a, kept_b, *branch_state = segment(
        [*token_grad(1, *grad_products), *sums_of((all_normed, pre_grad)), *branch_state],
        d_heads_a,
        d_heads_b,
        d_fc2_b,
    )
    d_fc1_a, d_fc1_b = as_sums([given_a, given_b, kept_a, kept_b])
    d_fc1_a.start()
    d_heads_b.second()
    got = to_core(far)
    left, left_given, right, right_given = last_stage(*branch_state)
    branch_state = [left, to_low(left_given), right, to_y(right_given)]
    kept, near_sums = token_grad(0, *grad_products)
    got, kept, near_sums, d_fc1_b.given, *branch_state = segment(
        [got, kept, near_sums, d_fc1_b.given, *branch_state], d_fc1_a, d_heads_a, d_heads_b
    )
    d_fc1_b.start()
    d_fc1_a.second()
    left, left_given, right, right_given = link_stage(kept, got, 10)
    grad_state = [left, to_y(left_given), right, to_low(right_given)]
    output = row_result(
        output_kernel, "output", *branch_state, tokens, dense_bias[None], fc2_bias[None]
    )
    fc2_weight_grad = final_grad(low_at, *d_fc2_a.halves(), *d_fc2_b.halves())
    sums = (near_sums + far_sums).reshape(2 * D)
    sums_got = to_core(sums)
    here = jnp.concatenate([jnp.sum(qkv_sums, axis=(0, 1)), pre_sums[0]])
    output, fc2_weight_grad, sums, sums_got, here, *grad_state = segment(
        [output, fc2_weight_grad, sums, sums_got, here, *grad_state],
        d_fc1_a,
        d_fc1_b,
        d_heads_a,
        d_heads_b,
    )
    d_fc1_b.second()
    d_heads_a.third()
    left, left_given, right, right_given = last_stage(*grad_state)
    grad_state = [left, to_low(left_given), right, to_y(right_given)]
    sums = sums + sums_got
    sums_got = to_y(sums)
    sums, sums_got, here, *grad_state = segment(
        [sums, sums_got, here, *grad_state], d_fc1_a, d_fc1_b, d_heads_a, d_heads_b
    )
    d_fc1_a.third()
    d_fc1_b.third()
    d_heads_b.third()
    packed = jnp.concatenate([sums + sums_got, here])
    packed_got = to_low(packed)
    input_grad = row_result(
        input_grad_kernel, "input_grad", *grad_state, tokens, out_grad, ln_gain[None]
    )
    input_grad, packed, packed_got = segment(
        [input_grad, packed, packed_got], d_fc1_a, d_fc1_b, d_heads_b
    )
    sums = jnp.concatenate(
        [packed[: 2 * D] + packed_got[: 2 * D], grad_sums[0], packed[2 * D :], packed_got[2 * D :]]
    )
    if pairwise:
        sums_got = [to_high(sums), to_x(sums), swap_both(sums, "zh", 1, "x", 1)]
    else:
        sums_got = [lax.psum(sums, ("zh", "x")) - sums]
    qkv_weight_grad, dense_weight_grad = final_heads(
        low_at, *d_heads_a.halves(), *d_heads_b.halves()
    )
    fc1_weight_grad = final_grad(low_at, *d_fc1_a.halves(), *d_fc1_b.halves())
    qkv_weight_grad, dense_weight_grad, fc1_weight_grad, sums, *sums_got = sync(
        qkv_weight_grad, dense_weight_grad, fc1_weight_grad, sums, *sums_got
    )
    sums = sum(sums_got, sums)
    both = sums[3 * D :].reshape(2, here.shape[0])
    both = jnp.where(low_at == 0, both, both[::-1])
    qkv_bias_grad = (
        both[:, : 3 * half].reshape(2, pairs, 3, pair).transpose(2, 0, 1, 3).reshape(3, 2 * half)
    )
    return (
        output,
        input_grad,
        sums[:D],
        sums[D : 2 * D],
        qkv_weight_grad.transpose(1, 0, 2),
        qkv_bias_grad,
        dense_weight_grad,
        sums[2 * D : 3 * D],
        fc1_weight_grad,
        both[:, 3 * half :].reshape(2 * hidden),
        fc2_weight_grad,
        sums[2 * D : 3 * D],
    )


def solution(mesh):
    dp, tensor = mesh.shape["dp"], mesh.shape["tensor"]
    rows = ("zh", "zl", "x")
    everywhere = (*rows, "t")
    split = Mesh(np.asarray(mesh.devices).reshape(dp // 4, 2, 2, tensor), everywhere)
    return jax.shard_map(
        body,
        mesh=split,
        in_specs=(
            P(everywhere, None),
            P(everywhere, None),
            P(rows, None),
            P(),
            P(),
            P(rows, None, "t"),
            P(None, "t"),
            P(rows, "t"),
            P(),
            P(rows, "t"),
            P("t"),
            P(rows, "t"),
            P(),
        ),
        out_specs=(
            P(everywhere, None),
            P(everywhere, None),
            P(),
            P(),
            P(rows, None, "t"),
            P(None, "t"),
            P(rows, "t"),
            P(),
            P(rows, "t"),
            P("t"),
            P(rows, "t"),
            P(),
        ),
        check_vma=False,
    )
```
